32 devices in a mesh: dp: 8 (over y, x, core), tensor: 4 (over z).
Axes of the slice: x: 2, y: 2, z: 4, core: 2. Of those that a mesh axis runs over, the one named last changes fastest.
Arguments:
- tokens: bfloat16 [32, 1024, 768], P('dp', 'tensor'), may hold values from -6 to 6
- segment_ids: int32 [32, 1024], P('dp'), may hold values from 0 to 3, never falling along the last dimension, each value on 1 to 512 neighbouring positions
- drop_flags: int32 [32], P('dp'), may hold values 0 or 1
- query_key_value_weight: bfloat16 [3, 768, 768], P(None, 'dp', 'tensor'), may hold values from -0.21875 to 0.21875
- query_value_bias: float32 [2, 768], replicated, may hold values from -3 to 3
- attention_output_weight: bfloat16 [768, 768], P('tensor', 'dp'), may hold values from -0.875 to 0.875
- attention_output_bias: float32 [768], replicated, may hold values from -2 to 2
- gain_one: float32 [768], replicated, may hold values from 0.5 to 1.5
- shift_one: float32 [768], replicated, may hold values from -2 to 2
- up_projection_weight: bfloat16 [768, 3072], P('dp', 'tensor'), may hold values from -0.21875 to 0.21875
- hidden_layer_bias: float32 [3072], replicated, may hold values from -3 to 3
- down_projection_weight: bfloat16 [3072, 768], P('tensor', 'dp'), may hold values from -0.109375 to 0.109375
- down_projection_bias: float32 [768], replicated, may hold values from -2 to 2
- gain_two: float32 [768], replicated, may hold values from 0.5 to 1.5
- shift_two: float32 [768], replicated, may hold values from -2 to 2
- cotangent: bfloat16 [32, 1024, 768], P('dp', 'tensor'), may hold values from -6 to 6
Outputs:
- layer_out: bfloat16 [32, 1024, 768], P('dp', 'tensor')
- grad_tokens: float32 [32, 1024, 768], P('dp', 'tensor')
- grad_w_qkv: float32 [3, 768, 768], P(None, 'dp', 'tensor')
- grad_bias_qv: float32 [2, 768], replicated
- grad_w_out: float32 [768, 768], P('tensor', 'dp')
- grad_bias_out: float32 [768], replicated
- grad_gain_one: float32 [768], replicated
- grad_shift_one: float32 [768], replicated
- expansion_factor_sensitivity: float32 [768, 3072], P('dp', 'tensor')
- grad_bias_in: float32 [3072], replicated
- grad_w_back: float32 [3072, 768], P('tensor', 'dp')
- grad_bias_back: float32 [768], replicated
- grad_gain_two: float32 [768], replicated
- grad_shift_two: float32 [768], replicated
The draws below stay inside these ranges and needn't reach their ends.
Inputs may be any that keep to these rules, and one draw needn't show every extreme that they name: `segment_ids`: along each sequence the ids never fall and every id from 0 to 3 appears; a document holds at most 512 positions. `drop_flags`: A 1 makes the layer the identity for that sequence.
All inputs are finite; a program needn't handle non-finite values. No bound on the sum of `drop_flags` on one device may be relied on, other than what follows from the above.
Results may differ from the reference program's by a relative error of at most 0.017.
Values may be sent and summed in bfloat16 or wider, within the bound.
A program may use at most 192 MiB of HBM per device.

```python
import math
import jax
import jax.numpy as jnp
import numpy as np
from jax import lax

D = 768
HEADS = 12
HD = 64
FF = 3072
LEN = 1024
DOCS = 4
SEQS = 32


def set_ends(array, rng, smallest, high):
    index_at = [jax.random.randint(jax.random.fold_in(rng, axis), (), 0, length) for axis, length in enumerate(array.shape)]
    main_axis = array.shape.index(max(array.shape))
    next_to = index_at[:main_axis] + [(index_at[main_axis] + 1) % array.shape[main_axis]] + index_at[main_axis + 1:]
    return array.at[tuple(index_at)].set(smallest).at[tuple(next_to)].set(high)


def block_scale(key, shape, pieces, least, largest):
    factor_of, own = 1.0, jax.random.fold_in(key, 6)
    for dim, blocks in pieces:
        draws = jnp.exp(jax.random.uniform(jax.random.fold_in(own, dim), (blocks,), jnp.float32, least / len(pieces), largest / len(pieces)))
        factor_of = factor_of * jnp.repeat(draws, shape[dim] // blocks).reshape([-1 if axis == dim else 1 for axis in range(len(shape))])
    return factor_of


def length_profile(number_of, total, most, lean):
    weights = [(1 << 20) // math.isqrt(rank ** lean) + 1 for rank in range(2, number_of + 1)]
    rest, counts = total - most - (number_of - 1), [1] * (number_of - 1)
    while rest > 0:
        movable = [i for i in range(number_of - 1) if counts[i] < most]
        mass, remaining = sum([weights[i] for i in movable]), rest
        for i in movable:
            more = min(most - counts[i], max(1, remaining * weights[i] // mass), rest)
            counts[i] = counts[i] + more
            rest = rest - more
    return np.array([most] + counts)


def uneven_parts(stream_key, number_of, total, limit, skew):
    if number_of == 2:
        one = jax.random.randint(stream_key, (), max(1, total - limit), min(limit, total - 1) + 1)
        return jnp.stack([one, total - one])
    tallies = jnp.asarray(length_profile(number_of, total, limit, skew), jnp.int32)
    couples = (number_of - 1) // 2
    donor, receiver = tallies[1:1 + 2 * couples:2], tallies[2:2 + 2 * couples:2]
    slack = jnp.minimum(donor - 1, limit - receiver)
    shifted = jax.random.randint(jax.random.fold_in(stream_key, 1), (couples,), 0, 1 << 20) % (slack + 1)
    tallies = tallies.at[1:1 + 2 * couples:2].set(donor - shifted).at[2:2 + 2 * couples:2].set(receiver + shifted)
    return tallies[jax.random.permutation(jax.random.fold_in(stream_key, 2), number_of)]


def noise(rng, extent, width, limit, cuts=(), held_as=jnp.bfloat16):
    entries = jax.random.normal(rng, extent, jnp.float32) * width
    if len(cuts) > 0:
        entries = block_scale(rng, extent, cuts, -0.22, 0.18) * entries
    return jnp.clip(entries, min=-limit, max=limit).astype(held_as)


def setup_inputs(seed: int = 0) -> dict:
    arg_keys = jax.random.split(jax.random.key(seed), 17)
    tokens = noise(arg_keys[0], (SEQS, LEN, D), 1.0, 6.0, ((0, 8), (1, 4)))
    segment_ids = jax.vmap(lambda own: jnp.searchsorted(jnp.cumsum(uneven_parts(own, DOCS, LEN, LEN // 2, 2)), jnp.arange(LEN), side="right"))(jax.random.split(arg_keys[1], SEQS)).reshape((SEQS, LEN)).astype(jnp.int32)
    drop_flags = set_ends((jax.random.randint(arg_keys[2], (SEQS,), 0, 4) < 1).astype(jnp.int32), jax.random.fold_in(arg_keys[2], 1), 0, 1)
    query_key_value_weight = noise(arg_keys[3], (3, D, D), D ** -0.5, 0.21875, ((1, 8), (2, 4)))
    query_value_bias = noise(arg_keys[4], (2, D), 0.5, 3.0, (), jnp.float32)
    attention_output_weight = noise(arg_keys[5], (D, D), (D // 16) ** -0.5, 0.875, ((0, 4), (1, 8)))
    attention_output_bias = noise(arg_keys[6], (D,), 0.3, 2.0, (), jnp.float32)
    gain_one = jnp.clip(1.0 + 0.1 * jax.random.normal(arg_keys[7], (D,), jnp.float32), 0.5, 1.5)
    shift_one = noise(arg_keys[8], (D,), 0.3, 2.0, (), jnp.float32)
    up_projection_weight = noise(arg_keys[9], (D, FF), D ** -0.5, 0.21875, ((0, 8), (1, 4)))
    hidden_layer_bias = noise(arg_keys[10], (FF,), 0.5, 3.0, (), jnp.float32)
    down_projection_weight = noise(arg_keys[11], (FF, D), FF ** -0.5, 0.109375, ((0, 4), (1, 8)))
    down_projection_bias = noise(arg_keys[12], (D,), 0.3, 2.0, (), jnp.float32)
    gain_two = jnp.clip(1.0 + 0.1 * jax.random.normal(arg_keys[13], (D,), jnp.float32), 0.5, 1.5)
    shift_two = noise(arg_keys[14], (D,), 0.3, 2.0, (), jnp.float32)
    cotangent = noise(arg_keys[15], (SEQS, LEN, D), 1.0, 6.0, ((0, 8), (1, 4)))
    return {"tokens": tokens, "segment_ids": segment_ids, "drop_flags": drop_flags, "query_key_value_weight": query_key_value_weight, "query_value_bias": query_value_bias, "attention_output_weight": attention_output_weight, "attention_output_bias": attention_output_bias, "gain_one": gain_one, "shift_one": shift_one, "up_projection_weight": up_projection_weight, "hidden_layer_bias": hidden_layer_bias, "down_projection_weight": down_projection_weight, "down_projection_bias": down_projection_bias, "gain_two": gain_two, "shift_two": shift_two, "cotangent": cotangent}


@jax.custom_vjp
def narrow_dtype(v):
    return lax.optimization_barrier(v.astype(jnp.bfloat16)).astype(jnp.float32)

@jax.custom_vjp
def narrow_backward_dtype(v):
    return v

def low_keep(v):
    return (narrow_dtype(v), None)

def low_pass(kept, grad):
    return (grad,)

def reverse_survival_flags(v):
    return (v, None)

def back_low(kept, grad):
    return (narrow_dtype(grad),)
narrow_dtype.defvjp(low_keep, low_pass)
narrow_backward_dtype.defvjp(reverse_survival_flags, back_low)
norm_eps = 1e-05
mask_value = -1000000000.0
root_half = 0.7071067811865476
highest_precision = lax.Precision.HIGHEST

def gelu_value(preactivation):
    return 0.5 * preactivation * (1.0 + lax.erf(preactivation * root_half))

def layer_norm(rows_in, gain_vec, shift_vec):
    row_mean = lax.optimization_barrier(jnp.mean(rows_in, axis=-1, keepdims=True))
    mean_shifted_entries = rows_in - row_mean
    inv_std = lax.rsqrt(lax.optimization_barrier(jnp.mean(mean_shifted_entries * mean_shifted_entries, axis=-1, keepdims=True)) + norm_eps)
    return mean_shifted_entries * inv_std * gain_vec + shift_vec

def sequence_attend(input_rows):
    query_matrix, key_matrix, value_matrix, document_label_line = input_rows
    query_heads = query_matrix.reshape(LEN, HEADS, HD)
    key_heads = key_matrix.reshape(LEN, HEADS, HD)
    value_heads = value_matrix.reshape(LEN, HEADS, HD)
    same_doc = document_label_line[:, None] == document_label_line[None, :]
    scores = jnp.einsum('qhd,khd->hqk', query_heads, key_heads, precision=highest_precision) * 0.125
    scores = jnp.where(same_doc[None], narrow_backward_dtype(scores), mask_value)
    probs = narrow_dtype(jax.nn.softmax(scores, axis=-1))
    attended_rows = jnp.einsum('hqk,khd->qhd', probs, value_heads, precision=highest_precision)
    return attended_rows.reshape(LEN, D)

def layer(input_rows, query_key_value_weight, query_value_bias, attention_output_weight, attention_output_bias, gain_one, shift_one, up_projection_weight, hidden_layer_bias, down_projection_weight, down_projection_bias, gain_two, shift_two, segment_ids, drop_flags):
    query_matrix = narrow_dtype(narrow_backward_dtype(jnp.einsum('abm,mi->abi', input_rows, query_key_value_weight[0], precision=highest_precision) + query_value_bias[0]))
    key_matrix = narrow_dtype(narrow_backward_dtype(jnp.einsum('abm,mi->abi', input_rows, query_key_value_weight[1], precision=highest_precision)))
    value_matrix = narrow_dtype(narrow_backward_dtype(jnp.einsum('abm,mi->abi', input_rows, query_key_value_weight[2], precision=highest_precision) + query_value_bias[1]))
    attended_rows = lax.map(jax.checkpoint(sequence_attend), (query_matrix, key_matrix, value_matrix, segment_ids))
    attended_rows = narrow_dtype(narrow_backward_dtype(attended_rows))
    residual_branch = narrow_backward_dtype(jnp.einsum('qbp,pz->qbz', attended_rows, attention_output_weight, precision=highest_precision) + attention_output_bias)
    hidden = layer_norm(input_rows + residual_branch, gain_one, shift_one)
    hidden_narrow = narrow_dtype(hidden)
    preactivation = narrow_backward_dtype(jnp.einsum('jxq,qz->jxz', hidden_narrow, up_projection_weight, precision=highest_precision) + hidden_layer_bias)
    activation_narrow = narrow_dtype(gelu_value(preactivation))
    feedforward_branch = narrow_backward_dtype(jnp.einsum('obq,qg->obg', activation_narrow, down_projection_weight, precision=highest_precision) + down_projection_bias)
    final = layer_norm(hidden + feedforward_branch, gain_two, shift_two)
    return jnp.where(drop_flags[:, None, None] == 1, input_rows, final)

def reference(tokens, segment_ids, drop_flags, query_key_value_weight, query_value_bias, attention_output_weight, attention_output_bias, gain_one, shift_one, up_projection_weight, hidden_layer_bias, down_projection_weight, down_projection_bias, gain_two, shift_two, cotangent):

    def forward(input_rows, qkv_f, bqv_f, out_f, bout_f, gone_f, sone_f, in_f, bin_f, back_f, bback_f, gtwo_f, stwo_f):
        return layer(input_rows, qkv_f, bqv_f, out_f, bout_f, gone_f, sone_f, in_f, bin_f, back_f, bback_f, gtwo_f, stwo_f, segment_ids, drop_flags)
    result, pull_back = jax.vjp(forward, tokens.astype(jnp.float32), query_key_value_weight.astype(jnp.float32), query_value_bias.astype(jnp.float32), attention_output_weight.astype(jnp.float32), attention_output_bias.astype(jnp.float32), gain_one.astype(jnp.float32), shift_one.astype(jnp.float32), up_projection_weight.astype(jnp.float32), hidden_layer_bias.astype(jnp.float32), down_projection_weight.astype(jnp.float32), down_projection_bias.astype(jnp.float32), gain_two.astype(jnp.float32), shift_two.astype(jnp.float32))
    grads = pull_back(cotangent.astype(jnp.float32))
    return (result.astype(jnp.bfloat16), grads[0], grads[1], grads[2], grads[3], grads[4], grads[5], grads[6], grads[7], grads[8], grads[9], grads[10], grads[11], grads[12])
```

```python
import functools
import jax
import jax.numpy as jnp
from jax import lax
from jax.experimental import pallas as pl
from jax.experimental.pallas import tpu as pltpu
from jax.sharding import PartitionSpec as P

HD = 64
EPS = 1e-05
NEG = -1000000000.0
BF = jnp.bfloat16
F32 = jnp.float32
VMEM_LIMIT = 60 * 1024 * 1024
BLK = 256


def dot_nn(a, b):
    return jnp.dot(a, b, preferred_element_type=F32)


def dot_nt(a, b):
    return lax.dot_general(a, b, (((1,), (1,)), ((), ())), preferred_element_type=F32)


def dot_tn(a, b):
    return lax.dot_general(a, b, (((0,), (0,)), ((), ())), preferred_element_type=F32)


def half_masks(shape):
    lane = lax.broadcasted_iota(jnp.int32, shape, 1)
    return lane < HD


def attend_kernel(lo_ref, hi_ref, q_ref, k_ref, v_ref, segc_ref, segr_ref, o_ref, lse_ref, s_scr):
    n = q_ref.shape[0] // BLK
    first = half_masks((BLK, 2 * HD))
    zero = jnp.zeros((), BF)

    def rows(i):
        return pl.ds(pl.multiple_of(i * BLK, BLK), BLK)

    def q_block(i, carry):
        q = q_ref[rows(i), :]
        qs = (jnp.where(first, q, zero), jnp.where(first, zero, q))
        segq = segc_ref[rows(i), :]
        segq = jnp.concatenate([segq] * (BLK // 128), axis=1)
        lo, hi = lo_ref[i], hi_ref[i]

        def score(j, tops):
            k = k_ref[rows(j), :]
            same = segq == segr_ref[j]
            new = []
            for h in range(2):
                s = jnp.where(same, dot_nt(qs[h], k) * 0.125, NEG)
                s_scr[h, j] = s
                top = tops[h]
                for c in range(BLK // 128):
                    top = jnp.maximum(top, s[:, c * 128 : (c + 1) * 128])
                new.append(top)
            return tuple(new)

        start = jnp.full((BLK, 128), NEG, F32)
        tops = lax.fori_loop(lo, hi, score, (start, start))
        tops = [jnp.max(t, axis=1, keepdims=True) for t in tops]

        def weigh(j, state):
            v = v_ref[rows(j), :]
            new = []
            for h in range(2):
                total, acc = state[h]
                p = jnp.exp(s_scr[h, j] - tops[h])
                for c in range(BLK // 128):
                    total = total + p[:, c * 128 : (c + 1) * 128]
                acc = acc + dot_nn(p.astype(BF), v)
                new.append((total, acc))
            return tuple(new)

        zeros = jnp.zeros((BLK, 128), F32)
        state = lax.fori_loop(lo, hi, weigh, ((zeros, zeros), (zeros, zeros)))
        outs = []
        for h in range(2):
            total = jnp.sum(state[h][0], axis=1, keepdims=True)
            outs.append(state[h][1] / total)
            lse = tops[h] + jnp.log(total)
            lse_ref[h : h + 1, rows(i)] = jnp.transpose(jnp.broadcast_to(lse, (BLK, 128)))[0:1, :]
        o_ref[rows(i), :] = jnp.where(first, outs[0], outs[1]).astype(BF)
        return carry

    lax.fori_loop(0, n, q_block, 0)


def attend(qkv, lo, hi, segc, segr):
    length, wide = qkv.shape
    d = wide // 3
    pairs = d // (2 * HD)
    n = length // BLK
    col = lambda off: pl.BlockSpec((length, 2 * HD), lambda p, *_: (0, off + p))
    return pl.pallas_call(
        attend_kernel,
        out_shape=(
            jax.ShapeDtypeStruct((length, d), BF),
            jax.ShapeDtypeStruct((pairs, 2, length), F32),
        ),
        grid_spec=pltpu.PrefetchScalarGridSpec(
            num_scalar_prefetch=2,
            grid=(pairs,),
            in_specs=[
                col(0),
                col(pairs),
                col(2 * pairs),
                pl.BlockSpec((length, 128), lambda p, *_: (0, 0)),
                pl.BlockSpec((n, 1, BLK), lambda p, *_: (0, 0, 0)),
            ],
            out_specs=[col(0), pl.BlockSpec((None, 2, length), lambda p, *_: (p, 0, 0))],
            scratch_shapes=[pltpu.VMEM((2, n, BLK, BLK), F32)],
        ),
        compiler_params=pltpu.CompilerParams(vmem_limit_bytes=VMEM_LIMIT),
        cost_estimate=pl.CostEstimate(
            flops=4 * length * length * d // 2,
            bytes_accessed=8 * length * d,
            transcendentals=length * length * d // HD // 2,
        ),
        name="attend_forward",
    )(lo, hi, qkv, qkv, qkv, segc, segr)


def attend_back_kernel(
    lo_ref, hi_ref, q_ref, k_ref, v_ref, att_ref, g_ref, lse_ref, segc_ref, segr_ref,
    gq_ref, gk_ref, gv_ref, dq_scr, delta_scr,
):
    length = q_ref.shape[0]
    n = length // BLK
    first = half_masks((BLK, 2 * HD))
    zero = jnp.zeros((), BF)

    def rows(i):
        return pl.ds(pl.multiple_of(i * BLK, BLK), BLK)

    sub = lax.broadcasted_iota(jnp.int32, (8, 2 * HD), 0)
    lane = lax.broadcasted_iota(jnp.int32, (8, 2 * HD), 1)
    pick = jnp.where(lane // HD == sub, 1.0, 0.0).astype(F32)
    prod = g_ref[...].astype(F32) * att_ref[...].astype(F32)
    delta_scr[...] = lax.dot_general(
        pick, prod, (((1,), (1,)), ((), ())),
        preferred_element_type=F32, precision=lax.Precision.HIGHEST,
    )
    dq_scr[...] = jnp.zeros_like(dq_scr)

    def k_block(j, carry):
        k = k_ref[rows(j), :]
        v = v_ref[rows(j), :]
        ks = (jnp.where(first, k, zero), jnp.where(first, zero, k))
        vs = (jnp.where(first, v, zero), jnp.where(first, zero, v))
        kcat = jnp.concatenate(ks, axis=0)
        segk = segc_ref[rows(j), :]
        segk = jnp.concatenate([segk] * (BLK // 128), axis=1)

        def q_step(i, state):
            q = q_ref[rows(i), :]
            g = g_ref[rows(i), :]
            same = segk == segr_ref[i]
            new, both = [], []
            for h in range(2):
                dk, dv = state[h]
                st = dot_nt(ks[h], q) * 0.125
                pt = jnp.where(same, jnp.exp(st - lse_ref[h : h + 1, rows(i)]), 0.0)
                dv = dv + dot_nn(pt.astype(BF), g)
                dpt = dot_nt(vs[h], g)
                dst = (pt * (dpt - delta_scr[h : h + 1, rows(i)])).astype(BF)
                dk = dk + dot_nn(dst, q)
                both.append(dst)
                new.append((dk, dv))
            dq_scr[rows(i), :] += dot_tn(jnp.concatenate(both, axis=0), kcat)
            return tuple(new)

        zeros = jnp.zeros((BLK, 2 * HD), F32)
        state = lax.fori_loop(lo_ref[j], hi_ref[j], q_step, ((zeros, zeros), (zeros, zeros)))
        gk_ref[rows(j), :] = (jnp.where(first, state[0][0], state[1][0]) * 0.125).astype(BF)
        gv_ref[rows(j), :] = jnp.where(first, state[0][1], state[1][1]).astype(BF)
        return carry

    lax.fori_loop(0, n, k_block, 0)
    gq_ref[...] = (dq_scr[...] * 0.125).astype(BF)


def attend_back(qkv, att, g_att, lse, lo, hi, segc, segr):
    length, wide = qkv.shape
    d = wide // 3
    pairs = d // (2 * HD)
    n = length // BLK
    col = lambda off: pl.BlockSpec((length, 2 * HD), lambda p, *_: (0, off + p))
    return pl.pallas_call(
        attend_back_kernel,
        out_shape=[jax.ShapeDtypeStruct((length, d), BF)] * 3,
        grid_spec=pltpu.PrefetchScalarGridSpec(
            num_scalar_prefetch=2,
            grid=(pairs,),
            in_specs=[
                col(0),
                col(pairs),
                col(2 * pairs),
                col(0),
                col(0),
                pl.BlockSpec((None, 2, length), lambda p, *_: (p, 0, 0)),
                pl.BlockSpec((length, 128), lambda p, *_: (0, 0)),
                pl.BlockSpec((n, 1, BLK), lambda p, *_: (0, 0, 0)),
            ],
            out_specs=[col(0)] * 3,
            scratch_shapes=[
                pltpu.VMEM((length, 2 * HD), F32),
                pltpu.VMEM((8, length), F32),
            ],
        ),
        compiler_params=pltpu.CompilerParams(vmem_limit_bytes=VMEM_LIMIT),
        cost_estimate=pl.CostEstimate(
            flops=10 * length * length * d // 2,
            bytes_accessed=16 * length * d,
            transcendentals=length * length * d // HD // 2,
        ),
        name="attend_backward",
    )(lo, hi, qkv, qkv, qkv, att, g_att, lse, segc, segr)


def gelu_parts(u):
    e = jnp.exp(-0.5 * u * u)
    t = 1.0 / (1.0 + (0.3275911 * 0.7071067811865476) * jnp.abs(u))
    poly = t * (
        0.5 * 0.254829592
        + t * (0.5 * -0.284496736 + t * (0.5 * 1.421413741 + t * (0.5 * -1.453152027 + t * (0.5 * 1.061405429))))
    )
    tail = poly * e
    cdf = jnp.where(u < 0.0, tail, 1.0 - tail)
    return u * cdf, cdf + u * e * 0.3989422804014327


def norm_rows(v):
    mean = jnp.mean(v, axis=-1, keepdims=True)
    c = v - mean
    inv = lax.rsqrt(jnp.mean(c * c, axis=-1, keepdims=True) + EPS)
    return c * inv, inv


def norm_back(g, normed, inv, gain):
    gn = g * gain
    return inv * (
        gn
        - jnp.mean(gn, axis=-1, keepdims=True)
        - normed * jnp.mean(gn * normed, axis=-1, keepdims=True)
    )


def middle_kernel(
    row_steps, drop_ref, att_ref, x_ref, cot_ref, wo_ref, up_ref, dn_ref, vec_ref, bin_ref,
    lo_ref, gatt_ref, ghpre_ref, gup_ref, gdn_ref, gwo_ref, vecg_ref, bing_ref,
    att_s, act_s, gpre_s, slope_s, ht_s, gb2t_s, gbt_s,
):
    step = pl.program_id(0)
    parts = up_ref.shape[0]

    @pl.when(step == 0)
    def _():
        vecg_ref[...] = jnp.zeros_like(vecg_ref)
        bing_ref[...] = jnp.zeros_like(bing_ref)

    @pl.when(step < row_steps)
    def _():
        at = pl.ds(pl.multiple_of(step * BLK, BLK), BLK)
        vec = lambda r: vec_ref[r : r + 1, :]
        dropped = drop_ref[0] == 1
        att = att_ref[...]
        att_s[at, :] = att
        x = x_ref[...].astype(F32)
        branch = dot_nt(att, wo_ref[...]) + vec(0)
        n1, inv1 = norm_rows(x + branch)
        hidden = n1 * vec(1) + vec(2)
        low = hidden.astype(BF)
        ht_s[:, at] = jnp.transpose(low)
        ffn = hidden + vec(3)
        for t in range(parts):
            pre = dot_nn(low, up_ref[t]) + bin_ref[t : t + 1, :]
            act, slope = gelu_parts(pre)
            act = act.astype(BF)
            act_s[t, at, :] = act
            slope_s[t] = slope
            ffn = ffn + dot_nt(act, dn_ref[t])
        n2, inv2 = norm_rows(ffn)
        final = n2 * vec(4) + vec(5)
        lo_ref[...] = jnp.where(dropped, x, final).astype(BF)
        g_final = jnp.where(dropped, 0.0, cot_ref[...].astype(F32))
        g_fpre = norm_back(g_final, n2, inv2, vec(4))
        gb2 = g_fpre.astype(BF)
        gb2t_s[:, at] = jnp.transpose(gb2)
        g_hidden = g_fpre
        for t in range(parts):
            gpre = (dot_nn(gb2, dn_ref[t]) * slope_s[t]).astype(BF)
            gpre_s[t, at, :] = gpre
            bing_ref[t : t + 1, :] += jnp.sum(gpre.astype(F32), axis=0, keepdims=True)
            g_hidden = g_hidden + dot_nt(gpre, up_ref[t])
        g_hpre = norm_back(g_hidden, n1, inv1, vec(1))
        gb = g_hpre.astype(BF)
        gbt_s[:, at] = jnp.transpose(gb)
        gatt_ref[...] = dot_nn(gb, wo_ref[...]).astype(BF)
        ghpre_ref[...] = g_hpre
        for r, v in enumerate(
            (gb.astype(F32), g_hidden * n1, g_hidden, gb2.astype(F32), g_final * n2, g_final)
        ):
            vecg_ref[r : r + 1, :] += jnp.sum(v, axis=0, keepdims=True)

    for t in range(parts):

        @pl.when(step == row_steps + t)
        def _():
            gup_ref[...] = dot_nn(ht_s[...], gpre_s[t]).astype(BF)
            gdn_ref[...] = dot_nn(gb2t_s[...], act_s[t]).astype(BF)

    @pl.when(step == row_steps + parts)
    def _():
        gwo_ref[...] = dot_nn(gbt_s[...], att_s[...]).astype(BF)


def middle(drop, att, x, cot, wo, up, dn, vec, bias_in):
    length, d = att.shape
    parts, _, fl = up.shape
    nr = length // BLK
    rows = pl.BlockSpec((BLK, d), lambda i: (jnp.minimum(i, nr - 1), 0))
    once = lambda shape: pl.BlockSpec(
        shape, lambda i: (0,) * len(shape), pipeline_mode=pl.Buffered(1)
    )
    part = pl.BlockSpec((None, d, fl), lambda i: (jnp.clip(i - nr, 0, parts - 1), 0, 0))
    whole = lambda shape: pl.BlockSpec(shape, lambda i: (0,) * len(shape))
    return pl.pallas_call(
        functools.partial(middle_kernel, nr),
        grid=(nr + parts + 1,),
        out_shape=(
            jax.ShapeDtypeStruct((length, d), BF),
            jax.ShapeDtypeStruct((length, d), BF),
            jax.ShapeDtypeStruct((length, d), F32),
            jax.ShapeDtypeStruct((parts, d, fl), BF),
            jax.ShapeDtypeStruct((parts, d, fl), BF),
            jax.ShapeDtypeStruct((d, d), BF),
            jax.ShapeDtypeStruct((8, d), F32),
            jax.ShapeDtypeStruct((parts, fl), F32),
        ),
        in_specs=[
            pl.BlockSpec(memory_space=pltpu.SMEM),
            rows,
            rows,
            rows,
            once((d, d)),
            once((parts, d, fl)),
            once((parts, d, fl)),
            once((8, d)),
            once((parts, fl)),
        ],
        out_specs=(rows, rows, rows, part, part, whole((d, d)), whole((8, d)), whole((parts, fl))),
        scratch_shapes=[
            pltpu.VMEM((length, d), BF),
            pltpu.VMEM((parts, length, fl), BF),
            pltpu.VMEM((parts, length, fl), BF),
            pltpu.VMEM((parts, BLK, fl), F32),
            pltpu.VMEM((d, length), BF),
            pltpu.VMEM((d, length), BF),
            pltpu.VMEM((d, length), BF),
        ],
        compiler_params=pltpu.CompilerParams(vmem_limit_bytes=VMEM_LIMIT),
        cost_estimate=pl.CostEstimate(
            flops=6 * length * d * (d + 2 * parts * fl),
            bytes_accessed=4 * length * d * 3 + 8 * parts * d * fl,
            transcendentals=2 * length * parts * fl,
        ),
        name="middle",
    )(drop, att, x, cot, wo, up, dn, vec, bias_in)


def block_range(seg):
    length = seg.shape[0]
    n = length // BLK
    blocks = seg.reshape(n, BLK)
    start = jnp.sum(seg[None, :] < blocks[:, :1], axis=1)
    end = jnp.sum(seg[None, :] <= blocks[:, -1:], axis=1)
    return (start // BLK).astype(jnp.int32), ((end + BLK - 1) // BLK).astype(jnp.int32)


def on_device(
    tokens, segment_ids, drop_flags, qkv_w, qv_b, wo_w, wo_b, gain1, shift1,
    up_w, up_b, dn_w, dn_b, gain2, shift2, cotangent,
):
    axes = ("tensor", "dp")
    me = lax.axis_index("tensor")
    nt = lax.axis_size("tensor")
    seqs, rows_local, d = tokens.shape
    length = segment_ids.shape[1]
    rw, wl = qkv_w.shape[1], qkv_w.shape[2]
    fl = up_w.shape[1]
    per = seqs // nt

    def to_seq(a):
        return lax.all_to_all(a, "tensor", 0, 1, tiled=True)

    def to_rows(a):
        return lax.all_to_all(a, "tensor", 1, 0, tiled=True)

    x_all = to_seq(tokens)
    cot_all = to_seq(cotangent)
    w1 = lax.all_gather(
        jnp.transpose(qkv_w, (1, 0, 2)).reshape(rw, 3 * wl), axes, axis=0, tiled=True
    )
    w2 = lax.all_gather(
        jnp.concatenate((up_w, dn_w.T, wo_w.T), axis=1), axes, axis=0, tiled=True
    ).reshape(nt, d, 2 * fl + wl)
    wqkv = w1.reshape(nt, d, 3, wl).transpose(1, 2, 0, 3).reshape(d, 3 * d)
    up = w2[:, :, :fl]
    dn = w2[:, :, fl : 2 * fl]
    wo = w2[:, :, 2 * fl :].transpose(1, 0, 2).reshape(d, d)
    bias = jnp.concatenate((qv_b[0], jnp.zeros((d,), F32), qv_b[1]))
    zero_row = jnp.zeros((d,), F32)
    vec = jnp.stack((wo_b, gain1, shift1, dn_b, gain2, shift2, zero_row, zero_row))
    bias_in = up_b.reshape(nt, fl)

    gw1 = gw2 = None
    outs, gxs = [], []
    vecg = bing = qvg = 0.0
    for s in range(per):
        x, cot = x_all[s], cot_all[s]
        seg = lax.dynamic_index_in_dim(segment_ids, me * per + s, 0, keepdims=False)
        drop = lax.dynamic_slice_in_dim(drop_flags, me * per + s, 1)
        lo, hi = block_range(seg)
        segc = jnp.broadcast_to(seg[:, None], (length, 128))
        segr = seg.reshape(length // BLK, 1, BLK)
        qkv = (dot_nn(x, wqkv) + bias).astype(BF)
        att, lse = attend(qkv, lo, hi, segc, segr)
        layer, g_att, g_hpre, gup, gdn, gwo, vg, bg = middle(
            drop, att, x, cot, wo, up, dn, vec, bias_in
        )
        gq, gk, gv = attend_back(qkv, att, g_att, lse, lo, hi, segc, segr)
        gqkv = jnp.concatenate((gq, gk, gv), axis=1)
        gx = g_hpre + dot_nt(gqkv, wqkv)
        gx = gx + jnp.where(drop[0] == 1, cot.astype(F32), 0.0)
        gwq = dot_tn(x, gqkv)
        g1 = gwq.astype(BF).reshape(d, 3, nt, wl).transpose(2, 0, 1, 3).reshape(nt * d, 3 * wl)
        g2 = jnp.concatenate(
            (gup, gdn, gwo.reshape(d, nt, wl).transpose(1, 0, 2)), axis=2
        ).reshape(nt * d, 2 * fl + wl)
        gw1 = g1 if gw1 is None else gw1 + g1
        gw2 = g2 if gw2 is None else gw2 + g2
        outs.append(layer)
        gxs.append(gx.astype(BF))
        vecg, bing = vecg + vg, bing + bg
        qvg = qvg + jnp.stack(
            (jnp.sum(gq.astype(F32), axis=0), jnp.sum(gv.astype(F32), axis=0))
        )
    layer_out = to_rows(jnp.stack(outs))
    g2 = lax.psum_scatter(gw2, axes, scatter_dimension=0, tiled=True).astype(F32)
    g1 = lax.psum_scatter(gw1, axes, scatter_dimension=0, tiled=True).astype(F32)
    grad_tokens = to_rows(jnp.stack(gxs)).astype(F32)
    vecg, bing, qvg = lax.psum((vecg, bing, qvg), axes)
    return (
        layer_out,
        grad_tokens,
        g1.reshape(rw, 3, wl).transpose(1, 0, 2),
        qvg,
        g2[:, 2 * fl :].T,
        vecg[0],
        vecg[1],
        vecg[2],
        g2[:, :fl],
        bing.reshape(-1),
        g2[:, fl : 2 * fl].T,
        vecg[3],
        vecg[4],
        vecg[5],
    )


def solution(mesh):
    rows = P("dp", "tensor", None)
    return jax.shard_map(
        on_device,
        mesh=mesh,
        in_specs=(
            rows, P("dp", None), P("dp"), P(None, "dp", "tensor"), P(), P("tensor", "dp"), P(), P(), P(),
            P("dp", "tensor"), P(), P("tensor", "dp"), P(), P(), P(), rows,
        ),
        out_specs=(
            rows, rows, P(None, "dp", "tensor"), P(), P("tensor", "dp"), P(), P(), P(),
            P("dp", "tensor"), P(), P("tensor", "dp"), P(), P(), P(),
        ),
        check_vma=False,
    )
```

```python
import functools
import jax
import jax.numpy as jnp
from jax import lax
from jax.experimental import pallas as pl
from jax.experimental.pallas import tpu as pltpu
from jax.sharding import PartitionSpec as P

HD = 64
EPS = 1e-05
NEG = -1000000000.0
BF = jnp.bfloat16
F32 = jnp.float32
VMEM_LIMIT = 60 * 1024 * 1024
BLK = 256


def dot_nn(a, b):
    return jnp.dot(a, b, preferred_element_type=F32)


def dot_nt(a, b):
    return lax.dot_general(a, b, (((1,), (1,)), ((), ())), preferred_element_type=F32)


def dot_tn(a, b):
    return lax.dot_general(a, b, (((0,), (0,)), ((), ())), preferred_element_type=F32)


def half_masks(shape):
    lane = lax.broadcasted_iota(jnp.int32, shape, 1)
    return lane < HD


def attend_kernel(lo_ref, hi_ref, q_ref, k_ref, v_ref, segc_ref, segr_ref, o_ref, lse_ref, s_scr):
    n = q_ref.shape[0] // BLK
    first = half_masks((BLK, 2 * HD))
    zero = jnp.zeros((), BF)

    def rows(i):
        return pl.ds(pl.multiple_of(i * BLK, BLK), BLK)

    def q_block(i, carry):
        q = q_ref[rows(i), :]
        qs = (jnp.where(first, q, zero), jnp.where(first, zero, q))
        segq = segc_ref[rows(i), :]
        segq = jnp.concatenate([segq] * (BLK // 128), axis=1)
        lo, hi = lo_ref[i], hi_ref[i]

        def score(j, tops):
            k = k_ref[rows(j), :]
            same = segq == segr_ref[j]
            new = []
            for h in range(2):
                s = jnp.where(same, dot_nt(qs[h], k) * 0.125, NEG)
                s_scr[h, j] = s
                top = tops[h]
                for c in range(BLK // 128):
                    top = jnp.maximum(top, s[:, c * 128 : (c + 1) * 128])
                new.append(top)
            return tuple(new)

        start = jnp.full((BLK, 128), NEG, F32)
        tops = lax.fori_loop(lo, hi, score, (start, start))
        tops = [jnp.max(t, axis=1, keepdims=True) for t in tops]

        def weigh(j, state):
            v = v_ref[rows(j), :]
            new = []
            for h in range(2):
                total, acc = state[h]
                p = jnp.exp(s_scr[h, j] - tops[h])
                for c in range(BLK // 128):
                    total = total + p[:, c * 128 : (c + 1) * 128]
                acc = acc + dot_nn(p.astype(BF), v)
                new.append((total, acc))
            return tuple(new)

        zeros = jnp.zeros((BLK, 128), F32)
        state = lax.fori_loop(lo, hi, weigh, ((zeros, zeros), (zeros, zeros)))
        outs = []
        for h in range(2):
            total = jnp.sum(state[h][0], axis=1, keepdims=True)
            outs.append(state[h][1] / total)
            lse = tops[h] + jnp.log(total)
            lse_ref[h : h + 1, rows(i)] = jnp.transpose(jnp.broadcast_to(lse, (BLK, 128)))[0:1, :]
        o_ref[rows(i), :] = jnp.where(first, outs[0], outs[1]).astype(BF)
        return carry

    lax.fori_loop(0, n, q_block, 0)


def attend(qkv, lo, hi, segc, segr):
    length, wide = qkv.shape
    d = wide // 3
    pairs = d // (2 * HD)
    n = length // BLK
    col = lambda off: pl.BlockSpec((length, 2 * HD), lambda p, *_: (0, off + p))
    return pl.pallas_call(
        attend_kernel,
        out_shape=(
            jax.ShapeDtypeStruct((length, d), BF),
            jax.ShapeDtypeStruct((pairs, 2, length), F32),
        ),
        grid_spec=pltpu.PrefetchScalarGridSpec(
            num_scalar_prefetch=2,
            grid=(pairs,),
            in_specs=[
                col(0),
                col(pairs),
                col(2 * pairs),
                pl.BlockSpec((length, 128), lambda p, *_: (0, 0)),
                pl.BlockSpec((n, 1, BLK), lambda p, *_: (0, 0, 0)),
            ],
            out_specs=[col(0), pl.BlockSpec((None, 2, length), lambda p, *_: (p, 0, 0))],
            scratch_shapes=[pltpu.VMEM((2, n, BLK, BLK), F32)],
        ),
        compiler_params=pltpu.CompilerParams(vmem_limit_bytes=VMEM_LIMIT),
        cost_estimate=pl.CostEstimate(
            flops=4 * length * length * d // 2,
            bytes_accessed=8 * length * d,
            transcendentals=length * length * d // HD // 2,
        ),
        name="attend_forward",
    )(lo, hi, qkv, qkv, qkv, segc, segr)


def attend_back_kernel(
    lo_ref, hi_ref, q_ref, k_ref, v_ref, att_ref, g_ref, lse_ref, segc_ref, segr_ref,
    gq_ref, gk_ref, gv_ref, dq_scr, delta_scr,
):
    length = q_ref.shape[0]
    n = length // BLK
    first = half_masks((BLK, 2 * HD))
    zero = jnp.zeros((), BF)

    def rows(i):
        return pl.ds(pl.multiple_of(i * BLK, BLK), BLK)

    sub = lax.broadcasted_iota(jnp.int32, (8, 2 * HD), 0)
    lane = lax.broadcasted_iota(jnp.int32, (8, 2 * HD), 1)
    pick = jnp.where(lane // HD == sub, 1.0, 0.0).astype(F32)
    prod = g_ref[...].astype(F32) * att_ref[...].astype(F32)
    delta_scr[...] = lax.dot_general(
        pick, prod, (((1,), (1,)), ((), ())),
        preferred_element_type=F32, precision=lax.Precision.HIGHEST,
    )
    dq_scr[...] = jnp.zeros_like(dq_scr)

    def k_block(j, carry):
        k = k_ref[rows(j), :]
        v = v_ref[rows(j), :]
        ks = (jnp.where(first, k, zero), jnp.where(first, zero, k))
        vs = (jnp.where(first, v, zero), jnp.where(first, zero, v))
        kcat = jnp.concatenate(ks, axis=0)
        segk = segc_ref[rows(j), :]
        segk = jnp.concatenate([segk] * (BLK // 128), axis=1)

        def q_step(i, state):
            q = q_ref[rows(i), :]
            g = g_ref[rows(i), :]
            same = segk == segr_ref[i]
            new, both = [], []
            for h in range(2):
                dk, dv = state[h]
                st = dot_nt(ks[h], q) * 0.125
                pt = jnp.where(same, jnp.exp(st - lse_ref[h : h + 1, rows(i)]), 0.0)
                dv = dv + dot_nn(pt.astype(BF), g)
                dpt = dot_nt(vs[h], g)
                dst = (pt * (dpt - delta_scr[h : h + 1, rows(i)])).astype(BF)
                dk = dk + dot_nn(dst, q)
                both.append(dst)
                new.append((dk, dv))
            dq_scr[rows(i), :] += dot_tn(jnp.concatenate(both, axis=0), kcat)
            return tuple(new)

        zeros = jnp.zeros((BLK, 2 * HD), F32)
        state = lax.fori_loop(lo_ref[j], hi_ref[j], q_step, ((zeros, zeros), (zeros, zeros)))
        gk_ref[rows(j), :] = (jnp.where(first, state[0][0], state[1][0]) * 0.125).astype(BF)
        gv_ref[rows(j), :] = jnp.where(first, state[0][1], state[1][1]).astype(BF)
        return carry

    lax.fori_loop(0, n, k_block, 0)
    gq_ref[...] = (dq_scr[...] * 0.125).astype(BF)


def attend_back(qkv, att, g_att, lse, lo, hi, segc, segr):
    length, wide = qkv.shape
    d = wide // 3
    pairs = d // (2 * HD)
    n = length // BLK
    col = lambda off: pl.BlockSpec((length, 2 * HD), lambda p, *_: (0, off + p))
    return pl.pallas_call(
        attend_back_kernel,
        out_shape=[jax.ShapeDtypeStruct((length, d), BF)] * 3,
        grid_spec=pltpu.PrefetchScalarGridSpec(
            num_scalar_prefetch=2,
            grid=(pairs,),
            in_specs=[
                col(0),
                col(pairs),
                col(2 * pairs),
                col(0),
                col(0),
                pl.BlockSpec((None, 2, length), lambda p, *_: (p, 0, 0)),
                pl.BlockSpec((length, 128), lambda p, *_: (0, 0)),
                pl.BlockSpec((n, 1, BLK), lambda p, *_: (0, 0, 0)),
            ],
            out_specs=[col(0)] * 3,
            scratch_shapes=[
                pltpu.VMEM((length, 2 * HD), F32),
                pltpu.VMEM((8, length), F32),
            ],
        ),
        compiler_params=pltpu.CompilerParams(vmem_limit_bytes=VMEM_LIMIT),
        cost_estimate=pl.CostEstimate(
            flops=10 * length * length * d // 2,
            bytes_accessed=16 * length * d,
            transcendentals=length * length * d // HD // 2,
        ),
        name="attend_backward",
    )(lo, hi, qkv, qkv, qkv, att, g_att, lse, segc, segr)


def gelu_parts(u):
    e = jnp.exp(-0.5 * u * u)
    t = 1.0 / (1.0 + (0.3275911 * 0.7071067811865476) * jnp.abs(u))
    poly = t * (
        0.5 * 0.254829592
        + t * (0.5 * -0.284496736 + t * (0.5 * 1.421413741 + t * (0.5 * -1.453152027 + t * (0.5 * 1.061405429))))
    )
    tail = poly * e
    cdf = jnp.where(u < 0.0, tail, 1.0 - tail)
    return u * cdf, cdf + u * e * 0.3989422804014327


def norm_rows(v):
    mean = jnp.mean(v, axis=-1, keepdims=True)
    c = v - mean
    inv = lax.rsqrt(jnp.mean(c * c, axis=-1, keepdims=True) + EPS)
    return c * inv, inv


def norm_back(g, normed, inv, gain):
    gn = g * gain
    return inv * (
        gn
        - jnp.mean(gn, axis=-1, keepdims=True)
        - normed * jnp.mean(gn * normed, axis=-1, keepdims=True)
    )


def middle_kernel(
    row_steps, drop_ref, att_ref, x_ref, cot_ref, wo_ref, up_ref, dn_ref, vec_ref, bin_ref,
    lo_ref, gatt_ref, ghpre_ref, gup_ref, gdn_ref, gwo_ref, vecg_ref, bing_ref,
    att_s, act_s, gpre_s, slope_s, ht_s, gb2t_s, gbt_s,
):
    step = pl.program_id(0)
    parts = up_ref.shape[0]

    @pl.when(step == 0)
    def _():
        vecg_ref[...] = jnp.zeros_like(vecg_ref)
        bing_ref[...] = jnp.zeros_like(bing_ref)

    @pl.when(step < row_steps)
    def _():
        at = pl.ds(pl.multiple_of(step * BLK, BLK), BLK)
        vec = lambda r: vec_ref[r : r + 1, :]
        dropped = drop_ref[0] == 1
        att = att_ref[...]
        att_s[at, :] = att
        x = x_ref[...].astype(F32)
        branch = dot_nt(att, wo_ref[...]) + vec(0)
        n1, inv1 = norm_rows(x + branch)
        hidden = n1 * vec(1) + vec(2)
        low = hidden.astype(BF)
        ht_s[:, at] = jnp.transpose(low)
        ffn = hidden + vec(3)
        for t in range(parts):
            pre = dot_nn(low, up_ref[t]) + bin_ref[t : t + 1, :]
            act, slope = gelu_parts(pre)
            act = act.astype(BF)
            act_s[t, at, :] = act
            slope_s[t] = slope
            ffn = ffn + dot_nt(act, dn_ref[t])
        n2, inv2 = norm_rows(ffn)
        final = n2 * vec(4) + vec(5)
        lo_ref[...] = jnp.where(dropped, x, final).astype(BF)
        g_final = jnp.where(dropped, 0.0, cot_ref[...].astype(F32))
        g_fpre = norm_back(g_final, n2, inv2, vec(4))
        gb2 = g_fpre.astype(BF)
        gb2t_s[:, at] = jnp.transpose(gb2)
        g_hidden = g_fpre
        for t in range(parts):
            gpre = (dot_nn(gb2, dn_ref[t]) * slope_s[t]).astype(BF)
            gpre_s[t, at, :] = gpre
            bing_ref[t : t + 1, :] += jnp.sum(gpre.astype(F32), axis=0, keepdims=True)
            g_hidden = g_hidden + dot_nt(gpre, up_ref[t])
        g_hpre = norm_back(g_hidden, n1, inv1, vec(1))
        gb = g_hpre.astype(BF)
        gbt_s[:, at] = jnp.transpose(gb)
        gatt_ref[...] = dot_nn(gb, wo_ref[...]).astype(BF)
        ghpre_ref[...] = g_hpre
        for r, v in enumerate(
            (gb.astype(F32), g_hidden * n1, g_hidden, gb2.astype(F32), g_final * n2, g_final)
        ):
            vecg_ref[r : r + 1, :] += jnp.sum(v, axis=0, keepdims=True)

    for t in range(parts):

        @pl.when(step == row_steps + t)
        def _():
            gup_ref[...] = dot_nn(ht_s[...], gpre_s[t]).astype(BF)
            gdn_ref[...] = dot_nn(gb2t_s[...], act_s[t]).astype(BF)

    @pl.when(step == row_steps + parts)
    def _():
        gwo_ref[...] = dot_nn(gbt_s[...], att_s[...]).astype(BF)


def middle(drop, att, x, cot, wo, w, vec, bias_in):
    length, d = att.shape
    _, parts, _, fl = w.shape
    nr = length // BLK
    rows = pl.BlockSpec((BLK, d), lambda i: (jnp.minimum(i, nr - 1), 0))
    once = lambda shape: pl.BlockSpec(
        shape, lambda i: (0,) * len(shape), pipeline_mode=pl.Buffered(1)
    )
    weight = lambda a: pl.BlockSpec(
        (None, parts, d, fl), lambda i: (a, 0, 0, 0), pipeline_mode=pl.Buffered(1)
    )
    part = pl.BlockSpec((None, d, fl), lambda i: (jnp.clip(i - nr, 0, parts - 1), 0, 0))
    whole = lambda shape: pl.BlockSpec(shape, lambda i: (0,) * len(shape))
    return pl.pallas_call(
        functools.partial(middle_kernel, nr),
        grid=(nr + parts + 1,),
        out_shape=(
            jax.ShapeDtypeStruct((length, d), BF),
            jax.ShapeDtypeStruct((length, d), BF),
            jax.ShapeDtypeStruct((length, d), F32),
            jax.ShapeDtypeStruct((parts, d, fl), BF),
            jax.ShapeDtypeStruct((parts, d, fl), BF),
            jax.ShapeDtypeStruct((d, d), BF),
            jax.ShapeDtypeStruct((8, d), F32),
            jax.ShapeDtypeStruct((parts, fl), F32),
        ),
        in_specs=[
            pl.BlockSpec(memory_space=pltpu.SMEM),
            rows,
            rows,
            rows,
            once((d, d)),
            weight(1),
            weight(2),
            once((8, d)),
            once((parts, fl)),
        ],
        out_specs=(rows, rows, rows, part, part, whole((d, d)), whole((8, d)), whole((parts, fl))),
        scratch_shapes=[
            pltpu.VMEM((length, d), BF),
            pltpu.VMEM((parts, length, fl), BF),
            pltpu.VMEM((parts, length, fl), BF),
            pltpu.VMEM((parts, BLK, fl), F32),
            pltpu.VMEM((d, length), BF),
            pltpu.VMEM((d, length), BF),
            pltpu.VMEM((d, length), BF),
        ],
        compiler_params=pltpu.CompilerParams(vmem_limit_bytes=VMEM_LIMIT),
        cost_estimate=pl.CostEstimate(
            flops=6 * length * d * (d + 2 * parts * fl),
            bytes_accessed=4 * length * d * 3 + 8 * parts * d * fl,
            transcendentals=2 * length * parts * fl,
        ),
        name="middle",
    )(drop, att, x, cot, wo, w, w, vec, bias_in)


def place(dp):
    yx, core = dp // 2, dp % 2
    y, x = yx // 2, yx % 2
    return yx, core, y * 2 + 1 - x, (1 - y) * 2 + x, 3 - yx


def remote(src, dst, send, recv, dp, z):
    return pltpu.make_async_remote_copy(
        src_ref=src,
        dst_ref=dst,
        send_sem=send,
        recv_sem=recv,
        device_id=(dp, z),
        device_id_type=pl.DeviceIdType.MESH,
    )


def greet(dp, z, yx, core, yx_x, yx_y, nz):
    barrier = pltpu.get_barrier_semaphore()
    others = [(yx_x * 2 + core, z), (yx_y * 2 + core, z), (yx * 2 + 1 - core, z)]
    others += [(dp, (z + k) % nz) for k in range(1, nz)]
    for dev in others:
        pl.semaphore_signal(
            barrier, inc=1, device_id=dev, device_id_type=pl.DeviceIdType.MESH
        )
    pl.semaphore_wait(barrier, len(others))


def inbound_kernel(tok_ref, sh_ref, x_ref, w_ref, send, recv, tsend, trecv, local):
    na, nz = w_ref.shape[0], w_ref.shape[1]
    half = w_ref.shape[4] // 2
    dp, z = lax.axis_index("dp"), lax.axis_index("tensor")
    yx, core, yx_x, yx_y, yx_d = place(dp)
    dev_x, dev_y, dev_c = yx_x * 2 + core, yx_y * 2 + core, yx * 2 + 1 - core
    low, high = pl.ds(0, half), pl.ds(half, half)
    greet(dp, z, yx, core, yx_x, yx_y, nz)

    def blk(a, t, where):
        return w_ref.at[a, t, where, core]

    def mine(a, t, own):
        return sh_ref.at[a] if own else blk(a, t, yx)

    def x_own(a, t, own):
        return remote(mine(a, t, own), blk(a, t, yx), send.at[a, t, 0], recv.at[a, t, 0], dev_x, z)

    def y_own(a, t, own):
        return remote(mine(a, t, own), blk(a, t, yx), send.at[a, t, 1], recv.at[a, t, 1], dev_y, z)

    def c_own(a, t, own):
        return remote(mine(a, t, own), blk(a, t, yx), send.at[a, t, 2], recv.at[a, t, 5], dev_c, z)

    def right(a, t, own):
        return remote(
            mine(a, t, own), blk(a, t, yx), send.at[a, t, 8], recv.at[a, t, 4], dp, (z + 1) % nz
        )

    def left(a, t, own):
        return remote(
            mine(a, t, own), blk(a, t, yx), send.at[a, t, 9], recv.at[a, t, 4], dp, (z + nz - 1) % nz
        )

    def fwd_y(a, t):
        b = blk(a, t, yx_x).at[low]
        return remote(b, b, send.at[a, t, 3], recv.at[a, t, 2], dev_y, z)

    def fwd_x(a, t):
        b = blk(a, t, yx_y).at[high]
        return remote(b, b, send.at[a, t, 4], recv.at[a, t, 3], dev_x, z)

    def c_fwd(a, t, where, kind):
        b = blk(a, t, where)
        return remote(b, b, send.at[a, t, kind], recv.at[a, t, 5], dev_c, z)

    def landed(ref, sem):
        pltpu.make_async_copy(ref, ref, sem).wait()

    def each(body):
        def run(a, carry):
            body(a)
            return carry

        lax.fori_loop(0, na, run, 0)

    def sides(s, body):
        if s == 0:
            body(z, None)
            return

        @pl.when(z >= s)
        def _():
            body(z - s, True)

        @pl.when(z + s < nz)
        def _():
            body(z + s, False)

    def stage1(s, a, t, from_left):
        own = s == 0
        if own:
            pltpu.make_async_copy(sh_ref.at[a], blk(a, t, yx), local.at[a]).start()
        else:
            landed(blk(a, t, yx), recv.at[a, t, 4])
        if own or from_left:

            @pl.when(z < nz - 1)
            def _():
                right(a, t, own).start()

        if own or not from_left:

            @pl.when(z > 0)
            def _():
                left(a, t, own).start()

        x_own(a, t, own).start()
        y_own(a, t, own).start()
        c_own(a, t, own).start()

    def stage2(a, t):
        landed(blk(a, t, yx_x), recv.at[a, t, 0])
        fwd_y(a, t).start()
        c_fwd(a, t, yx_x, 5).start()
        landed(blk(a, t, yx_y), recv.at[a, t, 1])
        fwd_x(a, t).start()
        c_fwd(a, t, yx_y, 6).start()

    def stage3(a, t):
        landed(blk(a, t, yx_d).at[low], recv.at[a, t, 2])
        landed(blk(a, t, yx_d).at[high], recv.at[a, t, 3])
        c_fwd(a, t, yx_d, 7).start()

    def tokens(k):
        to = (z + k) % nz
        return remote(tok_ref.at[to], x_ref.at[z], tsend.at[k], trecv.at[k], dp, to)

    own_tokens = pltpu.make_async_copy(tok_ref.at[z], x_ref.at[z], tsend.at[0])
    own_tokens.start()
    for s in range(nz + 2):
        if s < nz:
            each(lambda a: sides(s, lambda t, fl: stage1(s, a, t, fl)))
        if s == TOKENS_AT:
            for k in range(1, nz):
                tokens(k).start()
        if 1 <= s <= nz:
            each(lambda a: sides(s - 1, lambda t, fl: stage2(a, t)))
        if 2 <= s:
            each(lambda a: sides(s - 2, lambda t, fl: stage3(a, t)))

    def drain(s, a, t, from_left):
        own = s == 0
        landed(w_ref.at[a, t, :, 1 - core], recv.at[a, t, 5])
        if own:
            pltpu.make_async_copy(sh_ref.at[a], blk(a, t, yx), local.at[a]).wait()
        if own or from_left:

            @pl.when(z < nz - 1)
            def _():
                right(a, t, own).wait_send()

        if own or not from_left:

            @pl.when(z > 0)
            def _():
                left(a, t, own).wait_send()

        x_own(a, t, own).wait_send()
        y_own(a, t, own).wait_send()
        c_own(a, t, own).wait_send()
        fwd_y(a, t).wait_send()
        fwd_x(a, t).wait_send()
        c_fwd(a, t, yx_x, 5).wait_send()
        c_fwd(a, t, yx_y, 6).wait_send()
        c_fwd(a, t, yx_d, 7).wait_send()

    for s in range(nz):
        each(lambda a: sides(s, lambda t, fl: drain(s, a, t, fl)))
    own_tokens.wait()
    for k in range(1, nz):
        copy = tokens(k)
        copy.wait_send()
        landed(x_ref.at[(z + nz - k) % nz], trecv.at[k])


TOKENS_AT = 0


def inbound(tokens, shards):
    nz, nd = lax.axis_size("tensor"), lax.axis_size("dp")
    na, rw, wide = shards.shape
    if (nz, nd) != (4, 8):
        x = lax.all_to_all(tokens, "tensor", 0, 0)
        w = lax.all_gather(shards, ("tensor", "dp"), axis=1, tiled=True)
        return x.reshape(-1, x.shape[2]), w.reshape(na, nz, nd * rw, wide)
    x, w = pl.pallas_call(
        inbound_kernel,
        out_shape=(
            jax.ShapeDtypeStruct(tokens.shape, tokens.dtype),
            jax.ShapeDtypeStruct((na, nz, nd // 2, 2, rw, wide), shards.dtype),
        ),
        in_specs=[pl.BlockSpec(memory_space=pl.ANY)] * 2,
        out_specs=(pl.BlockSpec(memory_space=pl.ANY),) * 2,
        scratch_shapes=[
            pltpu.SemaphoreType.DMA((na, nz, 10)),
            pltpu.SemaphoreType.DMA((na, nz, 6)),
            pltpu.SemaphoreType.DMA((nz,)),
            pltpu.SemaphoreType.DMA((nz,)),
            pltpu.SemaphoreType.DMA((na,)),
        ],
        compiler_params=pltpu.CompilerParams(collective_id=0, has_side_effects=True),
        name="inbound",
    )(tokens, shards)
    return x.reshape(-1, x.shape[2]), w.reshape(na, nz, nd * rw, wide)


def outbound_kernel(
    gx_ref, g0_ref, g1_ref, g2_ref, vec_ref, rows_ref, out_ref, vsum_ref,
    own, rc, rda, rdb, rx, ry, rz, vbuf, send, recv, load, tsend, trecv, vsend, vrecv,
):
    na, nz = own.shape[0], own.shape[1]
    half = own.shape[4] // 2
    dp, z = lax.axis_index("dp"), lax.axis_index("tensor")
    yx, core, yx_x, yx_y, yx_d = place(dp)
    dev_x, dev_y, dev_c = yx_x * 2 + core, yx_y * 2 + core, yx * 2 + 1 - core
    low, high = pl.ds(0, half), pl.ds(half, half)
    order = [3 * (1 - z // 2), (2 + 3 * z) % 5, 1 + z % 2, z]

    def loads(a, t):
        g = (g0_ref, g1_ref, g2_ref)[a]
        return pltpu.make_async_copy(g.at[t], own.at[a, t], load.at[a, t])

    for t in order:
        for a in range(na):
            loads(a, t).start()
    vsum_ref[...] = vec_ref[...]
    greet(dp, z, yx, core, yx_x, yx_y, nz)

    def each(body):
        def run(a, carry):
            body(a)
            return carry

        lax.fori_loop(0, na, run, 0)

    def landed(ref, sem):
        pltpu.make_async_copy(ref, ref, sem).wait()

    def add(dst, src):
        dst[...] = (dst[...].astype(F32) + src[...].astype(F32)).astype(BF)

    def c_copy(a, t):
        return remote(
            own.at[a, t, :, 1 - core], rc.at[a, t], send.at[a, t, 0], recv.at[a, t, 0], dev_c, z
        )

    def da_copy(a, t):
        return remote(
            own.at[a, t, yx_d, core, low], rda.at[a, t], send.at[a, t, 1], recv.at[a, t, 1], dev_x, z
        )

    def db_copy(a, t):
        return remote(
            own.at[a, t, yx_d, core, high], rdb.at[a, t], send.at[a, t, 2], recv.at[a, t, 2], dev_y, z
        )

    def x_copy(a, t):
        return remote(
            own.at[a, t, yx_x, core], rx.at[a, t], send.at[a, t, 3], recv.at[a, t, 3], dev_x, z
        )

    def y_copy(a, t):
        return remote(
            own.at[a, t, yx_y, core], ry.at[a, t], send.at[a, t, 4], recv.at[a, t, 4], dev_y, z
        )

    def right(a, t):
        return remote(
            own.at[a, t, yx, core], rz.at[0, a, t], send.at[a, t, 5], recv.at[a, t, 5], dp, (z + 1) % nz
        )

    def left(a, t):
        return remote(
            own.at[a, t, yx, core], rz.at[1, a, t], send.at[a, t, 6], recv.at[a, t, 6], dp,
            (z + nz - 1) % nz,
        )

    def stage1(t):
        for a in range(na):
            loads(a, t).wait()
            c_copy(a, t).start()

    def stage2(a, t):
        landed(rc.at[a, t], recv.at[a, t, 0])
        for q in range(4):
            add(own.at[a, t, q, core], rc.at[a, t, q])
        da_copy(a, t).start()
        db_copy(a, t).start()

    def stage3(a, t):
        landed(rda.at[a, t], recv.at[a, t, 1])
        add(own.at[a, t, yx_y, core, low], rda.at[a, t])
        landed(rdb.at[a, t], recv.at[a, t, 2])
        add(own.at[a, t, yx_x, core, high], rdb.at[a, t])
        x_copy(a, t).start()
        y_copy(a, t).start()

    def stage4(a, t):
        landed(rx.at[a, t], recv.at[a, t, 3])
        landed(ry.at[a, t], recv.at[a, t, 4])
        here = own.at[a, t, yx, core]
        here[...] = (
            here[...].astype(F32) + rx[a, t].astype(F32) + ry[a, t].astype(F32)
        ).astype(BF)

    def pass_right(a, t):
        @pl.when(z > 0)
        def _():
            landed(rz.at[0, a, t], recv.at[a, t, 5])
            add(own.at[a, t, yx, core], rz.at[0, a, t])

        right(a, t).start()

    def pass_left(a, t):
        @pl.when(z < nz - 1)
        def _():
            landed(rz.at[1, a, t], recv.at[a, t, 6])
            add(own.at[a, t, yx, core], rz.at[1, a, t])

        left(a, t).start()

    def stage5(a, t):
        @pl.when(t > z)
        def _():
            pass_right(a, t)

        @pl.when(t < z)
        def _():
            pass_left(a, t)

    def finish(a):
        out_ref[a] = own[a, z, yx, core].astype(F32)

        @pl.when(z > 0)
        def _():
            landed(rz.at[0, a, z], recv.at[a, z, 5])
            out_ref[a] += rz[0, a, z].astype(F32)

        @pl.when(z < nz - 1)
        def _():
            landed(rz.at[1, a, z], recv.at[a, z, 6])
            out_ref[a] += rz[1, a, z].astype(F32)

    def rows(k):
        to = (z + k) % nz
        return remote(gx_ref.at[to], rows_ref.at[z], tsend.at[k], trecv.at[k], dp, to)

    partners = [(dev_c, z), (dev_x, z), (dev_y, z)]
    partners += [(dp, z + 1 - 2 * (z % 2)), (dp, (z + 2) % nz)]

    def vec_copy(k):
        return remote(vbuf.at[0, k], vbuf.at[1, k], vsend.at[k], vrecv.at[k], *partners[k])

    def vec_start(k):
        vbuf[0, k] = vsum_ref[...]
        vec_copy(k).start()

    def vec_finish(k):
        landed(vbuf.at[1, k], vrecv.at[k])
        vsum_ref[...] += vbuf[1, k]

    own_rows = pltpu.make_async_copy(gx_ref.at[z], rows_ref.at[z], tsend.at[0])
    own_rows.start()
    for k in range(1, nz):
        rows(k).start()
    vec_start(0)
    for k in range(nz):
        stage1(order[k])
    for k in range(nz + 3):
        if k < nz:
            each(lambda a: stage2(a, order[k]))
        if 1 <= k <= nz:
            each(lambda a: stage3(a, order[k - 1]))
        if k < len(partners):
            vec_finish(k)
            if k + 1 < len(partners):
                vec_start(k + 1)
        if 2 <= k <= nz + 1:
            each(lambda a: stage4(a, order[k - 2]))
        if 3 <= k <= nz + 1:
            each(lambda a: stage5(a, order[k - 3]))
    each(finish)

    def drain(k):
        t = order[k]

        def body(a):
            c_copy(a, t).wait_send()
            da_copy(a, t).wait_send()
            db_copy(a, t).wait_send()
            x_copy(a, t).wait_send()
            y_copy(a, t).wait_send()

            @pl.when(t > z)
            def _():
                right(a, t).wait_send()

            @pl.when(t < z)
            def _():
                left(a, t).wait_send()

        each(body)

    for k in range(nz):
        drain(k)
    for k in range(len(partners)):
        vec_copy(k).wait_send()
    own_rows.wait()
    for k in range(1, nz):
        rows(k).wait_send()
        landed(rows_ref.at[(z + nz - k) % nz], trecv.at[k])


def outbound(gx, grads, vec):
    nz, nd = lax.axis_size("tensor"), lax.axis_size("dp")
    length, d = gx.shape
    gx = gx.reshape(nz, length // nz, d)
    rw, wide = d // nd, grads[0].shape[2]
    if (nz, nd) != (4, 8):
        axes = ("tensor", "dp")
        rows = lax.all_to_all(gx, "tensor", 0, 0)
        parts = [
            lax.psum_scatter(g.reshape(nz * d, wide), axes, scatter_dimension=0, tiled=True)
            for g in grads
        ]
        return rows, [p.astype(F32) for p in parts], lax.psum(vec, axes)
    na = len(grads)
    unit = (nd // 2, 2, rw, wide)
    any_ = pl.BlockSpec(memory_space=pl.ANY)
    vmem = pl.BlockSpec(memory_space=pltpu.VMEM)
    dma = pltpu.SemaphoreType.DMA
    steps = 5
    rows, out, vsum = pl.pallas_call(
        outbound_kernel,
        out_shape=(
            jax.ShapeDtypeStruct(gx.shape, gx.dtype),
            jax.ShapeDtypeStruct((na, rw, wide), F32),
            jax.ShapeDtypeStruct(vec.shape, F32),
        ),
        in_specs=[any_] * 4 + [vmem],
        out_specs=(any_, vmem, vmem),
        scratch_shapes=[
            pltpu.VMEM((na, nz) + unit, BF),
            pltpu.VMEM((na, nz, nd // 2, rw, wide), BF),
            pltpu.VMEM((na, nz, rw // 2, wide), BF),
            pltpu.VMEM((na, nz, rw // 2, wide), BF),
            pltpu.VMEM((na, nz, rw, wide), BF),
            pltpu.VMEM((na, nz, rw, wide), BF),
            pltpu.VMEM((2, na, nz, rw, wide), BF),
            pltpu.VMEM((2, steps) + vec.shape, F32),
            dma((na, nz, 7)),
            dma((na, nz, 7)),
            dma((na, nz)),
            dma((nz,)),
            dma((nz,)),
            dma((steps,)),
            dma((steps,)),
        ],
        compiler_params=pltpu.CompilerParams(
            collective_id=1, has_side_effects=True, vmem_limit_bytes=VMEM_LIMIT
        ),
        name="outbound",
    )(gx, *(g.reshape((nz,) + unit) for g in grads), vec)
    return rows, [out[a] for a in range(na)], vsum


def project_kernel(x_ref, mix_ref, bias_ref, qkv_ref, w_ref, wo_ref):
    nz, d, wide = mix_ref.shape
    wl = wide // 4
    for j in range(4):
        whole = jnp.concatenate(
            [mix_ref[t, :, j * wl : (j + 1) * wl] for t in range(nz)], axis=1
        )
        if j < 3:
            w_ref[:, j * d : (j + 1) * d] = whole
        else:
            wo_ref[...] = whole
    n = x_ref.shape[0] // BLK

    def body(i, carry):
        at = pl.ds(pl.multiple_of(i * BLK, BLK), BLK)
        qkv_ref[at, :] = (dot_nn(x_ref[at, :], w_ref[...]) + bias_ref[...]).astype(BF)
        return carry

    lax.fori_loop(0, n, body, 0)


def project(x, w, bias):
    length, d = x.shape
    na, nz, _, wide = w.shape
    full = lambda shape: pl.BlockSpec(shape, lambda i: (0,) * len(shape))
    return pl.pallas_call(
        project_kernel,
        grid=(1,),
        out_shape=(
            jax.ShapeDtypeStruct((length, 3 * d), BF),
            jax.ShapeDtypeStruct((d, 3 * d), BF),
            jax.ShapeDtypeStruct((d, d), BF),
        ),
        in_specs=[
            full((length, d)),
            pl.BlockSpec((None, nz, d, wide), lambda i: (0, 0, 0, 0)),
            full((1, 3 * d)),
        ],
        out_specs=(full((length, 3 * d)), full((d, 3 * d)), full((d, d))),
        compiler_params=pltpu.CompilerParams(vmem_limit_bytes=VMEM_LIMIT),
        cost_estimate=pl.CostEstimate(
            flops=6 * length * d * d, bytes_accessed=10 * length * d + 14 * d * d, transcendentals=0
        ),
        name="project",
    )(x, w, bias)


def project_back_kernel(
    drop_ref, x_ref, cot_ref, ghpre_ref, gq_ref, gk_ref, gv_ref, w_ref, gwo_ref,
    gx_ref, gmix_ref, sums_ref, xt,
):
    nz, d, wide = gmix_ref.shape
    wl = wide // 4
    n = x_ref.shape[0] // BLK
    grads = (gq_ref, gk_ref, gv_ref)
    dropped = drop_ref[0] == 1

    def body(i, carry):
        at = pl.ds(pl.multiple_of(i * BLK, BLK), BLK)
        total = ghpre_ref[at, :] + jnp.where(dropped, cot_ref[at, :].astype(F32), 0.0)
        for j, g in enumerate(grads):
            total = total + dot_nt(g[at, :], w_ref[:, j * d : (j + 1) * d])
        gx_ref[at, :] = total.astype(BF)
        return carry

    lax.fori_loop(0, n, body, 0)
    for i in range(n):
        xt[:, i * BLK : (i + 1) * BLK] = jnp.transpose(x_ref[i * BLK : (i + 1) * BLK, :])
    sums_ref[...] = jnp.zeros_like(sums_ref)
    for j, g in enumerate(grads):
        grad = dot_nn(xt[...], g[...]).astype(BF)
        for t in range(nz):
            gmix_ref[t, :, j * wl : (j + 1) * wl] = grad[:, t * wl : (t + 1) * wl]
        sums_ref[j : j + 1, :] = jnp.sum(g[...].astype(F32), axis=0, keepdims=True)
    for t in range(nz):
        gmix_ref[t, :, 3 * wl :] = gwo_ref[:, t * wl : (t + 1) * wl]


def project_back(drop, x, cot, g_hpre, gq, gk, gv, wqkv, gwo, nz):
    length, d = x.shape
    wide = 4 * d // nz
    vmem = pl.BlockSpec(memory_space=pltpu.VMEM)
    return pl.pallas_call(
        project_back_kernel,
        out_shape=(
            jax.ShapeDtypeStruct((length, d), BF),
            jax.ShapeDtypeStruct((nz, d, wide), BF),
            jax.ShapeDtypeStruct((8, d), F32),
        ),
        in_specs=[pl.BlockSpec(memory_space=pltpu.SMEM)] + [vmem] * 8,
        out_specs=(vmem,) * 3,
        scratch_shapes=[pltpu.VMEM((d, length), BF)],
        compiler_params=pltpu.CompilerParams(vmem_limit_bytes=VMEM_LIMIT),
        cost_estimate=pl.CostEstimate(
            flops=12 * length * d * d, bytes_accessed=18 * length * d + 14 * d * d, transcendentals=0
        ),
        name="project_back",
    )(drop, x, cot, g_hpre, gq, gk, gv, wqkv, gwo)


def block_range(seg):
    length = seg.shape[0]
    n = length // BLK
    blocks = seg.reshape(n, BLK)
    start = jnp.sum(seg[None, :] < blocks[:, :1], axis=1)
    end = jnp.sum(seg[None, :] <= blocks[:, -1:], axis=1)
    return (start // BLK).astype(jnp.int32), ((end + BLK - 1) // BLK).astype(jnp.int32)


def on_device(
    tokens, segment_ids, drop_flags, qkv_w, qv_b, wo_w, wo_b, gain1, shift1,
    up_w, up_b, dn_w, dn_b, gain2, shift2, cotangent,
):
    me = lax.axis_index("tensor")
    nt = lax.axis_size("tensor")
    d = tokens.shape[2]
    length = segment_ids.shape[1]
    rw, wl = qkv_w.shape[1], qkv_w.shape[2]
    fl = up_w.shape[1]
    n = length // BLK

    mix = jnp.concatenate((qkv_w[0], qkv_w[1], qkv_w[2], wo_w.T), axis=1)
    x, w = inbound(tokens, jnp.stack((mix, up_w, dn_w.T)))
    cotangent, x = lax.optimization_barrier((cotangent, x))
    cot = lax.all_to_all(cotangent, "tensor", 0, 0).reshape(length, d)

    seg = lax.dynamic_index_in_dim(segment_ids, me, 0, keepdims=False)
    drop = lax.dynamic_slice_in_dim(drop_flags, me, 1)
    lo, hi = block_range(seg)
    segc = jnp.broadcast_to(seg[:, None], (length, 128))
    segr = seg.reshape(n, 1, BLK)
    bias = jnp.concatenate((qv_b[0], jnp.zeros((d,), F32), qv_b[1]))
    zero_row = jnp.zeros((d,), F32)
    vec = jnp.stack((wo_b, gain1, shift1, dn_b, gain2, shift2, zero_row, zero_row))

    qkv, wqkv, wo = project(x, w, bias[None])
    att, lse = attend(qkv, lo, hi, segc, segr)
    layer, g_att, g_hpre, gup, gdn, gwo, vecg, bing = middle(
        drop, att, x, cot, wo, w, vec, up_b.reshape(nt, fl)
    )
    layer_out = lax.all_to_all(layer.reshape(nt, length // nt, d), "tensor", 0, 0)
    gq, gk, gv = attend_back(qkv, att, g_att, lse, lo, hi, segc, segr)
    gx, gmix, sums = project_back(drop, x, cot, g_hpre, gq, gk, gv, wqkv, gwo, nt)
    flat = jnp.concatenate(
        (vecg[:6].reshape(-1), bing.reshape(-1), sums[0], sums[2])
    )
    pad = -flat.shape[0] % (8 * 128)
    flat_size = flat.shape[0]
    flat = jnp.concatenate((flat, jnp.zeros((pad,), F32))).reshape(-1, 128)
    rows, (g_mix, g_up, g_dn), total = outbound(gx, (gmix, gup, gdn), flat)
    total = total.reshape(-1)[:flat_size]
    vecs = total[: 6 * d].reshape(6, d)
    g_bin = total[6 * d : 6 * d + nt * fl]
    return (
        layer_out,
        rows.astype(F32),
        jnp.stack([g_mix[:, j * wl : (j + 1) * wl] for j in range(3)]),
        total[6 * d + nt * fl :].reshape(2, d),
        g_mix[:, 3 * wl :].T,
        vecs[0],
        vecs[1],
        vecs[2],
        g_up,
        g_bin,
        g_dn.T,
        vecs[3],
        vecs[4],
        vecs[5],
    )


def solution(mesh):
    rows = P("dp", "tensor", None)
    return jax.shard_map(
        on_device,
        mesh=mesh,
        in_specs=(
            rows, P("dp", None), P("dp"), P(None, "dp", "tensor"), P(), P("tensor", "dp"), P(), P(), P(),
            P("dp", "tensor"), P(), P("tensor", "dp"), P(), P(), P(), rows,
        ),
        out_specs=(
            rows, rows, P(None, "dp", "tensor"), P(), P("tensor", "dp"), P(), P(), P(),
            P("dp", "tensor"), P(), P("tensor", "dp"), P(), P(), P(),
        ),
        check_vma=False,
    )
```

```python
import functools
import jax
import jax.numpy as jnp
from jax import lax
from jax.experimental import pallas as pl
from jax.experimental.pallas import tpu as pltpu
from jax.sharding import PartitionSpec as P

HD = 64
EPS = 1e-05
NEG = -1000000000.0
BF = jnp.bfloat16
F32 = jnp.float32
VMEM_LIMIT = 60 * 1024 * 1024
BLK = 256


def dot_nn(a, b):
    return jnp.dot(a, b, preferred_element_type=F32)


def dot_nt(a, b):
    return lax.dot_general(a, b, (((1,), (1,)), ((), ())), preferred_element_type=F32)


def dot_tn(a, b):
    return lax.dot_general(a, b, (((0,), (0,)), ((), ())), preferred_element_type=F32)


WIDTHS = (384, 512, 640, 768, 1024)
LANES = 128


def rows_at(i, size):
    return pl.ds(pl.multiple_of(i * size, size), size)


def doc_lanes(segc_ref, kx_s, qx_s):
    lane = lax.broadcasted_iota(jnp.int32, segc_ref.shape, 1)
    same = (segc_ref[...] == lane).astype(F32)
    kx_s[:, LANES:] = same.astype(BF)
    qx_s[:, LANES:] = ((1.0 - same) * NEG).astype(BF)


def split_heads(pair):
    first = lax.broadcasted_iota(jnp.int32, pair.shape, 1) % (2 * HD) < HD
    zero = jnp.zeros((), pair.dtype)
    return jnp.where(first, pair, zero), jnp.where(first, zero, pair)


def attend_kernel(lo_ref, kind_ref, q_ref, k_ref, v_ref, segc_ref, o_ref, lse_ref, kx_s, qx_s, vt_s):
    length = q_ref.shape[0]

    @pl.when(pl.program_id(0) == 0)
    def _():
        doc_lanes(segc_ref, kx_s, qx_s)
        vt_s[:, HD:, :] = jnp.ones((2, vt_s.shape[1] - HD, length), BF)

    kx_s[:, :LANES] = k_ref[...]
    qx_s[:, :LANES] = (q_ref[...].astype(F32) * 0.125).astype(BF)
    vt = jnp.transpose(v_ref[...])
    vt_s[0, :HD, :] = vt[:HD, :]
    vt_s[1, :HD, :] = vt[HD:, :]

    def block(i, width):
        at = rows_at(i, BLK)
        keys = pl.ds(pl.multiple_of(lo_ref[i] * LANES, LANES), width)
        kx = kx_s[keys, :]
        ext = qx_s[at, LANES:]
        outs, lses = [], []
        scores = [
            dot_nt(kx, jnp.concatenate((q, ext), axis=1)) for q in split_heads(qx_s[at, :LANES])
        ]
        for h in range(2):
            top = jnp.max(scores[h], axis=0, keepdims=True)
            p = jnp.exp(scores[h] - top).astype(BF)
            o = dot_nn(vt_s[h, :, keys], p)
            total = o[HD : HD + 1, :]
            outs.append(o[:HD, :] / total)
            lses.append(top + jnp.log(total))
        o_ref[at, :] = jnp.transpose(jnp.concatenate(outs, axis=0)).astype(BF)
        lse_ref[:, at] = jnp.concatenate(lses, axis=0)

    def step(i, carry):
        for c, width in enumerate(WIDTHS):

            @pl.when(kind_ref[i] == c)
            def _():
                block(i, width)

        return carry

    lax.fori_loop(0, length // BLK, step, 0)


def attend_specs(length, d):
    pairs = d // LANES
    col = lambda off: pl.BlockSpec((length, LANES), lambda p, *_: (0, off + p))
    seg = pl.BlockSpec((length, LANES), lambda p, *_: (0, 0))
    lse = pl.BlockSpec((None, 2, length), lambda p, *_: (p, 0, 0))
    return pairs, col, seg, lse


def attend(qkv, lo, kind, segc):
    length, wide = qkv.shape
    d = wide // 3
    pairs, col, seg, lse = attend_specs(length, d)
    return pl.pallas_call(
        attend_kernel,
        out_shape=(
            jax.ShapeDtypeStruct((length, d), BF),
            jax.ShapeDtypeStruct((pairs, 2, length), F32),
        ),
        grid_spec=pltpu.PrefetchScalarGridSpec(
            num_scalar_prefetch=2,
            grid=(pairs,),
            in_specs=[col(0), col(pairs), col(2 * pairs), seg],
            out_specs=[col(0), lse],
            scratch_shapes=[
                pltpu.VMEM((length, 2 * LANES), BF),
                pltpu.VMEM((length, 2 * LANES), BF),
                pltpu.VMEM((2, HD + 16, length), BF),
            ],
        ),
        compiler_params=pltpu.CompilerParams(vmem_limit_bytes=VMEM_LIMIT),
        cost_estimate=pl.CostEstimate(
            flops=4 * length * length * d,
            bytes_accessed=8 * length * d,
            transcendentals=length * length * d // HD // 2,
        ),
        name="attend_forward",
    )(lo, kind, qkv, qkv, qkv, segc)


def attend_back_kernel(
    lo_ref, kind_ref, q_ref, k_ref, v_ref, att_ref, g_ref, lse_ref, segc_ref,
    gq_ref, gk_ref, gv_ref, kx_s, qx_s, kt_s, delta_s, dk_s, dv_s,
):
    length = q_ref.shape[0]

    @pl.when(pl.program_id(0) == 0)
    def _():
        doc_lanes(segc_ref, kx_s, qx_s)

    kx_s[:, :LANES] = k_ref[...]
    qx_s[:, :LANES] = (q_ref[...].astype(F32) * 0.125).astype(BF)
    kt_s[...] = jnp.transpose(k_ref[...])
    sub = lax.broadcasted_iota(jnp.int32, (8, LANES), 0)
    lane = lax.broadcasted_iota(jnp.int32, (8, LANES), 1)
    pick = jnp.where(lane // HD == sub, 1.0, 0.0).astype(F32)
    prod = g_ref[...].astype(F32) * att_ref[...].astype(F32)
    delta_s[...] = lax.dot_general(
        pick, prod, (((1,), (1,)), ((), ())),
        preferred_element_type=F32, precision=lax.Precision.HIGHEST,
    )
    dk_s[...] = jnp.zeros_like(dk_s)
    dv_s[...] = jnp.zeros_like(dv_s)

    def block(i, width):
        at = rows_at(i, BLK)
        keys = pl.ds(pl.multiple_of(lo_ref[i] * LANES, LANES), width)
        kx = kx_s[keys, :]
        v = v_ref[keys, :]
        ext = qx_s[at, LANES:]
        qs = split_heads(qx_s[at, :LANES])
        gs = split_heads(g_ref[at, :])
        ps, ds, dq = [], [], []
        for h in range(2):
            s = dot_nt(kx, jnp.concatenate((qs[h], ext), axis=1))
            p = jnp.exp(s - lse_ref[h : h + 1, at])
            dp = dot_nt(v, gs[h])
            d = (p * (dp - delta_s[h : h + 1, at])).astype(BF)
            ps.append(p.astype(BF))
            ds.append(d)
            dq.append(dot_nn(kt_s[h * HD : (h + 1) * HD, keys], d))
        dv_s[keys, :] += dot_nn(jnp.concatenate(ps, axis=1), jnp.concatenate(gs, axis=0))
        dk_s[keys, :] += dot_nn(jnp.concatenate(ds, axis=1), jnp.concatenate(qs, axis=0))
        gq_ref[at, :] = (jnp.transpose(jnp.concatenate(dq, axis=0)) * 0.125).astype(BF)

    def step(i, carry):
        for c, width in enumerate(WIDTHS):

            @pl.when(kind_ref[i] == c)
            def _():
                block(i, width)

        return carry

    lax.fori_loop(0, length // BLK, step, 0)
    gk_ref[...] = dk_s[...].astype(BF)
    gv_ref[...] = dv_s[...].astype(BF)


def attend_back(qkv, att, g_att, lse_rows, lo, kind, segc):
    length, wide = qkv.shape
    d = wide // 3
    pairs, col, seg, lse = attend_specs(length, d)
    return pl.pallas_call(
        attend_back_kernel,
        out_shape=[jax.ShapeDtypeStruct((length, d), BF)] * 3,
        grid_spec=pltpu.PrefetchScalarGridSpec(
            num_scalar_prefetch=2,
            grid=(pairs,),
            in_specs=[col(0), col(pairs), col(2 * pairs), col(0), col(0), lse, seg],
            out_specs=[col(0)] * 3,
            scratch_shapes=[
                pltpu.VMEM((length, 2 * LANES), BF),
                pltpu.VMEM((length, 2 * LANES), BF),
                pltpu.VMEM((LANES, length), BF),
                pltpu.VMEM((8, length), F32),
                pltpu.VMEM((length, LANES), F32),
                pltpu.VMEM((length, LANES), F32),
            ],
        ),
        compiler_params=pltpu.CompilerParams(vmem_limit_bytes=VMEM_LIMIT),
        cost_estimate=pl.CostEstimate(
            flops=10 * length * length * d,
            bytes_accessed=16 * length * d,
            transcendentals=length * length * d // HD // 2,
        ),
        name="attend_backward",
    )(lo, kind, qkv, qkv, qkv, att, g_att, lse_rows, segc)


def gelu_parts(u):
    e = jnp.exp(-0.5 * u * u)
    t = 1.0 / (1.0 + (0.3275911 * 0.7071067811865476) * jnp.abs(u))
    poly = t * (
        0.5 * 0.254829592
        + t * (0.5 * -0.284496736 + t * (0.5 * 1.421413741 + t * (0.5 * -1.453152027 + t * (0.5 * 1.061405429))))
    )
    tail = poly * e
    cdf = jnp.where(u < 0.0, tail, 1.0 - tail)
    return u * cdf, cdf + u * e * 0.3989422804014327


def norm_rows(v):
    mean = jnp.mean(v, axis=-1, keepdims=True)
    c = v - mean
    inv = lax.rsqrt(jnp.mean(c * c, axis=-1, keepdims=True) + EPS)
    return c * inv, inv


def norm_back(g, normed, inv, gain):
    gn = g * gain
    return inv * (
        gn
        - jnp.mean(gn, axis=-1, keepdims=True)
        - normed * jnp.mean(gn * normed, axis=-1, keepdims=True)
    )


def middle_kernel(
    row_steps, drop_ref, att_ref, x_ref, cot_ref, wo_ref, up_ref, dn_ref, vec_ref, bin_ref,
    lo_ref, gatt_ref, ghpre_ref, gup_ref, gdn_ref, gwo_ref, vecg_ref, bing_ref,
    att_s, act_s, gpre_s, slope_s, ht_s, gb2t_s, gbt_s,
):
    step = pl.program_id(0)
    parts = up_ref.shape[0]

    @pl.when(step == 0)
    def _():
        vecg_ref[...] = jnp.zeros_like(vecg_ref)
        bing_ref[...] = jnp.zeros_like(bing_ref)

    @pl.when(step < row_steps)
    def _():
        at = pl.ds(pl.multiple_of(step * BLK, BLK), BLK)
        vec = lambda r: vec_ref[r : r + 1, :]
        dropped = drop_ref[0] == 1
        att = att_ref[...]
        att_s[at, :] = att
        x = x_ref[...].astype(F32)
        branch = dot_nt(att, wo_ref[...]) + vec(0)
        n1, inv1 = norm_rows(x + branch)
        hidden = n1 * vec(1) + vec(2)
        low = hidden.astype(BF)
        ht_s[:, at] = jnp.transpose(low)
        ffn = hidden + vec(3)
        for t in range(parts):
            pre = dot_nn(low, up_ref[t]) + bin_ref[t : t + 1, :]
            act, slope = gelu_parts(pre)
            act = act.astype(BF)
            act_s[t, at, :] = act
            slope_s[t] = slope
            ffn = ffn + dot_nt(act, dn_ref[t])
        n2, inv2 = norm_rows(ffn)
        final = n2 * vec(4) + vec(5)
        lo_ref[...] = jnp.where(dropped, x, final).astype(BF)
        g_final = jnp.where(dropped, 0.0, cot_ref[...].astype(F32))
        g_fpre = norm_back(g_final, n2, inv2, vec(4))
        gb2 = g_fpre.astype(BF)
        gb2t_s[:, at] = jnp.transpose(gb2)
        g_hidden = g_fpre
        for t in range(parts):
            gpre = (dot_nn(gb2, dn_ref[t]) * slope_s[t]).astype(BF)
            gpre_s[t, at, :] = gpre
            bing_ref[t : t + 1, :] += jnp.sum(gpre.astype(F32), axis=0, keepdims=True)
            g_hidden = g_hidden + dot_nt(gpre, up_ref[t])
        g_hpre = norm_back(g_hidden, n1, inv1, vec(1))
        gb = g_hpre.astype(BF)
        gbt_s[:, at] = jnp.transpose(gb)
        gatt_ref[...] = dot_nn(gb, wo_ref[...]).astype(BF)
        ghpre_ref[...] = g_hpre
        for r, v in enumerate(
            (gb.astype(F32), g_hidden * n1, g_hidden, gb2.astype(F32), g_final * n2, g_final)
        ):
            vecg_ref[r : r + 1, :] += jnp.sum(v, axis=0, keepdims=True)

    for t in range(parts):

        @pl.when(step == row_steps + t)
        def _():
            gup_ref[...] = dot_nn(ht_s[...], gpre_s[t]).astype(BF)
            gdn_ref[...] = dot_nn(gb2t_s[...], act_s[t]).astype(BF)

    @pl.when(step == row_steps + parts)
    def _():
        gwo_ref[...] = dot_nn(gbt_s[...], att_s[...]).astype(BF)


def middle(drop, att, x, cot, wo, w, vec, bias_in):
    length, d = att.shape
    _, parts, _, fl = w.shape
    nr = length // BLK
    rows = pl.BlockSpec((BLK, d), lambda i: (jnp.minimum(i, nr - 1), 0))
    once = lambda shape: pl.BlockSpec(
        shape, lambda i: (0,) * len(shape), pipeline_mode=pl.Buffered(1)
    )
    weight = lambda a: pl.BlockSpec(
        (None, parts, d, fl), lambda i: (a, 0, 0, 0), pipeline_mode=pl.Buffered(1)
    )
    part = pl.BlockSpec((None, d, fl), lambda i: (jnp.clip(i - nr, 0, parts - 1), 0, 0))
    whole = lambda shape: pl.BlockSpec(shape, lambda i: (0,) * len(shape))
    return pl.pallas_call(
        functools.partial(middle_kernel, nr),
        grid=(nr + parts + 1,),
        out_shape=(
            jax.ShapeDtypeStruct((length, d), BF),
            jax.ShapeDtypeStruct((length, d), BF),
            jax.ShapeDtypeStruct((length, d), F32),
            jax.ShapeDtypeStruct((parts, d, fl), BF),
            jax.ShapeDtypeStruct((parts, d, fl), BF),
            jax.ShapeDtypeStruct((d, d), BF),
            jax.ShapeDtypeStruct((8, d), F32),
            jax.ShapeDtypeStruct((parts, fl), F32),
        ),
        in_specs=[
            pl.BlockSpec(memory_space=pltpu.SMEM),
            rows,
            rows,
            rows,
            once((d, d)),
            weight(1),
            weight(2),
            once((8, d)),
            once((parts, fl)),
        ],
        out_specs=(rows, rows, rows, part, part, whole((d, d)), whole((8, d)), whole((parts, fl))),
        scratch_shapes=[
            pltpu.VMEM((length, d), BF),
            pltpu.VMEM((parts, length, fl), BF),
            pltpu.VMEM((parts, length, fl), BF),
            pltpu.VMEM((parts, BLK, fl), F32),
            pltpu.VMEM((d, length), BF),
            pltpu.VMEM((d, length), BF),
            pltpu.VMEM((d, length), BF),
        ],
        compiler_params=pltpu.CompilerParams(vmem_limit_bytes=VMEM_LIMIT),
        cost_estimate=pl.CostEstimate(
            flops=6 * length * d * (d + 2 * parts * fl),
            bytes_accessed=4 * length * d * 3 + 8 * parts * d * fl,
            transcendentals=2 * length * parts * fl,
        ),
        name="middle",
    )(drop, att, x, cot, wo, w, w, vec, bias_in)


def place(dp):
    yx, core = dp // 2, dp % 2
    y, x = yx // 2, yx % 2
    return yx, core, y * 2 + 1 - x, (1 - y) * 2 + x, 3 - yx


def remote(src, dst, send, recv, dp, z):
    return pltpu.make_async_remote_copy(
        src_ref=src,
        dst_ref=dst,
        send_sem=send,
        recv_sem=recv,
        device_id=(dp, z),
        device_id_type=pl.DeviceIdType.MESH,
    )


def greet(dp, z, yx, core, yx_x, yx_y, nz):
    barrier = pltpu.get_barrier_semaphore()
    others = [(yx_x * 2 + core, z), (yx_y * 2 + core, z), (yx * 2 + 1 - core, z)]
    others += [(dp, (z + k) % nz) for k in range(1, nz)]
    for dev in others:
        pl.semaphore_signal(
            barrier, inc=1, device_id=dev, device_id_type=pl.DeviceIdType.MESH
        )
    pl.semaphore_wait(barrier, len(others))


def inbound_kernel(tok_ref, sh_ref, x_ref, w_ref, send, recv, tsend, trecv, local):
    na, nz = w_ref.shape[0], w_ref.shape[1]
    half = w_ref.shape[4] // 2
    dp, z = lax.axis_index("dp"), lax.axis_index("tensor")
    yx, core, yx_x, yx_y, yx_d = place(dp)
    dev_x, dev_y, dev_c = yx_x * 2 + core, yx_y * 2 + core, yx * 2 + 1 - core
    low, high = pl.ds(0, half), pl.ds(half, half)
    greet(dp, z, yx, core, yx_x, yx_y, nz)

    def blk(a, t, where):
        return w_ref.at[a, t, where, core]

    def mine(a, t, own):
        return sh_ref.at[a] if own else blk(a, t, yx)

    def x_own(a, t, own):
        return remote(mine(a, t, own), blk(a, t, yx), send.at[a, t, 0], recv.at[a, t, 0], dev_x, z)

    def y_own(a, t, own):
        return remote(mine(a, t, own), blk(a, t, yx), send.at[a, t, 1], recv.at[a, t, 1], dev_y, z)

    def c_own(a, t, own):
        return remote(mine(a, t, own), blk(a, t, yx), send.at[a, t, 2], recv.at[a, t, 5], dev_c, z)

    def right(a, t, own):
        return remote(
            mine(a, t, own), blk(a, t, yx), send.at[a, t, 8], recv.at[a, t, 4], dp, (z + 1) % nz
        )

    def left(a, t, own):
        return remote(
            mine(a, t, own), blk(a, t, yx), send.at[a, t, 9], recv.at[a, t, 4], dp, (z + nz - 1) % nz
        )

    def fwd_y(a, t):
        b = blk(a, t, yx_x).at[low]
        return remote(b, b, send.at[a, t, 3], recv.at[a, t, 2], dev_y, z)

    def fwd_x(a, t):
        b = blk(a, t, yx_y).at[high]
        return remote(b, b, send.at[a, t, 4], recv.at[a, t, 3], dev_x, z)

    def c_fwd(a, t, where, kind):
        b = blk(a, t, where)
        return remote(b, b, send.at[a, t, kind], recv.at[a, t, 5], dev_c, z)

    def landed(ref, sem):
        pltpu.make_async_copy(ref, ref, sem).wait()

    def each(body):
        def run(a, carry):
            body(a)
            return carry

        lax.fori_loop(0, na, run, 0)

    def sides(s, body):
        if s == 0:
            body(z, None)
            return

        @pl.when(z >= s)
        def _():
            body(z - s, True)

        @pl.when(z + s < nz)
        def _():
            body(z + s, False)

    def stage1(s, a, t, from_left):
        own = s == 0
        if own:
            pltpu.make_async_copy(sh_ref.at[a], blk(a, t, yx), local.at[a]).start()
        else:
            landed(blk(a, t, yx), recv.at[a, t, 4])
        if own or from_left:

            @pl.when(z < nz - 1)
            def _():
                right(a, t, own).start()

        if own or not from_left:

            @pl.when(z > 0)
            def _():
                left(a, t, own).start()

        x_own(a, t, own).start()
        y_own(a, t, own).start()
        c_own(a, t, own).start()

    def stage2(a, t):
        landed(blk(a, t, yx_x), recv.at[a, t, 0])
        fwd_y(a, t).start()
        c_fwd(a, t, yx_x, 5).start()
        landed(blk(a, t, yx_y), recv.at[a, t, 1])
        fwd_x(a, t).start()
        c_fwd(a, t, yx_y, 6).start()

    def stage3(a, t):
        landed(blk(a, t, yx_d).at[low], recv.at[a, t, 2])
        landed(blk(a, t, yx_d).at[high], recv.at[a, t, 3])
        c_fwd(a, t, yx_d, 7).start()

    def tokens(k):
        to = (z + k) % nz
        return remote(tok_ref.at[to], x_ref.at[z], tsend.at[k], trecv.at[k], dp, to)

    own_tokens = pltpu.make_async_copy(tok_ref.at[z], x_ref.at[z], tsend.at[0])
    own_tokens.start()
    for s in range(nz + 2):
        if s < nz:
            each(lambda a: sides(s, lambda t, fl: stage1(s, a, t, fl)))
        if s == TOKENS_AT:
            for k in range(1, nz):
                tokens(k).start()
        if 1 <= s <= nz:
            each(lambda a: sides(s - 1, lambda t, fl: stage2(a, t)))
        if 2 <= s:
            each(lambda a: sides(s - 2, lambda t, fl: stage3(a, t)))

    def drain(s, a, t, from_left):
        own = s == 0
        landed(w_ref.at[a, t, :, 1 - core], recv.at[a, t, 5])
        if own:
            pltpu.make_async_copy(sh_ref.at[a], blk(a, t, yx), local.at[a]).wait()
        if own or from_left:

            @pl.when(z < nz - 1)
            def _():
                right(a, t, own).wait_send()

        if own or not from_left:

            @pl.when(z > 0)
            def _():
                left(a, t, own).wait_send()

        x_own(a, t, own).wait_send()
        y_own(a, t, own).wait_send()
        c_own(a, t, own).wait_send()
        fwd_y(a, t).wait_send()
        fwd_x(a, t).wait_send()
        c_fwd(a, t, yx_x, 5).wait_send()
        c_fwd(a, t, yx_y, 6).wait_send()
        c_fwd(a, t, yx_d, 7).wait_send()

    for s in range(nz):
        each(lambda a: sides(s, lambda t, fl: drain(s, a, t, fl)))
    own_tokens.wait()
    for k in range(1, nz):
        copy = tokens(k)
        copy.wait_send()
        landed(x_ref.at[(z + nz - k) % nz], trecv.at[k])


TOKENS_AT = 0


def inbound(tokens, shards):
    nz, nd = lax.axis_size("tensor"), lax.axis_size("dp")
    na, rw, wide = shards.shape
    if (nz, nd) != (4, 8):
        x = lax.all_to_all(tokens, "tensor", 0, 0)
        w = lax.all_gather(shards, ("tensor", "dp"), axis=1, tiled=True)
        return x.reshape(-1, x.shape[2]), w.reshape(na, nz, nd * rw, wide)
    x, w = pl.pallas_call(
        inbound_kernel,
        out_shape=(
            jax.ShapeDtypeStruct(tokens.shape, tokens.dtype),
            jax.ShapeDtypeStruct((na, nz, nd // 2, 2, rw, wide), shards.dtype),
        ),
        in_specs=[pl.BlockSpec(memory_space=pl.ANY)] * 2,
        out_specs=(pl.BlockSpec(memory_space=pl.ANY),) * 2,
        scratch_shapes=[
            pltpu.SemaphoreType.DMA((na, nz, 10)),
            pltpu.SemaphoreType.DMA((na, nz, 6)),
            pltpu.SemaphoreType.DMA((nz,)),
            pltpu.SemaphoreType.DMA((nz,)),
            pltpu.SemaphoreType.DMA((na,)),
        ],
        compiler_params=pltpu.CompilerParams(collective_id=0, has_side_effects=True),
        name="inbound",
    )(tokens, shards)
    return x.reshape(-1, x.shape[2]), w.reshape(na, nz, nd * rw, wide)


def outbound_kernel(
    gx_ref, g0_ref, g1_ref, g2_ref, vec_ref, rows_ref, out_ref, vsum_ref,
    own, rc, rda, rdb, rx, ry, rz, vbuf, send, recv, load, tsend, trecv, vsend, vrecv,
):
    na, nz = own.shape[0], own.shape[1]
    half = own.shape[4] // 2
    dp, z = lax.axis_index("dp"), lax.axis_index("tensor")
    yx, core, yx_x, yx_y, yx_d = place(dp)
    dev_x, dev_y, dev_c = yx_x * 2 + core, yx_y * 2 + core, yx * 2 + 1 - core
    low, high = pl.ds(0, half), pl.ds(half, half)
    order = [3 * (1 - z // 2), (2 + 3 * z) % 5, 1 + z % 2, z]

    def loads(a, t):
        g = (g0_ref, g1_ref, g2_ref)[a]
        return pltpu.make_async_copy(g.at[t], own.at[a, t], load.at[a, t])

    for t in order:
        for a in range(na):
            loads(a, t).start()
    vsum_ref[...] = vec_ref[...]
    greet(dp, z, yx, core, yx_x, yx_y, nz)

    def each(body):
        def run(a, carry):
            body(a)
            return carry

        lax.fori_loop(0, na, run, 0)

    def landed(ref, sem):
        pltpu.make_async_copy(ref, ref, sem).wait()

    def add(dst, src):
        dst[...] = (dst[...].astype(F32) + src[...].astype(F32)).astype(BF)

    def c_copy(a, t):
        return remote(
            own.at[a, t, :, 1 - core], rc.at[a, t], send.at[a, t, 0], recv.at[a, t, 0], dev_c, z
        )

    def da_copy(a, t):
        return remote(
            own.at[a, t, yx_d, core, low], rda.at[a, t], send.at[a, t, 1], recv.at[a, t, 1], dev_x, z
        )

    def db_copy(a, t):
        return remote(
            own.at[a, t, yx_d, core, high], rdb.at[a, t], send.at[a, t, 2], recv.at[a, t, 2], dev_y, z
        )

    def x_copy(a, t):
        return remote(
            own.at[a, t, yx_x, core], rx.at[a, t], send.at[a, t, 3], recv.at[a, t, 3], dev_x, z
        )

    def y_copy(a, t):
        return remote(
            own.at[a, t, yx_y, core], ry.at[a, t], send.at[a, t, 4], recv.at[a, t, 4], dev_y, z
        )

    def right(a, t):
        return remote(
            own.at[a, t, yx, core], rz.at[0, a, t], send.at[a, t, 5], recv.at[a, t, 5], dp, (z + 1) % nz
        )

    def left(a, t):
        return remote(
            own.at[a, t, yx, core], rz.at[1, a, t], send.at[a, t, 6], recv.at[a, t, 6], dp,
            (z + nz - 1) % nz,
        )

    def stage1(t):
        for a in range(na):
            loads(a, t).wait()
            c_copy(a, t).start()

    def stage2(a, t):
        landed(rc.at[a, t], recv.at[a, t, 0])
        for q in range(4):
            add(own.at[a, t, q, core], rc.at[a, t, q])
        da_copy(a, t).start()
        db_copy(a, t).start()

    def stage3(a, t):
        landed(rda.at[a, t], recv.at[a, t, 1])
        add(own.at[a, t, yx_y, core, low], rda.at[a, t])
        landed(rdb.at[a, t], recv.at[a, t, 2])
        add(own.at[a, t, yx_x, core, high], rdb.at[a, t])
        x_copy(a, t).start()
        y_copy(a, t).start()

    def stage4(a, t):
        landed(rx.at[a, t], recv.at[a, t, 3])
        landed(ry.at[a, t], recv.at[a, t, 4])
        here = own.at[a, t, yx, core]
        here[...] = (
            here[...].astype(F32) + rx[a, t].astype(F32) + ry[a, t].astype(F32)
        ).astype(BF)

    def pass_right(a, t):
        @pl.when(z > 0)
        def _():
            landed(rz.at[0, a, t], recv.at[a, t, 5])
            add(own.at[a, t, yx, core], rz.at[0, a, t])

        right(a, t).start()

    def pass_left(a, t):
        @pl.when(z < nz - 1)
        def _():
            landed(rz.at[1, a, t], recv.at[a, t, 6])
            add(own.at[a, t, yx, core], rz.at[1, a, t])

        left(a, t).start()

    def stage5(a, t):
        @pl.when(t > z)
        def _():
            pass_right(a, t)

        @pl.when(t < z)
        def _():
            pass_left(a, t)

    def finish(a):
        out_ref[a] = own[a, z, yx, core].astype(F32)

        @pl.when(z > 0)
        def _():
            landed(rz.at[0, a, z], recv.at[a, z, 5])
            out_ref[a] += rz[0, a, z].astype(F32)

        @pl.when(z < nz - 1)
        def _():
            landed(rz.at[1, a, z], recv.at[a, z, 6])
            out_ref[a] += rz[1, a, z].astype(F32)

    def rows(k):
        to = (z + k) % nz
        return remote(gx_ref.at[to], rows_ref.at[z], tsend.at[k], trecv.at[k], dp, to)

    partners = [(dev_c, z), (dev_x, z), (dev_y, z)]
    partners += [(dp, z + 1 - 2 * (z % 2)), (dp, (z + 2) % nz)]

    def vec_copy(k):
        return remote(vbuf.at[0, k], vbuf.at[1, k], vsend.at[k], vrecv.at[k], *partners[k])

    def vec_start(k):
        vbuf[0, k] = vsum_ref[...]
        vec_copy(k).start()

    def vec_finish(k):
        landed(vbuf.at[1, k], vrecv.at[k])
        vsum_ref[...] += vbuf[1, k]

    own_rows = pltpu.make_async_copy(gx_ref.at[z], rows_ref.at[z], tsend.at[0])
    own_rows.start()
    for k in range(1, nz):
        rows(k).start()
    vec_start(0)
    for k in range(nz):
        stage1(order[k])
    for k in range(nz + 3):
        if k < nz:
            each(lambda a: stage2(a, order[k]))
        if 1 <= k <= nz:
            each(lambda a: stage3(a, order[k - 1]))
        if k < len(partners):
            vec_finish(k)
            if k + 1 < len(partners):
                vec_start(k + 1)
        if 2 <= k <= nz + 1:
            each(lambda a: stage4(a, order[k - 2]))
        if 3 <= k <= nz + 1:
            each(lambda a: stage5(a, order[k - 3]))
    each(finish)

    def drain(k):
        t = order[k]

        def body(a):
            c_copy(a, t).wait_send()
            da_copy(a, t).wait_send()
            db_copy(a, t).wait_send()
            x_copy(a, t).wait_send()
            y_copy(a, t).wait_send()

            @pl.when(t > z)
            def _():
                right(a, t).wait_send()

            @pl.when(t < z)
            def _():
                left(a, t).wait_send()

        each(body)

    for k in range(nz):
        drain(k)
    for k in range(len(partners)):
        vec_copy(k).wait_send()
    own_rows.wait()
    for k in range(1, nz):
        rows(k).wait_send()
        landed(rows_ref.at[(z + nz - k) % nz], trecv.at[k])


def outbound(gx, grads, vec):
    nz, nd = lax.axis_size("tensor"), lax.axis_size("dp")
    length, d = gx.shape
    gx = gx.reshape(nz, length // nz, d)
    rw, wide = d // nd, grads[0].shape[2]
    if (nz, nd) != (4, 8):
        axes = ("tensor", "dp")
        rows = lax.all_to_all(gx, "tensor", 0, 0)
        parts = [
            lax.psum_scatter(g.reshape(nz * d, wide), axes, scatter_dimension=0, tiled=True)
            for g in grads
        ]
        return rows, [p.astype(F32) for p in parts], lax.psum(vec, axes)
    na = len(grads)
    unit = (nd // 2, 2, rw, wide)
    any_ = pl.BlockSpec(memory_space=pl.ANY)
    vmem = pl.BlockSpec(memory_space=pltpu.VMEM)
    dma = pltpu.SemaphoreType.DMA
    steps = 5
    rows, out, vsum = pl.pallas_call(
        outbound_kernel,
        out_shape=(
            jax.ShapeDtypeStruct(gx.shape, gx.dtype),
            jax.ShapeDtypeStruct((na, rw, wide), F32),
            jax.ShapeDtypeStruct(vec.shape, F32),
        ),
        in_specs=[any_] * 4 + [vmem],
        out_specs=(any_, vmem, vmem),
        scratch_shapes=[
            pltpu.VMEM((na, nz) + unit, BF),
            pltpu.VMEM((na, nz, nd // 2, rw, wide), BF),
            pltpu.VMEM((na, nz, rw // 2, wide), BF),
            pltpu.VMEM((na, nz, rw // 2, wide), BF),
            pltpu.VMEM((na, nz, rw, wide), BF),
            pltpu.VMEM((na, nz, rw, wide), BF),
            pltpu.VMEM((2, na, nz, rw, wide), BF),
            pltpu.VMEM((2, steps) + vec.shape, F32),
            dma((na, nz, 7)),
            dma((na, nz, 7)),
            dma((na, nz)),
            dma((nz,)),
            dma((nz,)),
            dma((steps,)),
            dma((steps,)),
        ],
        compiler_params=pltpu.CompilerParams(
            collective_id=1, has_side_effects=True, vmem_limit_bytes=VMEM_LIMIT
        ),
        name="outbound",
    )(gx, *(g.reshape((nz,) + unit) for g in grads), vec)
    return rows, [out[a] for a in range(na)], vsum


def project_kernel(x_ref, mix_ref, bias_ref, qkv_ref, w_ref, wo_ref):
    nz, d, wide = mix_ref.shape
    wl = wide // 4
    for j in range(4):
        whole = jnp.concatenate(
            [mix_ref[t, :, j * wl : (j + 1) * wl] for t in range(nz)], axis=1
        )
        if j < 3:
            w_ref[:, j * d : (j + 1) * d] = whole
        else:
            wo_ref[...] = whole
    n = x_ref.shape[0] // BLK

    def body(i, carry):
        at = pl.ds(pl.multiple_of(i * BLK, BLK), BLK)
        qkv_ref[at, :] = (dot_nn(x_ref[at, :], w_ref[...]) + bias_ref[...]).astype(BF)
        return carry

    lax.fori_loop(0, n, body, 0)


def project(x, w, bias):
    length, d = x.shape
    na, nz, _, wide = w.shape
    full = lambda shape: pl.BlockSpec(shape, lambda i: (0,) * len(shape))
    return pl.pallas_call(
        project_kernel,
        grid=(1,),
        out_shape=(
            jax.ShapeDtypeStruct((length, 3 * d), BF),
            jax.ShapeDtypeStruct((d, 3 * d), BF),
            jax.ShapeDtypeStruct((d, d), BF),
        ),
        in_specs=[
            full((length, d)),
            pl.BlockSpec((None, nz, d, wide), lambda i: (0, 0, 0, 0)),
            full((1, 3 * d)),
        ],
        out_specs=(full((length, 3 * d)), full((d, 3 * d)), full((d, d))),
        compiler_params=pltpu.CompilerParams(vmem_limit_bytes=VMEM_LIMIT),
        cost_estimate=pl.CostEstimate(
            flops=6 * length * d * d, bytes_accessed=10 * length * d + 14 * d * d, transcendentals=0
        ),
        name="project",
    )(x, w, bias)


def project_back_kernel(
    drop_ref, x_ref, cot_ref, ghpre_ref, gq_ref, gk_ref, gv_ref, w_ref, gwo_ref,
    gx_ref, gmix_ref, sums_ref, xt,
):
    nz, d, wide = gmix_ref.shape
    wl = wide // 4
    n = x_ref.shape[0] // BLK
    grads = (gq_ref, gk_ref, gv_ref)
    dropped = drop_ref[0] == 1

    def body(i, carry):
        at = pl.ds(pl.multiple_of(i * BLK, BLK), BLK)
        total = ghpre_ref[at, :] + jnp.where(dropped, cot_ref[at, :].astype(F32), 0.0)
        for j, g in enumerate(grads):
            total = total + dot_nt(g[at, :], w_ref[:, j * d : (j + 1) * d])
        gx_ref[at, :] = total.astype(BF)
        return carry

    lax.fori_loop(0, n, body, 0)
    for i in range(n):
        xt[:, i * BLK : (i + 1) * BLK] = jnp.transpose(x_ref[i * BLK : (i + 1) * BLK, :])
    sums_ref[...] = jnp.zeros_like(sums_ref)
    for j, g in enumerate(grads):
        grad = dot_nn(xt[...], g[...]).astype(BF)
        for t in range(nz):
            gmix_ref[t, :, j * wl : (j + 1) * wl] = grad[:, t * wl : (t + 1) * wl]
        sums_ref[j : j + 1, :] = jnp.sum(g[...].astype(F32), axis=0, keepdims=True)
    for t in range(nz):
        gmix_ref[t, :, 3 * wl :] = gwo_ref[:, t * wl : (t + 1) * wl]


def project_back(drop, x, cot, g_hpre, gq, gk, gv, wqkv, gwo, nz):
    length, d = x.shape
    wide = 4 * d // nz
    vmem = pl.BlockSpec(memory_space=pltpu.VMEM)
    return pl.pallas_call(
        project_back_kernel,
        out_shape=(
            jax.ShapeDtypeStruct((length, d), BF),
            jax.ShapeDtypeStruct((nz, d, wide), BF),
            jax.ShapeDtypeStruct((8, d), F32),
        ),
        in_specs=[pl.BlockSpec(memory_space=pltpu.SMEM)] + [vmem] * 8,
        out_specs=(vmem,) * 3,
        scratch_shapes=[pltpu.VMEM((d, length), BF)],
        compiler_params=pltpu.CompilerParams(vmem_limit_bytes=VMEM_LIMIT),
        cost_estimate=pl.CostEstimate(
            flops=12 * length * d * d, bytes_accessed=18 * length * d + 14 * d * d, transcendentals=0
        ),
        name="project_back",
    )(drop, x, cot, g_hpre, gq, gk, gv, wqkv, gwo)


def block_range(seg):
    length = seg.shape[0]
    blocks = seg.reshape(length // BLK, BLK)
    start = jnp.sum(seg[None, :] < blocks[:, :1], axis=1) // LANES
    end = (jnp.sum(seg[None, :] <= blocks[:, -1:], axis=1) + LANES - 1) // LANES
    tiles = jnp.array([w // LANES for w in WIDTHS], jnp.int32)
    kind = jnp.sum((end - start)[:, None] > tiles[None, :], axis=1)
    lo = jnp.minimum(start, length // LANES - tiles[kind])
    return lo.astype(jnp.int32), kind.astype(jnp.int32)


def on_device(
    tokens, segment_ids, drop_flags, qkv_w, qv_b, wo_w, wo_b, gain1, shift1,
    up_w, up_b, dn_w, dn_b, gain2, shift2, cotangent,
):
    me = lax.axis_index("tensor")
    nt = lax.axis_size("tensor")
    d = tokens.shape[2]
    length = segment_ids.shape[1]
    rw, wl = qkv_w.shape[1], qkv_w.shape[2]
    fl = up_w.shape[1]

    mix = jnp.concatenate((qkv_w[0], qkv_w[1], qkv_w[2], wo_w.T), axis=1)
    x, w = inbound(tokens, jnp.stack((mix, up_w, dn_w.T)))
    cotangent, x = lax.optimization_barrier((cotangent, x))
    cot = lax.all_to_all(cotangent, "tensor", 0, 0).reshape(length, d)

    seg = lax.dynamic_index_in_dim(segment_ids, me, 0, keepdims=False)
    drop = lax.dynamic_slice_in_dim(drop_flags, me, 1)
    lo, kind = block_range(seg)
    segc = jnp.broadcast_to(seg[:, None], (length, 128))
    bias = jnp.concatenate((qv_b[0], jnp.zeros((d,), F32), qv_b[1]))
    zero_row = jnp.zeros((d,), F32)
    vec = jnp.stack((wo_b, gain1, shift1, dn_b, gain2, shift2, zero_row, zero_row))

    qkv, wqkv, wo = project(x, w, bias[None])
    att, lse = attend(qkv, lo, kind, segc)
    layer, g_att, g_hpre, gup, gdn, gwo, vecg, bing = middle(
        drop, att, x, cot, wo, w, vec, up_b.reshape(nt, fl)
    )
    layer_out = lax.all_to_all(layer.reshape(nt, length // nt, d), "tensor", 0, 0)
    gq, gk, gv = attend_back(qkv, att, g_att, lse, lo, kind, segc)
    gx, gmix, sums = project_back(drop, x, cot, g_hpre, gq, gk, gv, wqkv, gwo, nt)
    flat = jnp.concatenate(
        (vecg[:6].reshape(-1), bing.reshape(-1), sums[0], sums[2])
    )
    pad = -flat.shape[0] % (8 * 128)
    flat_size = flat.shape[0]
    flat = jnp.concatenate((flat, jnp.zeros((pad,), F32))).reshape(-1, 128)
    rows, (g_mix, g_up, g_dn), total = outbound(gx, (gmix, gup, gdn), flat)
    total = total.reshape(-1)[:flat_size]
    vecs = total[: 6 * d].reshape(6, d)
    g_bin = total[6 * d : 6 * d + nt * fl]
    return (
        layer_out,
        rows.astype(F32),
        jnp.stack([g_mix[:, j * wl : (j + 1) * wl] for j in range(3)]),
        total[6 * d + nt * fl :].reshape(2, d),
        g_mix[:, 3 * wl :].T,
        vecs[0],
        vecs[1],
        vecs[2],
        g_up,
        g_bin,
        g_dn.T,
        vecs[3],
        vecs[4],
        vecs[5],
    )


def solution(mesh):
    rows = P("dp", "tensor", None)
    return jax.shard_map(
        on_device,
        mesh=mesh,
        in_specs=(
            rows, P("dp", None), P("dp"), P(None, "dp", "tensor"), P(), P("tensor", "dp"), P(), P(), P(),
            P("dp", "tensor"), P(), P("tensor", "dp"), P(), P(), P(), rows,
        ),
        out_specs=(
            rows, rows, P(None, "dp", "tensor"), P(), P("tensor", "dp"), P(), P(), P(),
            P("dp", "tensor"), P(), P("tensor", "dp"), P(), P(), P(),
        ),
        check_vma=False,
    )
```

```python
import functools
import jax
import jax.numpy as jnp
from jax import lax
from jax.experimental import pallas as pl
from jax.experimental.pallas import tpu as pltpu
from jax.sharding import PartitionSpec as P

HD = 64
EPS = 1e-05
NEG = -1000000000.0
BF = jnp.bfloat16
F32 = jnp.float32
VMEM_LIMIT = 60 * 1024 * 1024
BLK = 256
LANES = 128


def dot_nn(a, b):
    return jnp.dot(a, b, preferred_element_type=F32)


def dot_nt(a, b):
    return lax.dot_general(a, b, (((1,), (1,)), ((), ())), preferred_element_type=F32)


def dot_tn(a, b):
    return lax.dot_general(a, b, (((0,), (0,)), ((), ())), preferred_element_type=F32)


def doc_lanes(segc_ref, kx_s, qx_s):
    lane = lax.broadcasted_iota(jnp.int32, segc_ref.shape, 1)
    same = (segc_ref[...] == lane).astype(F32)
    kx_s[:, LANES:] = same.astype(BF)
    qx_s[:, LANES:] = ((1.0 - same) * NEG).astype(BF)


def split_heads(pair):
    first = lax.broadcasted_iota(jnp.int32, pair.shape, 1) % (2 * HD) < HD
    zero = jnp.zeros((), pair.dtype)
    return jnp.where(first, pair, zero), jnp.where(first, zero, pair)


def attend_pair(q, k, v, kx_s, qx_s, vt_s):
    kx_s[:, :LANES] = k
    qx_s[:, :LANES] = (q.astype(F32) * 0.125).astype(BF)
    vt = jnp.transpose(v)
    vt_s[0, :HD, :] = vt[:HD, :]
    vt_s[1, :HD, :] = vt[HD:, :]
    kx = kx_s[...]
    ext = qx_s[:, LANES:]
    outs, lses = [], []
    scores = [
        dot_nt(kx, jnp.concatenate((h, ext), axis=1)) for h in split_heads(qx_s[:, :LANES])
    ]
    for h in range(2):
        top = jnp.max(scores[h], axis=0, keepdims=True)
        p = jnp.exp(scores[h] - top).astype(BF)
        o = dot_nn(vt_s[h], p)
        total = o[HD : HD + 1, :]
        outs.append(o[:HD, :] / total)
        lses.append(top + jnp.log(total))
    return jnp.transpose(jnp.concatenate(outs, axis=0)).astype(BF), jnp.concatenate(lses, axis=0)


def attend_pair_back(q_ref, k_ref, v_ref, att_ref, g_ref, lse, kx_s, qx_s, kt_s, delta_s, dk_s, dv_s, put_q):
    length = q_ref.shape[0]
    kx_s[:, :LANES] = k_ref[...]
    qx_s[:, :LANES] = (q_ref[...].astype(F32) * 0.125).astype(BF)
    kt_s[...] = jnp.transpose(k_ref[...])
    sub = lax.broadcasted_iota(jnp.int32, (8, LANES), 0)
    lane = lax.broadcasted_iota(jnp.int32, (8, LANES), 1)
    pick = jnp.where(lane // HD == sub, 1.0, 0.0).astype(F32)
    prod = g_ref[...].astype(F32) * att_ref[...].astype(F32)
    delta_s[...] = lax.dot_general(
        pick, prod, (((1,), (1,)), ((), ())),
        preferred_element_type=F32, precision=lax.Precision.HIGHEST,
    )
    for i in range(length // QB):
        at = slice(i * QB, (i + 1) * QB)
        kx = kx_s[...]
        v = v_ref[...]
        ext = qx_s[at, LANES:]
        qs = split_heads(qx_s[at, :LANES])
        gs = split_heads(g_ref[at, :])
        ps, ds, dq = [], [], []
        for h in range(2):
            s = dot_nt(kx, jnp.concatenate((qs[h], ext), axis=1))
            p = jnp.exp(s - lse[h : h + 1, at])
            dp = dot_nt(v, gs[h])
            d = (p * (dp - delta_s[h : h + 1, at])).astype(BF)
            ps.append(p.astype(BF))
            ds.append(d)
            dq.append(dot_nn(kt_s[h * HD : (h + 1) * HD, :], d))
        dv = dot_nn(jnp.concatenate(ps, axis=1), jnp.concatenate(gs, axis=0))
        dk = dot_nn(jnp.concatenate(ds, axis=1), jnp.concatenate(qs, axis=0))
        dv_s[...] = dv if i == 0 else dv_s[...] + dv
        dk_s[...] = dk if i == 0 else dk_s[...] + dk
        put_q(at, (jnp.transpose(jnp.concatenate(dq, axis=0)) * 0.125).astype(BF))


QB = 512


def gelu_parts(u):
    e = jnp.exp(-0.5 * u * u)
    t = 1.0 / (1.0 + (0.3275911 * 0.7071067811865476) * jnp.abs(u))
    poly = t * (
        0.5 * 0.254829592
        + t * (0.5 * -0.284496736 + t * (0.5 * 1.421413741 + t * (0.5 * -1.453152027 + t * (0.5 * 1.061405429))))
    )
    tail = poly * e
    cdf = jnp.where(u < 0.0, tail, 1.0 - tail)
    return u * cdf, cdf + u * e * 0.3989422804014327


def norm_rows(v):
    mean = jnp.mean(v, axis=-1, keepdims=True)
    c = v - mean
    inv = lax.rsqrt(jnp.mean(c * c, axis=-1, keepdims=True) + EPS)
    return c * inv, inv


def norm_back(g, normed, inv, gain):
    gn = g * gain
    return inv * (
        gn
        - jnp.mean(gn, axis=-1, keepdims=True)
        - normed * jnp.mean(gn * normed, axis=-1, keepdims=True)
    )


def middle_kernel(
    row_steps, drop_ref, att_ref, x_ref, cot_ref, wo_ref, up_ref, dn_ref, vec_ref, bin_ref,
    lo_ref, gatt_ref, ghpre_ref, gup_ref, gdn_ref, gwo_ref, vecg_ref, bing_ref,
    att_s, act_s, gpre_s, slope_s, ht_s, gb2t_s, gbt_s,
):
    step = pl.program_id(0)
    parts = up_ref.shape[0]

    @pl.when(step == 0)
    def _():
        vecg_ref[...] = jnp.zeros_like(vecg_ref)
        bing_ref[...] = jnp.zeros_like(bing_ref)

    @pl.when(step < row_steps)
    def _():
        at = pl.ds(pl.multiple_of(step * BLK, BLK), BLK)
        vec = lambda r: vec_ref[r : r + 1, :]
        dropped = drop_ref[0] == 1
        att = att_ref[...]
        att_s[at, :] = att
        x = x_ref[...].astype(F32)
        branch = dot_nt(att, wo_ref[...]) + vec(0)
        n1, inv1 = norm_rows(x + branch)
        hidden = n1 * vec(1) + vec(2)
        low = hidden.astype(BF)
        ht_s[:, at] = jnp.transpose(low)
        ffn = hidden + vec(3)
        for t in range(parts):
            pre = dot_nn(low, up_ref[t]) + bin_ref[t : t + 1, :]
            act, slope = gelu_parts(pre)
            act = act.astype(BF)
            act_s[t, at, :] = act
            slope_s[t] = slope
            ffn = ffn + dot_nt(act, dn_ref[t])
        n2, inv2 = norm_rows(ffn)
        final = n2 * vec(4) + vec(5)
        lo_ref[...] = jnp.where(dropped, x, final).astype(BF)
        g_final = jnp.where(dropped, 0.0, cot_ref[...].astype(F32))
        g_fpre = norm_back(g_final, n2, inv2, vec(4))
        gb2 = g_fpre.astype(BF)
        gb2t_s[:, at] = jnp.transpose(gb2)
        g_hidden = g_fpre
        for t in range(parts):
            gpre = (dot_nn(gb2, dn_ref[t]) * slope_s[t]).astype(BF)
            gpre_s[t, at, :] = gpre
            bing_ref[t : t + 1, :] += jnp.sum(gpre.astype(F32), axis=0, keepdims=True)
            g_hidden = g_hidden + dot_nt(gpre, up_ref[t])
        g_hpre = norm_back(g_hidden, n1, inv1, vec(1))
        gb = g_hpre.astype(BF)
        gbt_s[:, at] = jnp.transpose(gb)
        gatt_ref[...] = dot_nn(gb, wo_ref[...]).astype(BF)
        ghpre_ref[...] = g_hpre + jnp.where(dropped, cot_ref[...].astype(F32), 0.0)
        for r, v in enumerate(
            (gb.astype(F32), g_hidden * n1, g_hidden, gb2.astype(F32), g_final * n2, g_final)
        ):
            vecg_ref[r : r + 1, :] += jnp.sum(v, axis=0, keepdims=True)

    for t in range(parts):

        @pl.when(step == row_steps + t)
        def _():
            gup_ref[...] = dot_nn(ht_s[...], gpre_s[t]).astype(BF)
            gdn_ref[...] = dot_nn(gb2t_s[...], act_s[t]).astype(BF)

    @pl.when(step == row_steps + parts)
    def _():
        gwo_ref[...] = dot_nn(gbt_s[...], att_s[...]).astype(BF)


def middle(drop, att, x, cot, wo, w, vec, bias_in):
    length, d = att.shape
    _, parts, _, fl = w.shape
    nr = length // BLK
    rows = pl.BlockSpec((BLK, d), lambda i: (jnp.minimum(i, nr - 1), 0))
    once = lambda shape: pl.BlockSpec(
        shape, lambda i: (0,) * len(shape), pipeline_mode=pl.Buffered(1)
    )
    weight = lambda a: pl.BlockSpec(
        (None, parts, d, fl), lambda i: (a, 0, 0, 0), pipeline_mode=pl.Buffered(1)
    )
    part = pl.BlockSpec((None, d, fl), lambda i: (jnp.clip(i - nr, 0, parts - 1), 0, 0))
    whole = lambda shape: pl.BlockSpec(shape, lambda i: (0,) * len(shape))
    return pl.pallas_call(
        functools.partial(middle_kernel, nr),
        grid=(nr + parts + 1,),
        out_shape=(
            jax.ShapeDtypeStruct((length, d), BF),
            jax.ShapeDtypeStruct((length, d), BF),
            jax.ShapeDtypeStruct((length, d), F32),
            jax.ShapeDtypeStruct((parts, d, fl), BF),
            jax.ShapeDtypeStruct((parts, d, fl), BF),
            jax.ShapeDtypeStruct((d, d), BF),
            jax.ShapeDtypeStruct((8, d), F32),
            jax.ShapeDtypeStruct((parts, fl), F32),
        ),
        in_specs=[
            pl.BlockSpec(memory_space=pltpu.SMEM),
            rows,
            rows,
            rows,
            once((d, d)),
            weight(0),
            weight(1),
            once((8, d)),
            once((parts, fl)),
        ],
        out_specs=(rows, rows, rows, part, part, whole((d, d)), whole((8, d)), whole((parts, fl))),
        scratch_shapes=[
            pltpu.VMEM((length, d), BF),
            pltpu.VMEM((parts, length, fl), BF),
            pltpu.VMEM((parts, length, fl), BF),
            pltpu.VMEM((parts, BLK, fl), F32),
            pltpu.VMEM((d, length), BF),
            pltpu.VMEM((d, length), BF),
            pltpu.VMEM((d, length), BF),
        ],
        compiler_params=pltpu.CompilerParams(vmem_limit_bytes=VMEM_LIMIT),
        cost_estimate=pl.CostEstimate(
            flops=6 * length * d * (d + 2 * parts * fl),
            bytes_accessed=4 * length * d * 3 + 8 * parts * d * fl,
            transcendentals=2 * length * parts * fl,
        ),
        name="middle",
    )(drop, att, x, cot, wo, w, w, vec, bias_in)


def place(dp):
    yx, core = dp // 2, dp % 2
    y, x = yx // 2, yx % 2
    return yx, core, y * 2 + 1 - x, (1 - y) * 2 + x, 3 - yx


def remote(src, dst, send, recv, dp, z):
    return pltpu.make_async_remote_copy(
        src_ref=src,
        dst_ref=dst,
        send_sem=send,
        recv_sem=recv,
        device_id=(dp, z),
        device_id_type=pl.DeviceIdType.MESH,
    )


def greet(dp, z, yx, core, yx_x, yx_y, nz):
    barrier = pltpu.get_barrier_semaphore()
    others = [(yx_x * 2 + core, z), (yx_y * 2 + core, z), (yx * 2 + 1 - core, z)]
    others += [(dp, (z + k) % nz) for k in range(1, nz)]
    for dev in others:
        pl.semaphore_signal(
            barrier, inc=1, device_id=dev, device_id_type=pl.DeviceIdType.MESH
        )
    pl.semaphore_wait(barrier, len(others))


def landed(ref, sem):
    pltpu.make_async_copy(ref, ref, sem).wait()


class Here:
    def __init__(self, nz):
        self.nz = nz
        self.dp, self.z = lax.axis_index("dp"), lax.axis_index("tensor")
        self.yx, self.core, self.yx_x, self.yx_y, self.yx_d = place(self.dp)
        self.dev_x = self.yx_x * 2 + self.core
        self.dev_y = self.yx_y * 2 + self.core
        self.dev_c = self.yx * 2 + 1 - self.core

    def greet(self):
        greet(self.dp, self.z, self.yx, self.core, self.yx_x, self.yx_y, self.nz)

    def sides(self, s, body):
        if s == 0:
            body(self.z, None)
            return

        @pl.when(self.z >= s)
        def _():
            body(self.z - s, True)

        @pl.when(self.z + s < self.nz)
        def _():
            body(self.z + s, False)


class Exchange:
    def __init__(self, here, src, dst, send, recv):
        self.here, self.src, self.dst, self.send, self.recv = here, src, dst, send, recv

    def copy(self, k):
        h = self.here
        to = (h.z + k) % h.nz
        return remote(
            self.src.at[to], self.dst.at[h.z], self.send.at[k], self.recv.at[k], h.dp, to
        )

    def own(self):
        z = self.here.z
        return pltpu.make_async_copy(self.src.at[z], self.dst.at[z], self.send.at[0])

    def start(self):
        self.own().start()
        for k in range(1, self.here.nz):
            self.copy(k).start()

    def wait_recv(self):
        h = self.here
        self.own().wait()
        for k in range(1, h.nz):
            landed(self.dst.at[(h.z + h.nz - k) % h.nz], self.recv.at[k])

    def wait_send(self):
        for k in range(1, self.here.nz):
            self.copy(k).wait_send()


class Gather:
    def __init__(self, here, w_ref, sh_ref, first, count, send, recv, local):
        self.here, self.w, self.sh, self.first, self.count = here, w_ref, sh_ref, first, count
        self.send, self.recv, self.local = send, recv, local

    def blk(self, a, t, yx):
        return self.w.at[a, t, yx, self.here.core]

    def copy(self, src, dst, a, t, sender, receiver, dp, z):
        f = self.first + a
        return remote(src, dst, self.send.at[f, t, sender], self.recv.at[f, t, receiver], dp, z)

    def firsts(self, a, t, own):
        h = self.here
        dst = self.blk(a, t, h.yx)
        src = self.sh.at[self.first + a] if own else dst
        return (
            lambda: self.copy(src, dst, a, t, 0, 0, h.dev_x, h.z),
            lambda: self.copy(src, dst, a, t, 1, 1, h.dev_y, h.z),
            lambda: self.copy(src, dst, a, t, 2, 5, h.dev_c, h.z),
            lambda: self.copy(src, dst, a, t, 8, 4, h.dp, (h.z + 1) % h.nz),
            lambda: self.copy(src, dst, a, t, 9, 4, h.dp, (h.z + h.nz - 1) % h.nz),
        )

    def own_copy(self, a, t):
        return pltpu.make_async_copy(
            self.sh.at[self.first + a], self.blk(a, t, self.here.yx), self.local.at[self.first + a]
        )

    def halves(self, a, t):
        h = self.here
        half = self.w.shape[4] // 2
        to_y = self.blk(a, t, h.yx_x).at[pl.ds(0, half)]
        to_x = self.blk(a, t, h.yx_y).at[pl.ds(half, half)]
        return (
            self.copy(to_y, to_y, a, t, 3, 2, h.dev_y, h.z),
            self.copy(to_x, to_x, a, t, 4, 3, h.dev_x, h.z),
        )

    def to_core(self, a, t, yx, kind):
        b = self.blk(a, t, yx)
        return self.copy(b, b, a, t, kind, 5, self.here.dev_c, self.here.z)

    def each(self, s, body):
        def run(a, carry):
            self.here.sides(s, lambda t, from_left: body(a, t, from_left))
            return carry

        lax.fori_loop(0, self.count, run, 0)

    def along(self, own, from_left, right, left):
        h = self.here
        if own or from_left:
            pl.when(h.z < h.nz - 1)(right)
        if own or not from_left:
            pl.when(h.z > 0)(left)

    def stage1(self, s):
        h, own = self.here, s == 0

        def body(a, t, from_left):
            if own:
                self.own_copy(a, t).start()
            else:
                landed(self.blk(a, t, h.yx), self.recv.at[self.first + a, t, 4])
            x, y, c, right, left = self.firsts(a, t, own)
            self.along(own, from_left, lambda: right().start(), lambda: left().start())
            x().start()
            y().start()
            c().start()

        self.each(s, body)

    def stage2(self, s):
        h = self.here

        def body(a, t, from_left):
            f = self.first + a
            to_y, to_x = self.halves(a, t)
            landed(self.blk(a, t, h.yx_x), self.recv.at[f, t, 0])
            to_y.start()
            self.to_core(a, t, h.yx_x, 5).start()
            landed(self.blk(a, t, h.yx_y), self.recv.at[f, t, 1])
            to_x.start()
            self.to_core(a, t, h.yx_y, 6).start()

        self.each(s, body)

    def stage3(self, s):
        h = self.here
        half = self.w.shape[4] // 2

        def body(a, t, from_left):
            f = self.first + a
            b = self.blk(a, t, h.yx_d)
            landed(b.at[pl.ds(0, half)], self.recv.at[f, t, 2])
            landed(b.at[pl.ds(half, half)], self.recv.at[f, t, 3])
            self.to_core(a, t, h.yx_d, 7).start()

        self.each(s, body)

    def drain(self):
        h = self.here
        for s in range(h.nz):
            own = s == 0

            def body(a, t, from_left):
                landed(self.w.at[a, t, :, 1 - h.core], self.recv.at[self.first + a, t, 5])
                if own:
                    self.own_copy(a, t).wait()
                x, y, c, right, left = self.firsts(a, t, own)
                self.along(own, from_left, lambda: right().wait_send(), lambda: left().wait_send())
                for copy in (x(), y(), c(), *self.halves(a, t)):
                    copy.wait_send()
                for yx, kind in ((h.yx_x, 5), (h.yx_y, 6), (h.yx_d, 7)):
                    self.to_core(a, t, yx, kind).wait_send()

            self.each(s, body)


class Scatter:
    def __init__(self, here, own, rc, rda, rdb, rx, ry, rz, first, send, recv):
        self.here, self.own, self.first, self.count = here, own, first, own.shape[0]
        self.rc, self.rda, self.rdb, self.rx, self.ry, self.rz = rc, rda, rdb, rx, ry, rz
        self.send, self.recv = send, recv
        z = here.z
        self.order = [3 * (1 - z // 2), (2 + 3 * z) % 5, 1 + z % 2, z]

    def copies(self, a, t):
        h, own, f = self.here, self.own, self.first + a
        half = own.shape[4] // 2
        d = own.at[a, t, h.yx_d, h.core]
        mine = own.at[a, t, h.yx, h.core]
        sem = lambda k: (self.send.at[f, t, k], self.recv.at[f, t, k])
        return (
            lambda: remote(own.at[a, t, :, 1 - h.core], self.rc.at[a, t], *sem(0), h.dev_c, h.z),
            lambda: remote(d.at[pl.ds(0, half)], self.rda.at[a, t], *sem(1), h.dev_x, h.z),
            lambda: remote(d.at[pl.ds(half, half)], self.rdb.at[a, t], *sem(2), h.dev_y, h.z),
            lambda: remote(own.at[a, t, h.yx_x, h.core], self.rx.at[a, t], *sem(3), h.dev_x, h.z),
            lambda: remote(own.at[a, t, h.yx_y, h.core], self.ry.at[a, t], *sem(4), h.dev_y, h.z),
            lambda: remote(mine, self.rz.at[0, a, t], *sem(5), h.dp, (h.z + 1) % h.nz),
            lambda: remote(mine, self.rz.at[1, a, t], *sem(6), h.dp, (h.z + h.nz - 1) % h.nz),
        )

    def each(self, k, body):
        t = self.order[k]

        def run(a, carry):
            body(a, t, self.copies(a, t))
            return carry

        lax.fori_loop(0, self.count, run, 0)

    def got(self, ref, a, t, kind):
        landed(ref, self.recv.at[self.first + a, t, kind])

    def add(self, dst, src):
        dst[...] = (dst[...].astype(F32) + src[...].astype(F32)).astype(BF)

    def stage1(self, k):
        self.each(k, lambda a, t, copies: copies[0]().start())

    def stage2(self, k):
        h = self.here

        def body(a, t, copies):
            self.got(self.rc.at[a, t], a, t, 0)
            for q in range(4):
                self.add(self.own.at[a, t, q, h.core], self.rc.at[a, t, q])
            copies[1]().start()
            copies[2]().start()

        self.each(k, body)

    def stage3(self, k):
        h = self.here
        half = self.own.shape[4] // 2

        def body(a, t, copies):
            self.got(self.rda.at[a, t], a, t, 1)
            self.add(self.own.at[a, t, h.yx_y, h.core, pl.ds(0, half)], self.rda.at[a, t])
            copies[4]().start()
            self.got(self.rdb.at[a, t], a, t, 2)
            self.add(self.own.at[a, t, h.yx_x, h.core, pl.ds(half, half)], self.rdb.at[a, t])
            copies[3]().start()

        self.each(k, body)

    def stage4(self, k):
        h = self.here

        def body(a, t, copies):
            mine = self.own.at[a, t, h.yx, h.core]
            self.got(self.rx.at[a, t], a, t, 3)
            self.got(self.ry.at[a, t], a, t, 4)
            mine[...] = (
                mine[...].astype(F32) + self.rx[a, t].astype(F32) + self.ry[a, t].astype(F32)
            ).astype(BF)

        self.each(k, body)

    def stage5(self, k):
        h = self.here

        def body(a, t, copies):
            mine = self.own.at[a, t, h.yx, h.core]

            @pl.when(t > h.z)
            def _():
                @pl.when(h.z > 0)
                def _():
                    self.got(self.rz.at[0, a, t], a, t, 5)
                    self.add(mine, self.rz.at[0, a, t])

                copies[5]().start()

            @pl.when(t < h.z)
            def _():
                @pl.when(h.z < h.nz - 1)
                def _():
                    self.got(self.rz.at[1, a, t], a, t, 6)
                    self.add(mine, self.rz.at[1, a, t])

                copies[6]().start()

        self.each(k, body)

    def finish(self, out_ref):
        h = self.here

        def run(a, carry):
            f, z = self.first + a, h.z
            out_ref[f] = self.own[a, z, h.yx, h.core].astype(F32)

            @pl.when(z > 0)
            def _():
                self.got(self.rz.at[0, a, z], a, z, 5)
                out_ref[f] += self.rz[0, a, z].astype(F32)

            @pl.when(z < h.nz - 1)
            def _():
                self.got(self.rz.at[1, a, z], a, z, 6)
                out_ref[f] += self.rz[1, a, z].astype(F32)

            return carry

        lax.fori_loop(0, self.count, run, 0)

    def drain(self):
        h = self.here

        def body(a, t, copies):
            for copy in copies[:5]:
                copy().wait_send()
            pl.when(t > h.z)(lambda: copies[5]().wait_send())
            pl.when(t < h.z)(lambda: copies[6]().wait_send())

        for k in range(h.nz):
            self.each(k, body)


def scatter_scratch(na, nz, nd, rw, wide):
    return [
        pltpu.VMEM((na, nz, nd // 2, 2, rw, wide), BF),
        pltpu.VMEM((na, nz, nd // 2, rw, wide), BF),
        pltpu.VMEM((na, nz, rw // 2, wide), BF),
        pltpu.VMEM((na, nz, rw // 2, wide), BF),
        pltpu.VMEM((na, nz, rw, wide), BF),
        pltpu.VMEM((na, nz, rw, wide), BF),
        pltpu.VMEM((2, na, nz, rw, wide), BF),
    ]


def every_pair(pairs, work, between):
    def step(p, carry):
        work(p)
        for at, steps in enumerate(between):

            @pl.when(p == at)
            def _():
                for run in steps:
                    run()

        return carry

    lax.fori_loop(0, pairs, step, 0)


def columns(p, start=0):
    return pl.ds(pl.multiple_of(start + p * LANES, LANES), LANES)


def assemble(mix, nz, wqkv_ref, wo_ref):
    d = wo_ref.shape[0]
    wl = d // nz
    for j in range(4):
        whole = jnp.concatenate([mix(t)[:, j * wl : (j + 1) * wl] for t in range(nz)], axis=1)
        if j < 3:
            wqkv_ref[:, j * d : (j + 1) * d] = whole
        else:
            wo_ref[...] = whole


def first_kernel(
    comm, tok_ref, cot_ref, sh_ref, bias_ref, segc_ref,
    x_out, cot_out, wud_out, qkv_out, wqkv_out, xt_out, wo_ref, att_ref, lse_ref,
    mix_s, x_s, qkv_s, wqkv_s, xt_s, kx_s, qx_s, vt_s, out_sem, *sems,
):
    nz = mix_s.shape[1]
    length, d = att_ref.shape
    pairs = d // LANES
    blk = length // nz
    if comm:
        send, recv, local, tsend, trecv, csend, crecv = sems
        here = Here(nz)
        here.greet()
        mix = Gather(here, mix_s, sh_ref, 0, 1, send, recv, local)
        rest = Gather(here, wud_out, sh_ref, 1, 2, send, recv, local)
        tokens = Exchange(here, tok_ref, x_s, tsend, trecv)
        cots = Exchange(here, cot_ref, cot_out, csend, crecv)
        mix.stage1(0)
        tokens.start()
        doc_lanes(segc_ref, kx_s, qx_s)
        vt_s[:, HD:, :] = jnp.ones((2, vt_s.shape[1] - HD, length), BF)
        mix.stage1(1)
        mix.stage2(0)
        mix.stage1(2)
        mix.stage2(1)
        mix.stage3(0)
        rest.stage1(0)
        mix.stage1(3)
        mix.stage2(2)
        mix.stage3(1)
        mix.stage2(3)
        mix.stage3(2)
        mix.stage3(3)
        tokens.wait_recv()
        cots.start()
        rest.stage1(1)
        mix.drain()
        between = [
            [lambda: rest.stage2(0), lambda: rest.stage1(2)],
            [lambda: rest.stage3(0), lambda: rest.stage2(1), lambda: rest.stage1(3)],
            [lambda: rest.stage3(1), lambda: rest.stage2(2)],
            [lambda: rest.stage3(2), lambda: rest.stage2(3)],
            [lambda: rest.stage3(3)],
            [],
        ]
    out_x = pltpu.make_async_copy(x_s, x_out, out_sem.at[0])
    out_qkv = pltpu.make_async_copy(qkv_s, qkv_out, out_sem.at[1])
    out_w = pltpu.make_async_copy(wqkv_s, wqkv_out, out_sem.at[2])
    out_xt = pltpu.make_async_copy(xt_s, xt_out, out_sem.at[3])
    out_x.start()
    assemble(lambda t: mix_s[0, t].reshape(d, -1), nz, wqkv_s, wo_ref)
    out_w.start()

    def body(i, carry):
        at = pl.ds(pl.multiple_of(i * blk, blk), blk)
        qkv_s[at, :] = (dot_nn(x_s[i], wqkv_s[...]) + bias_ref[...]).astype(BF)
        return carry

    lax.fori_loop(0, nz, body, 0)
    out_qkv.start()
    for i in range(nz):
        xt_s[:, i * blk : (i + 1) * blk] = jnp.transpose(x_s[i])
    out_xt.start()

    def work(p):
        o, lse = attend_pair(
            qkv_s[:, columns(p)], qkv_s[:, columns(p, d)], qkv_s[:, columns(p, 2 * d)], kx_s, qx_s, vt_s
        )
        att_ref[:, columns(p)] = o
        lse_ref[p] = lse

    every_pair(pairs, work, between)
    rest.drain()
    tokens.wait_send()
    cots.wait_recv()
    cots.wait_send()
    for copy in (out_x, out_qkv, out_w, out_xt):
        copy.wait()


def first(tokens, cot, shards, bias, segc):
    nz, nd = lax.axis_size("tensor"), lax.axis_size("dp")
    na, rw, wide = shards.shape
    _, blk, d = tokens.shape
    length = segc.shape[0]
    pairs = d // LANES
    any_ = pl.BlockSpec(memory_space=pl.ANY)
    vmem = pl.BlockSpec(memory_space=pltpu.VMEM)
    dma = pltpu.SemaphoreType.DMA
    s = jax.ShapeDtypeStruct
    unit = (nz, nd // 2, 2, rw, wide)
    return pl.pallas_call(
        functools.partial(first_kernel, True),
        out_shape=(
            s(tokens.shape, BF),
            s(tokens.shape, BF),
            s((na - 1,) + unit, BF),
            s((length, 3 * d), BF),
            s((d, 3 * d), BF),
            s((d, length), BF),
            s((d, d), BF),
            s((length, d), BF),
            s((pairs, 2, length), F32),
        ),
        in_specs=[any_, any_, any_, vmem, vmem],
        out_specs=(any_,) * 6 + (vmem,) * 3,
        scratch_shapes=[
            pltpu.VMEM((1,) + unit, BF),
            pltpu.VMEM((nz, blk, d), BF),
            pltpu.VMEM((length, 3 * d), BF),
            pltpu.VMEM((d, 3 * d), BF),
            pltpu.VMEM((d, length), BF),
            pltpu.VMEM((length, 2 * LANES), BF),
            pltpu.VMEM((length, 2 * LANES), BF),
            pltpu.VMEM((2, HD + 16, length), BF),
            dma((4,)),
            dma((na, nz, 10)),
            dma((na, nz, 6)),
            dma((na,)),
            dma((nz,)),
            dma((nz,)),
            dma((nz,)),
            dma((nz,)),
        ],
        compiler_params=pltpu.CompilerParams(
            collective_id=0, has_side_effects=True, vmem_limit_bytes=VMEM_LIMIT
        ),
        name="first",
    )(tokens, cot, shards, bias, segc)


def last_kernel(
    layer_ref, gup_ref, gdn_ref, gwo_ref, ghpre_ref, qkv_ref, att_ref, gatt_ref, wqkv_ref, xt_ref,
    lse_ref, segc_ref, vec_ref,
    lrows_ref, grows_ref, out_ref, vsum_ref,
    pair_s, g_s, w_s, xt_s, hpre_s, gwo_s, gx_s, kx_s, qx_s, kt_s, delta_s, dk_s, dv_s, vbuf,
    u0, u1, u2, u3, u4, u5, u6, m0, m1, m2, m3, m4, m5, m6,
    psem, hsem, load, uload, send, recv, lsend, lrecv, xsend, xrecv, vsend, vrecv,
):
    nz = u0.shape[1]
    length, d = g_s.shape[1:]
    pairs = d // LANES
    blk = length // nz
    wl = d // nz
    here = Here(nz)
    z = here.z
    ud = Scatter(here, u0, u1, u2, u3, u4, u5, u6, 1, send, recv)
    mx = Scatter(here, m0, m1, m2, m3, m4, m5, m6, 0, send, recv)
    layer = Exchange(here, layer_ref, lrows_ref, lsend, lrecv)
    rows = Exchange(here, gx_s, grows_ref, xsend, xrecv)

    def pair_loads(p, slot):
        srcs = (
            qkv_ref.at[:, columns(p)], qkv_ref.at[:, columns(p, d)], qkv_ref.at[:, columns(p, 2 * d)],
            att_ref.at[:, columns(p)], gatt_ref.at[:, columns(p)],
        )
        return [
            pltpu.make_async_copy(src, pair_s.at[slot, j], psem.at[slot, j])
            for j, src in enumerate(srcs)
        ]

    def ud_loads(k):
        t = ud.order[k]
        return [
            pltpu.make_async_copy(g.at[t], u0.at[a, t], uload.at[a, t])
            for a, g in enumerate((gup_ref, gdn_ref))
        ]

    later = [
        pltpu.make_async_copy(src, dst, load.at[i])
        for i, (src, dst) in enumerate(((wqkv_ref, w_s), (xt_ref, xt_s), (gwo_ref, gwo_s)))
    ]

    def hpre_load(i, slot):
        return pltpu.make_async_copy(ghpre_ref.at[i], hpre_s.at[slot], hsem.at[slot])

    for copy in pair_loads(0, 0):
        copy.start()
    for k in range(nz):
        for copy in ud_loads(k):
            copy.start()
    here.greet()
    layer.start()
    doc_lanes(segc_ref, kx_s, qx_s)

    def work(p):
        slot = p % 2

        @pl.when(p + 1 < pairs)
        def _():
            for copy in pair_loads(p + 1, 1 - slot):
                copy.start()

        for copy in pair_loads(p, slot):
            copy.wait()
        q, k, v, att, g = [pair_s.at[slot, j] for j in range(5)]

        def put_q(at, value):
            g_s[0, at, columns(p)] = value

        attend_pair_back(q, k, v, att, g, lse_ref[p], kx_s, qx_s, kt_s, delta_s, dk_s, dv_s, put_q)
        g_s[1, :, columns(p)] = dk_s[...].astype(BF)
        g_s[2, :, columns(p)] = dv_s[...].astype(BF)

    def cores():
        for k in range(nz):
            for copy in ud_loads(k):
                copy.wait()
            ud.stage1(k)

    def start_later():
        for copy in later:
            copy.start()

    def run(*names):
        return [lambda name=name, k=k: getattr(ud, name)(k) for name, k in names]

    between = [
        [cores],
        run(("stage2", 0), ("stage2", 1)),
        run(("stage3", 0), ("stage2", 2), ("stage3", 1), ("stage2", 3)),
        run(("stage4", 0), ("stage5", 0), ("stage3", 2)) + [start_later],
        run(("stage3", 3), ("stage4", 1), ("stage5", 1)),
        run(("stage4", 2), ("stage5", 2), ("stage4", 3)),
    ]
    every_pair(pairs, work, between)

    place_of = [(z + k) % nz for k in (1, 2, 3, 0)]
    hpre_load(place_of[0], 0).start()
    for copy in later:
        copy.wait()
    for i, to in enumerate(place_of):
        if i + 1 < nz:
            hpre_load(place_of[i + 1], (i + 1) % 2).start()
        hpre_load(to, i % 2).wait()
        at = pl.ds(pl.multiple_of(to * blk, blk), blk)
        total = hpre_s[i % 2]
        for j in range(3):
            total = total + dot_nt(g_s[j, at, :], w_s[:, j * d : (j + 1) * d])
        gx_s[to] = total.astype(BF)
        if i + 1 < nz:
            rows.copy(i + 1).start()
        else:
            rows.own().start()

    vsum_ref[...] = vec_ref[...]
    xt = xt_s[...]
    for j in range(3):
        grad = dot_nn(xt, g_s[j]).astype(BF)
        for t in range(nz):
            part = grad[:, t * wl : (t + 1) * wl]
            m0[0, t, :, :, :, j * wl : (j + 1) * wl] = part.reshape(m0.shape[2:5] + (wl,))
        if j != 1:
            sums = jnp.sum(g_s[j].astype(F32), axis=0, keepdims=True)
            r = vec_ref.shape[0] - 2 + j // 2
            vsum_ref[r : r + 1, :] = sums
    for t in range(nz):
        part = gwo_s[:, t * wl : (t + 1) * wl]
        m0[0, t, :, :, :, 3 * wl :] = part.reshape(m0.shape[2:5] + (wl,))

    partners = [(here.dev_c, z), (here.dev_x, z), (here.dev_y, z)]
    partners += [(here.dp, z + 1 - 2 * (z % 2)), (here.dp, (z + 2) % nz)]

    def vec_copy(k):
        return remote(vbuf.at[0, k], vbuf.at[1, k], vsend.at[k], vrecv.at[k], *partners[k])

    def vec_start(k):
        vbuf[0, k] = vsum_ref[...]
        vec_copy(k).start()

    def vec_finish(k):
        landed(vbuf.at[1, k], vrecv.at[k])
        vsum_ref[...] += vbuf[1, k]

    for k in range(nz):
        mx.stage1(k)
    vec_start(0)
    for k in range(nz + 3):
        if k < nz:
            mx.stage2(k)
        if 1 <= k <= nz:
            mx.stage3(k - 1)
        if k < len(partners):
            vec_finish(k)
            if k + 1 < len(partners):
                vec_start(k + 1)
        if 2 <= k <= nz + 1:
            mx.stage4(k - 2)
        if 3 <= k <= nz + 1:
            mx.stage5(k - 3)
    ud.finish(out_ref)
    mx.finish(out_ref)
    ud.drain()
    mx.drain()
    for k in range(len(partners)):
        vec_copy(k).wait_send()
    layer.wait_recv()
    layer.wait_send()
    rows.wait_recv()
    rows.wait_send()


def last(layer, gup, gdn, gwo, ghpre, qkv, att, gatt, wqkv, xt, lse, segc, vec):
    nz, nd = lax.axis_size("tensor"), lax.axis_size("dp")
    length, d = att.shape
    rw, wide = d // nd, gup.shape[2]
    blk = length // nz
    unit = (nz, nd // 2, 2, rw, wide)
    any_ = pl.BlockSpec(memory_space=pl.ANY)
    vmem = pl.BlockSpec(memory_space=pltpu.VMEM)
    dma = pltpu.SemaphoreType.DMA
    s = jax.ShapeDtypeStruct
    steps = 5
    return pl.pallas_call(
        last_kernel,
        out_shape=(
            s((nz, blk, d), BF),
            s((nz, blk, d), BF),
            s((3, rw, wide), F32),
            s(vec.shape, F32),
        ),
        in_specs=[any_] * 10 + [vmem] * 3,
        out_specs=(any_, any_, vmem, vmem),
        scratch_shapes=[
            pltpu.VMEM((2, 5, length, LANES), BF),
            pltpu.VMEM((3, length, d), BF),
            pltpu.VMEM((d, 3 * d), BF),
            pltpu.VMEM((d, length), BF),
            pltpu.VMEM((2, blk, d), F32),
            pltpu.VMEM((d, d), BF),
            pltpu.VMEM((nz, blk, d), BF),
            pltpu.VMEM((length, 2 * LANES), BF),
            pltpu.VMEM((length, 2 * LANES), BF),
            pltpu.VMEM((LANES, length), BF),
            pltpu.VMEM((8, length), F32),
            pltpu.VMEM((length, LANES), F32),
            pltpu.VMEM((length, LANES), F32),
            pltpu.VMEM((2, steps) + vec.shape, F32),
        ]
        + scatter_scratch(2, nz, nd, rw, wide)
        + scatter_scratch(1, nz, nd, rw, wide)
        + [
            dma((2, 5)),
            dma((2,)),
            dma((3,)),
            dma((2, nz)),
            dma((3, nz, 7)),
            dma((3, nz, 7)),
            dma((nz,)),
            dma((nz,)),
            dma((nz,)),
            dma((nz,)),
            dma((steps,)),
            dma((steps,)),
        ],
        compiler_params=pltpu.CompilerParams(
            collective_id=1, has_side_effects=True, vmem_limit_bytes=LAST_LIMIT
        ),
        name="last",
    )(
        layer.reshape(nz, blk, d), gup.reshape(unit), gdn.reshape(unit), gwo,
        ghpre.reshape(nz, blk, d), qkv, att, gatt, wqkv, xt, lse, segc, vec,
    )


LAST_LIMIT = 61 * 1024 * 1024


def plain_attend_kernel(q_ref, k_ref, v_ref, segc_ref, o_ref, lse_ref, kx_s, qx_s, vt_s):
    doc_lanes(segc_ref, kx_s, qx_s)
    vt_s[:, HD:, :] = jnp.ones((2, vt_s.shape[1] - HD, vt_s.shape[2]), BF)
    o_ref[...], lse_ref[...] = attend_pair(q_ref[...], k_ref[...], v_ref[...], kx_s, qx_s, vt_s)


def plain_attend_back_kernel(
    q_ref, k_ref, v_ref, att_ref, g_ref, lse_ref, segc_ref, gq_ref, gk_ref, gv_ref,
    kx_s, qx_s, kt_s, delta_s, dk_s, dv_s,
):
    doc_lanes(segc_ref, kx_s, qx_s)

    def put_q(at, value):
        gq_ref[at, :] = value

    attend_pair_back(
        q_ref, k_ref, v_ref, att_ref, g_ref, lse_ref[...], kx_s, qx_s, kt_s, delta_s, dk_s, dv_s, put_q
    )
    gk_ref[...] = dk_s[...].astype(BF)
    gv_ref[...] = dv_s[...].astype(BF)


def plain_specs(length, d):
    col = lambda off: pl.BlockSpec((length, LANES), lambda p: (0, off + p))
    seg = pl.BlockSpec((length, LANES), lambda p: (0, 0))
    lse = pl.BlockSpec((None, 2, length), lambda p: (p, 0, 0))
    wide = pltpu.VMEM((length, 2 * LANES), BF)
    return d // LANES, col, seg, lse, wide


def plain_first(tokens, cot, shards, bias, segc):
    axes = ("tensor", "dp")
    nz = lax.axis_size("tensor")
    length, d = segc.shape[0], tokens.shape[2]
    pairs, col, seg, lse_spec, wide = plain_specs(length, d)
    x = lax.all_to_all(tokens, "tensor", 0, 0)
    cot = lax.all_to_all(cot, "tensor", 0, 0)
    w = lax.all_gather(shards, axes, axis=1, tiled=True).reshape(3, nz, d, shards.shape[2])
    parts = w[0].reshape(nz, d, 4, d // nz).transpose(1, 2, 0, 3).reshape(d, 4 * d)
    wqkv, wo = parts[:, : 3 * d], parts[:, 3 * d :]
    rows = x.reshape(length, d)
    qkv = (dot_nn(rows, wqkv) + bias).astype(BF)
    att, lse = pl.pallas_call(
        plain_attend_kernel,
        grid=(pairs,),
        out_shape=(
            jax.ShapeDtypeStruct((length, d), BF),
            jax.ShapeDtypeStruct((pairs, 2, length), F32),
        ),
        in_specs=[col(0), col(pairs), col(2 * pairs), seg],
        out_specs=(col(0), lse_spec),
        scratch_shapes=[wide, wide, pltpu.VMEM((2, HD + 16, length), BF)],
        compiler_params=pltpu.CompilerParams(vmem_limit_bytes=VMEM_LIMIT),
        name="plain_attend",
    )(qkv, qkv, qkv, segc)
    return x, cot, w[1:], qkv, wqkv, rows.T, wo, att, lse


def plain_last(layer, gup, gdn, gwo, ghpre, qkv, att, gatt, wqkv, xt, lse, segc, vec):
    axes = ("tensor", "dp")
    nz = lax.axis_size("tensor")
    length, d = att.shape
    pairs, col, seg, lse_spec, wide = plain_specs(length, d)
    f32_wide = pltpu.VMEM((length, LANES), F32)
    grads = pl.pallas_call(
        plain_attend_back_kernel,
        grid=(pairs,),
        out_shape=[jax.ShapeDtypeStruct((length, d), BF)] * 3,
        in_specs=[col(0), col(pairs), col(2 * pairs), col(0), col(0), lse_spec, seg],
        out_specs=[col(0)] * 3,
        scratch_shapes=[
            wide, wide, pltpu.VMEM((LANES, length), BF), pltpu.VMEM((8, length), F32), f32_wide, f32_wide,
        ],
        compiler_params=pltpu.CompilerParams(vmem_limit_bytes=VMEM_LIMIT),
        name="plain_attend_back",
    )(qkv, qkv, qkv, att, gatt, lse, segc)
    g = jnp.concatenate(grads, axis=1)
    gx = (ghpre + dot_nt(g, wqkv)).astype(BF)
    gmix = jnp.concatenate((dot_nn(xt, g).astype(BF), gwo), axis=1)
    gmix = gmix.reshape(d, 4, nz, d // nz).transpose(2, 0, 1, 3).reshape(nz, d, -1)
    split = lambda a: a.reshape(nz, length // nz, d)
    parts = [
        lax.psum_scatter(p.reshape(nz * d, -1), axes, scatter_dimension=0, tiled=True)
        for p in (gmix, gup, gdn)
    ]
    sums = [jnp.sum(grads[j].astype(F32), axis=0, keepdims=True) for j in (0, 2)]
    vec = jnp.concatenate((vec[:-2], *sums), axis=0)
    return (
        lax.all_to_all(split(layer), "tensor", 0, 0),
        lax.all_to_all(split(gx), "tensor", 0, 0),
        jnp.stack(parts).astype(F32),
        lax.psum(vec, axes),
    )


def on_device(
    tokens, segment_ids, drop_flags, qkv_w, qv_b, wo_w, wo_b, gain1, shift1,
    up_w, up_b, dn_w, dn_b, gain2, shift2, cotangent,
):
    me = lax.axis_index("tensor")
    nt, nd = lax.axis_size("tensor"), lax.axis_size("dp")
    d = tokens.shape[2]
    length = segment_ids.shape[1]
    wl = qkv_w.shape[2]
    fl = up_w.shape[1]
    begin, end = (first, last) if (nt, nd) == (4, 8) else (plain_first, plain_last)

    mix = jnp.concatenate((qkv_w[0], qkv_w[1], qkv_w[2], wo_w.T), axis=1)
    shards = jnp.stack((mix, up_w, dn_w.T))
    seg = lax.dynamic_index_in_dim(segment_ids, me, 0, keepdims=False)
    drop = lax.dynamic_slice_in_dim(drop_flags, me, 1)
    segc = jnp.broadcast_to(seg[:, None], (length, LANES))
    bias = jnp.concatenate((qv_b[0], jnp.zeros((d,), F32), qv_b[1]))
    zero_row = jnp.zeros((d,), F32)
    vec = jnp.stack((wo_b, gain1, shift1, dn_b, gain2, shift2, zero_row, zero_row))

    x, cot, wud, qkv, wqkv, xt, wo, att, lse = begin(tokens, cotangent, shards, bias[None], segc)
    layer, g_att, g_hpre, gup, gdn, gwo, vecg, bing = middle(
        drop, att, x.reshape(length, d), cot.reshape(length, d), wo, wud.reshape(2, nt, d, fl), vec,
        up_b.reshape(nt, fl),
    )
    flat = jnp.concatenate((vecg[:6], bing.reshape(-1, d), jnp.zeros((6, d), F32)), axis=0)
    layer_out, rows, grads, total = end(
        layer, gup, gdn, gwo, g_hpre, qkv, att, g_att, wqkv, xt, lse, segc, flat
    )
    g_mix, g_up, g_dn = grads[0], grads[1], grads[2]
    n_bin = nt * fl // d
    return (
        layer_out,
        rows.astype(F32),
        jnp.stack([g_mix[:, j * wl : (j + 1) * wl] for j in range(3)]),
        total[-2:],
        g_mix[:, 3 * wl :].T,
        total[0],
        total[1],
        total[2],
        g_up,
        total[6 : 6 + n_bin].reshape(-1),
        g_dn.T,
        total[3],
        total[4],
        total[5],
    )


def solution(mesh):
    rows = P("dp", "tensor", None)
    return jax.shard_map(
        on_device,
        mesh=mesh,
        in_specs=(
            rows, P("dp", None), P("dp"), P(None, "dp", "tensor"), P(), P("tensor", "dp"), P(), P(), P(),
            P("dp", "tensor"), P(), P("tensor", "dp"), P(), P(), P(), rows,
        ),
        out_specs=(
            rows, rows, P(None, "dp", "tensor"), P(), P("tensor", "dp"), P(), P(), P(),
            P("dp", "tensor"), P(), P("tensor", "dp"), P(), P(), P(),
        ),
        check_vma=False,
    )
```

```python
import functools
import jax
import jax.numpy as jnp
from jax import lax
from jax.experimental import pallas as pl
from jax.experimental.pallas import tpu as pltpu
from jax.sharding import PartitionSpec as P

HD = 64
EPS = 1e-05
NEG = -1000000000.0
BF = jnp.bfloat16
F32 = jnp.float32
VMEM_LIMIT = 60 * 1024 * 1024
BLK = 256
LANES = 128


def dot_nn(a, b):
    return jnp.dot(a, b, preferred_element_type=F32)


def dot_nt(a, b):
    return lax.dot_general(a, b, (((1,), (1,)), ((), ())), preferred_element_type=F32)


def dot_tn(a, b):
    return lax.dot_general(a, b, (((0,), (0,)), ((), ())), preferred_element_type=F32)


def doc_lanes(seg, kx_s, qx_s):
    lane = lax.broadcasted_iota(jnp.int32, seg.shape, 1)
    same = (seg == lane).astype(F32)
    kx_s[:, LANES:] = same.astype(BF)
    qx_s[:, LANES:] = ((1.0 - same) * NEG).astype(BF)


def split_heads(pair):
    first = lax.broadcasted_iota(jnp.int32, pair.shape, 1) % (2 * HD) < HD
    zero = jnp.zeros((), pair.dtype)
    return jnp.where(first, pair, zero), jnp.where(first, zero, pair)


def attend_pair(q, k, v, kx_s, qx_s, vt_s):
    kx_s[:, :LANES] = k
    qx_s[:, :LANES] = (q.astype(F32) * 0.125).astype(BF)
    vt = jnp.transpose(v)
    vt_s[0, :HD, :] = vt[:HD, :]
    vt_s[1, :HD, :] = vt[HD:, :]
    kx = kx_s[...]
    ext = qx_s[:, LANES:]
    outs, lses = [], []
    scores = [
        dot_nt(kx, jnp.concatenate((h, ext), axis=1)) for h in split_heads(qx_s[:, :LANES])
    ]
    for h in range(2):
        top = jnp.max(scores[h], axis=0, keepdims=True)
        p = jnp.exp(scores[h] - top).astype(BF)
        o = dot_nn(vt_s[h], p)
        total = o[HD : HD + 1, :]
        outs.append(o[:HD, :] / total)
        lses.append(top + jnp.log(total))
    return jnp.transpose(jnp.concatenate(outs, axis=0)).astype(BF), jnp.concatenate(lses, axis=0)


def attend_pair_back(q_ref, k_ref, v_ref, att_ref, g_ref, lse, kx_s, qx_s, kt_s, delta_s, dk_s, dv_s, put_q):
    length = q_ref.shape[0]
    kx_s[:, :LANES] = k_ref[...]
    qx_s[:, :LANES] = (q_ref[...].astype(F32) * 0.125).astype(BF)
    kt_s[...] = jnp.transpose(k_ref[...])
    sub = lax.broadcasted_iota(jnp.int32, (8, LANES), 0)
    lane = lax.broadcasted_iota(jnp.int32, (8, LANES), 1)
    pick = jnp.where(lane // HD == sub, 1.0, 0.0).astype(F32)
    prod = g_ref[...].astype(F32) * att_ref[...].astype(F32)
    delta_s[...] = lax.dot_general(
        pick, prod, (((1,), (1,)), ((), ())),
        preferred_element_type=F32, precision=lax.Precision.HIGHEST,
    )
    for i in range(length // QB):
        at = slice(i * QB, (i + 1) * QB)
        kx = kx_s[...]
        v = v_ref[...]
        ext = qx_s[at, LANES:]
        qs = split_heads(qx_s[at, :LANES])
        gs = split_heads(g_ref[at, :])
        ps, ds, dq = [], [], []
        for h in range(2):
            s = dot_nt(kx, jnp.concatenate((qs[h], ext), axis=1))
            p = jnp.exp(s - lse[h : h + 1, at])
            dp = dot_nt(v, gs[h])
            d = (p * (dp - delta_s[h : h + 1, at])).astype(BF)
            ps.append(p.astype(BF))
            ds.append(d)
            dq.append(dot_nn(kt_s[h * HD : (h + 1) * HD, :], d))
        dv = dot_nn(jnp.concatenate(ps, axis=1), jnp.concatenate(gs, axis=0))
        dk = dot_nn(jnp.concatenate(ds, axis=1), jnp.concatenate(qs, axis=0))
        dv_s[...] = dv if i == 0 else dv_s[...] + dv
        dk_s[...] = dk if i == 0 else dk_s[...] + dk
        put_q(at, (jnp.transpose(jnp.concatenate(dq, axis=0)) * 0.125).astype(BF))


QB = 512


def place(dp):
    yx, core = dp // 2, dp % 2
    y, x = yx // 2, yx % 2
    return yx, core, y * 2 + 1 - x, (1 - y) * 2 + x, 3 - yx


def remote(src, dst, send, recv, dp, z):
    return pltpu.make_async_remote_copy(
        src_ref=src,
        dst_ref=dst,
        send_sem=send,
        recv_sem=recv,
        device_id=(dp, z),
        device_id_type=pl.DeviceIdType.MESH,
    )


def greet(dp, z, yx, core, yx_x, yx_y, nz):
    barrier = pltpu.get_barrier_semaphore()
    others = [(yx_x * 2 + core, z), (yx_y * 2 + core, z), (yx * 2 + 1 - core, z)]
    others += [(dp, (z + k) % nz) for k in range(1, nz)]
    for dev in others:
        pl.semaphore_signal(
            barrier, inc=1, device_id=dev, device_id_type=pl.DeviceIdType.MESH
        )
    pl.semaphore_wait(barrier, len(others))


def landed(ref, sem):
    pltpu.make_async_copy(ref, ref, sem).wait()


class Here:
    def __init__(self, nz):
        self.nz = nz
        self.dp, self.z = lax.axis_index("dp"), lax.axis_index("tensor")
        self.yx, self.core, self.yx_x, self.yx_y, self.yx_d = place(self.dp)
        self.dev_x = self.yx_x * 2 + self.core
        self.dev_y = self.yx_y * 2 + self.core
        self.dev_c = self.yx * 2 + 1 - self.core

    def greet(self):
        greet(self.dp, self.z, self.yx, self.core, self.yx_x, self.yx_y, self.nz)

    def sides(self, s, body):
        if s == 0:
            body(self.z, None)
            return

        @pl.when(self.z >= s)
        def _():
            body(self.z - s, True)

        @pl.when(self.z + s < self.nz)
        def _():
            body(self.z + s, False)


def flip(z, i):
    return (z % 2 + i % 2) % 2 + 2 * ((z // 2 + i // 2) % 2)


class Exchange:
    def __init__(self, here, src, dst, send, recv, ks=(1, 2, 3)):
        self.here, self.src, self.dst, self.send, self.recv, self.ks = here, src, dst, send, recv, ks

    def copy(self, k):
        h = self.here
        to = flip(h.z, k)
        return remote(
            self.src.at[to], self.dst.at[h.z], self.send.at[k], self.recv.at[k], h.dp, to
        )

    def own(self):
        z = self.here.z
        return pltpu.make_async_copy(self.src.at[z], self.dst.at[z], self.send.at[0])

    def start(self):
        for k in self.ks:
            self.copy(k).start()
        self.own().start()

    def got(self, k):
        landed(self.dst.at[flip(self.here.z, k)], self.recv.at[k])

    def wait_recv(self):
        self.own().wait()
        for k in self.ks:
            self.got(k)

    def wait_send(self):
        for k in self.ks:
            self.copy(k).wait_send()


class Gather:
    def __init__(self, here, w_ref, sh_ref, first, count, send, recv, local):
        self.here, self.w, self.sh, self.first, self.count = here, w_ref, sh_ref, first, count
        self.send, self.recv, self.local = send, recv, local

    def blk(self, a, t, yx):
        return self.w.at[a, t, yx, self.here.core]

    def copy(self, src, dst, a, t, sender, receiver, dp, z):
        f = self.first + a
        return remote(src, dst, self.send.at[f, t, sender], self.recv.at[f, t, receiver], dp, z)

    def firsts(self, a, t, own):
        h = self.here
        dst = self.blk(a, t, h.yx)
        src = self.sh.at[self.first + a] if own else dst
        return (
            lambda: self.copy(src, dst, a, t, 0, 0, h.dev_x, h.z),
            lambda: self.copy(src, dst, a, t, 1, 1, h.dev_y, h.z),
            lambda: self.copy(src, dst, a, t, 2, 5, h.dev_c, h.z),
            lambda: self.copy(src, dst, a, t, 8, 4, h.dp, (h.z + 1) % h.nz),
            lambda: self.copy(src, dst, a, t, 9, 4, h.dp, (h.z + h.nz - 1) % h.nz),
        )

    def own_copy(self, a, t):
        return pltpu.make_async_copy(
            self.sh.at[self.first + a], self.blk(a, t, self.here.yx), self.local.at[self.first + a]
        )

    def halves(self, a, t):
        h = self.here
        half = self.w.shape[4] // 2
        to_y = self.blk(a, t, h.yx_x).at[pl.ds(0, half)]
        to_x = self.blk(a, t, h.yx_y).at[pl.ds(half, half)]
        return (
            self.copy(to_y, to_y, a, t, 3, 2, h.dev_y, h.z),
            self.copy(to_x, to_x, a, t, 4, 3, h.dev_x, h.z),
        )

    def to_core(self, a, t, yx, kind):
        b = self.blk(a, t, yx)
        return self.copy(b, b, a, t, kind, 5, self.here.dev_c, self.here.z)

    def each(self, s, body):
        def run(a, carry):
            self.here.sides(s, lambda t, from_left: body(a, t, from_left))
            return carry

        lax.fori_loop(0, self.count, run, 0)

    def along(self, own, from_left, right, left):
        h = self.here
        if own or from_left:
            pl.when(h.z < h.nz - 1)(right)
        if own or not from_left:
            pl.when(h.z > 0)(left)

    def stage1(self, s):
        h, own = self.here, s == 0

        def body(a, t, from_left):
            if own:
                self.own_copy(a, t).start()
            else:
                landed(self.blk(a, t, h.yx), self.recv.at[self.first + a, t, 4])
            x, y, c, right, left = self.firsts(a, t, own)
            self.along(own, from_left, lambda: right().start(), lambda: left().start())
            x().start()
            y().start()
            c().start()

        self.each(s, body)

    def stage2(self, s):
        h = self.here

        def body(a, t, from_left):
            f = self.first + a
            to_y, to_x = self.halves(a, t)
            landed(self.blk(a, t, h.yx_x), self.recv.at[f, t, 0])
            to_y.start()
            self.to_core(a, t, h.yx_x, 5).start()
            landed(self.blk(a, t, h.yx_y), self.recv.at[f, t, 1])
            to_x.start()
            self.to_core(a, t, h.yx_y, 6).start()

        self.each(s, body)

    def stage3(self, s):
        h = self.here
        half = self.w.shape[4] // 2

        def body(a, t, from_left):
            f = self.first + a
            b = self.blk(a, t, h.yx_d)
            landed(b.at[pl.ds(0, half)], self.recv.at[f, t, 2])
            landed(b.at[pl.ds(half, half)], self.recv.at[f, t, 3])
            self.to_core(a, t, h.yx_d, 7).start()

        self.each(s, body)

    def drain(self):
        h = self.here
        for s in range(h.nz):
            own = s == 0

            def body(a, t, from_left):
                landed(self.w.at[a, t, :, 1 - h.core], self.recv.at[self.first + a, t, 5])
                if own:
                    self.own_copy(a, t).wait()
                x, y, c, right, left = self.firsts(a, t, own)
                self.along(own, from_left, lambda: right().wait_send(), lambda: left().wait_send())
                for copy in (x(), y(), c(), *self.halves(a, t)):
                    copy.wait_send()
                for yx, kind in ((h.yx_x, 5), (h.yx_y, 6), (h.yx_d, 7)):
                    self.to_core(a, t, yx, kind).wait_send()

            self.each(s, body)


class Scatter:
    def __init__(self, here, own, rc, rda, rdb, rx, ry, rz, first, send, recv):
        self.here, self.own, self.first, self.count = here, own, first, own.shape[0]
        self.rc, self.rda, self.rdb, self.rx, self.ry, self.rz = rc, rda, rdb, rx, ry, rz
        self.send, self.recv = send, recv
        z = here.z
        self.order = [3 * (1 - z // 2), (2 + 3 * z) % 5, 1 + z % 2, z]

    def copies(self, a, t):
        h, own, f = self.here, self.own, self.first + a
        half = own.shape[4] // 2
        d = own.at[a, t, h.yx_d, h.core]
        mine = own.at[a, t, h.yx, h.core]
        sem = lambda k: (self.send.at[f, t, k], self.recv.at[f, t, k])
        return (
            lambda: remote(own.at[a, t, :, 1 - h.core], self.rc.at[a, t], *sem(0), h.dev_c, h.z),
            lambda: remote(d.at[pl.ds(0, half)], self.rda.at[a, t], *sem(1), h.dev_x, h.z),
            lambda: remote(d.at[pl.ds(half, half)], self.rdb.at[a, t], *sem(2), h.dev_y, h.z),
            lambda: remote(own.at[a, t, h.yx_x, h.core], self.rx.at[a, t], *sem(3), h.dev_x, h.z),
            lambda: remote(own.at[a, t, h.yx_y, h.core], self.ry.at[a, t], *sem(4), h.dev_y, h.z),
            lambda: remote(mine, self.rz.at[0, a, t], *sem(5), h.dp, (h.z + 1) % h.nz),
            lambda: remote(mine, self.rz.at[1, a, t], *sem(6), h.dp, (h.z + h.nz - 1) % h.nz),
        )

    def each(self, k, body):
        t = self.order[k]

        def run(a, carry):
            body(a, t, self.copies(a, t))
            return carry

        lax.fori_loop(0, self.count, run, 0)

    def got(self, ref, a, t, kind):
        landed(ref, self.recv.at[self.first + a, t, kind])

    def add(self, dst, src):
        dst[...] = (dst[...].astype(F32) + src[...].astype(F32)).astype(BF)

    def stage1(self, k):
        self.each(k, lambda a, t, copies: copies[0]().start())

    def stage2(self, k):
        h = self.here

        def body(a, t, copies):
            self.got(self.rc.at[a, t], a, t, 0)
            for q in range(4):
                self.add(self.own.at[a, t, q, h.core], self.rc.at[a, t, q])
            copies[1]().start()
            copies[2]().start()

        self.each(k, body)

    def stage3(self, k):
        h = self.here
        half = self.own.shape[4] // 2

        def body(a, t, copies):
            self.got(self.rda.at[a, t], a, t, 1)
            self.add(self.own.at[a, t, h.yx_y, h.core, pl.ds(0, half)], self.rda.at[a, t])
            copies[4]().start()
            self.got(self.rdb.at[a, t], a, t, 2)
            self.add(self.own.at[a, t, h.yx_x, h.core, pl.ds(half, half)], self.rdb.at[a, t])
            copies[3]().start()

        self.each(k, body)

    def stage4(self, k):
        h = self.here

        def body(a, t, copies):
            mine = self.own.at[a, t, h.yx, h.core]
            self.got(self.rx.at[a, t], a, t, 3)
            self.got(self.ry.at[a, t], a, t, 4)
            mine[...] = (
                mine[...].astype(F32) + self.rx[a, t].astype(F32) + self.ry[a, t].astype(F32)
            ).astype(BF)

        self.each(k, body)

    def stage5(self, k):
        h = self.here

        def body(a, t, copies):
            mine = self.own.at[a, t, h.yx, h.core]

            @pl.when(t > h.z)
            def _():
                @pl.when(h.z > 0)
                def _():
                    self.got(self.rz.at[0, a, t], a, t, 5)
                    self.add(mine, self.rz.at[0, a, t])

                copies[5]().start()

            @pl.when(t < h.z)
            def _():
                @pl.when(h.z < h.nz - 1)
                def _():
                    self.got(self.rz.at[1, a, t], a, t, 6)
                    self.add(mine, self.rz.at[1, a, t])

                copies[6]().start()

        self.each(k, body)

    def finish(self, out_ref):
        h = self.here

        def run(a, carry):
            f, z = self.first + a, h.z
            out_ref[f] = self.own[a, z, h.yx, h.core].astype(F32)

            @pl.when(z > 0)
            def _():
                self.got(self.rz.at[0, a, z], a, z, 5)
                out_ref[f] += self.rz[0, a, z].astype(F32)

            @pl.when(z < h.nz - 1)
            def _():
                self.got(self.rz.at[1, a, z], a, z, 6)
                out_ref[f] += self.rz[1, a, z].astype(F32)

            return carry

        lax.fori_loop(0, self.count, run, 0)

    def drain(self):
        h = self.here

        def body(a, t, copies):
            for copy in copies[:5]:
                copy().wait_send()
            pl.when(t > h.z)(lambda: copies[5]().wait_send())
            pl.when(t < h.z)(lambda: copies[6]().wait_send())

        for k in range(h.nz):
            self.each(k, body)


def scatter_scratch(na, nz, nd, rw, wide):
    return [
        pltpu.VMEM((na, nz, nd // 2, 2, rw, wide), BF),
        pltpu.VMEM((na, nz, nd // 2, rw, wide), BF),
        pltpu.VMEM((na, nz, rw // 2, wide), BF),
        pltpu.VMEM((na, nz, rw // 2, wide), BF),
        pltpu.VMEM((na, nz, rw, wide), BF),
        pltpu.VMEM((na, nz, rw, wide), BF),
        pltpu.VMEM((2, na, nz, rw, wide), BF),
    ]


def every_pair(pairs, work, between):
    def step(p, carry):
        work(p)
        for at, steps in enumerate(between):

            @pl.when(p == at)
            def _():
                for run in steps:
                    run()

        return carry

    lax.fori_loop(0, pairs, step, 0)


def gelu_parts(u):
    cdf = 0.5 + 0.5 * lax.erf(u * 0.7071067811865476)
    return u * cdf, cdf + u * jnp.exp(-0.5 * u * u) * 0.3989422804014327


def norm_rows(v):
    mean = jnp.mean(v, axis=-1, keepdims=True)
    c = v - mean
    inv = lax.rsqrt(jnp.mean(c * c, axis=-1, keepdims=True) + EPS)
    return c * inv, inv


def norm_back(g, normed, inv, gain):
    gn = g * gain
    return inv * (
        gn
        - jnp.mean(gn, axis=-1, keepdims=True)
        - normed * jnp.mean(gn * normed, axis=-1, keepdims=True)
    )


def middle_kernel(comm, row_steps, *refs):
    drop_ref, att_ref, x_ref, cot_ref, crows_ref, wo_ref, up_ref, dn_ref = refs[:8]
    vecs, bin_ref = refs[8:14], refs[14]
    lo_ref, gatt_ref, ghpre_ref, gup_ref, gdn_ref, gwo_ref, vecg_ref, bing_ref = refs[15:23]
    att_s, act_s, gpre_s, slope_s, ht_s, gb2t_s, gbt_s = refs[23:30]
    step = pl.program_id(0)
    parts, _, fl = up_ref.shape
    vec = lambda r: vecs[r][...][None, :]
    if comm:
        cot_s, c3_s, l_s, lsend, lrecv, csend, crecv = refs[30:]
        here = Here(row_steps)
        z = here.z
        layer = Exchange(here, l_s, lo_ref, lsend, lrecv)
        last_cot = lambda: remote(
            crows_ref.at[flip(z, 3)], c3_s, csend.at[0], crecv.at[0], here.dp, flip(z, 3)
        )

    @pl.when(step == 0)
    def _():
        if comm:
            barrier = pltpu.get_barrier_semaphore()
            for k in range(1, row_steps):
                pl.semaphore_signal(
                    barrier, inc=1, device_id=(here.dp, flip(z, k)), device_id_type=pl.DeviceIdType.MESH
                )
            pl.semaphore_wait(barrier, row_steps - 1)
            last_cot().start()
        vecg_ref[...] = jnp.zeros_like(vecg_ref)
        bing_ref[...] = jnp.zeros_like(bing_ref)

    if comm:

        @pl.when(step < row_steps - 1)
        def _():
            cot_s[...] = cot_ref[...]

        @pl.when(step == row_steps - 1)
        def _():
            landed(c3_s, crecv.at[0])
            cot_s[...] = c3_s[...]

    @pl.when(step < row_steps)
    def _():
        at = pl.ds(pl.multiple_of(step * BLK, BLK), BLK)
        dropped = drop_ref[lax.axis_index("tensor")] == 1
        cot = (cot_s if comm else cot_ref)[...].astype(F32)
        att = att_ref[...]
        att_s[at, :] = att
        x = x_ref[...].astype(F32)
        branch = dot_nt(att, wo_ref[...]) + vec(0)
        n1, inv1 = norm_rows(x + branch)
        hidden = n1 * vec(1) + vec(2)
        low = hidden.astype(BF)
        ht_s[:, at] = jnp.transpose(low)
        ffn = hidden + vec(3)
        for t in range(parts):
            pre = dot_nn(low, up_ref[t]) + bin_ref[t * fl : (t + 1) * fl][None, :]
            act, slope = gelu_parts(pre)
            act = act.astype(BF)
            act_s[t, at, :] = act
            slope_s[t] = slope
            ffn = ffn + dot_nt(act, dn_ref[t])
        n2, inv2 = norm_rows(ffn)
        final = n2 * vec(4) + vec(5)
        layer_rows = jnp.where(dropped, x, final).astype(BF)
        if comm:
            l_s[flip(z, step)] = layer_rows
        else:
            lo_ref[...] = layer_rows
        g_final = jnp.where(dropped, 0.0, cot)
        g_fpre = norm_back(g_final, n2, inv2, vec(4))
        gb2 = g_fpre.astype(BF)
        gb2t_s[:, at] = jnp.transpose(gb2)
        g_hidden = g_fpre
        for t in range(parts):
            gpre = (dot_nn(gb2, dn_ref[t]) * slope_s[t]).astype(BF)
            gpre_s[t, at, :] = gpre
            bing_ref[:, t * fl : (t + 1) * fl] += jnp.sum(gpre.astype(F32), axis=0, keepdims=True)
            g_hidden = g_hidden + dot_nt(gpre, up_ref[t])
        g_hpre = norm_back(g_hidden, n1, inv1, vec(1))
        gb = g_hpre.astype(BF)
        gbt_s[:, at] = jnp.transpose(gb)
        gatt_ref[...] = dot_nn(gb, wo_ref[...]).astype(BF)
        ghpre_ref[...] = g_hpre + jnp.where(dropped, cot, 0.0)
        for r, v in enumerate(
            (gb.astype(F32), g_hidden * n1, g_hidden, gb2.astype(F32), g_final * n2, g_final)
        ):
            vecg_ref[r : r + 1, :] += jnp.sum(v, axis=0, keepdims=True)

    if comm:
        for k in range(row_steps):

            @pl.when(step == k)
            def _():
                if k == 0:
                    layer.own().start()
                else:
                    layer.copy(k).start()

    @pl.when((step >= row_steps) & (step < row_steps + parts))
    def _():
        t = step - row_steps
        gup_ref[...] = dot_nn(ht_s[...], gpre_s[t]).astype(BF)
        gdn_ref[...] = dot_nn(gb2t_s[...], act_s[t]).astype(BF)

    @pl.when(step == row_steps + parts)
    def _():
        gwo_ref[...] = dot_nn(gbt_s[...], att_s[...]).astype(BF)
        if comm:
            last_cot().wait_send()
            layer.wait_recv()
            layer.wait_send()


def middle(comm, drop, att, x, cot, cot_rows, wo, w, vecs, bias_in):
    length, d = att.shape
    _, parts, _, fl = w.shape
    nr = length // BLK

    def place_of(i):
        return flip(lax.axis_index("tensor"), i) if comm else i

    rows = pl.BlockSpec((BLK, d), lambda i: (place_of(jnp.minimum(i, nr - 1)), 0))
    cot_spec = pl.BlockSpec((BLK, d), lambda i: (place_of(jnp.minimum(i, nr - 1 - comm)), 0))
    any_ = pl.BlockSpec(memory_space=pl.ANY)
    once = lambda shape: pl.BlockSpec(
        shape, lambda i: (0,) * len(shape), pipeline_mode=pl.Buffered(1)
    )
    weight = lambda a: pl.BlockSpec(
        (None, parts, d, fl), lambda i: (a, 0, 0, 0), pipeline_mode=pl.Buffered(1)
    )
    part = pl.BlockSpec((None, d, fl), lambda i: (jnp.clip(i - nr, 0, parts - 1), 0, 0))
    whole = lambda shape: pl.BlockSpec(shape, lambda i: (0,) * len(shape))
    dma = pltpu.SemaphoreType.DMA
    comm_scratch = [
        pltpu.VMEM((BLK, d), BF),
        pltpu.VMEM((BLK, d), BF),
        pltpu.VMEM((nr, BLK, d), BF),
        dma((nr,)),
        dma((nr,)),
        dma((1,)),
        dma((1,)),
    ]
    extra = dict(collective_id=2, has_side_effects=True) if comm else {}
    return pl.pallas_call(
        functools.partial(middle_kernel, comm, nr),
        grid=(nr + parts + 1,),
        out_shape=(
            jax.ShapeDtypeStruct((nr, BLK, d) if comm else (length, d), BF),
            jax.ShapeDtypeStruct((length, d), BF),
            jax.ShapeDtypeStruct((length, d), F32),
            jax.ShapeDtypeStruct((parts, d, fl), BF),
            jax.ShapeDtypeStruct((parts, d, fl), BF),
            jax.ShapeDtypeStruct((d, d), BF),
            jax.ShapeDtypeStruct((8, d), F32),
            jax.ShapeDtypeStruct((1, parts * fl), F32),
        ),
        in_specs=[
            pl.BlockSpec(memory_space=pltpu.SMEM),
            rows,
            rows,
            cot_spec,
            any_,
            once((d, d)),
            weight(0),
            weight(1),
            *[once((d,))] * 6,
            once((parts * fl,)),
        ],
        out_specs=(
            any_ if comm else rows, rows, rows, part, part, whole((d, d)), whole((8, d)), whole((1, parts * fl)),
        ),
        scratch_shapes=[
            pltpu.VMEM((length, d), BF),
            pltpu.VMEM((parts, length, fl), BF),
            pltpu.VMEM((parts, length, fl), BF),
            pltpu.VMEM((parts, BLK, fl), F32),
            pltpu.VMEM((d, length), BF),
            pltpu.VMEM((d, length), BF),
            pltpu.VMEM((d, length), BF),
            *(comm_scratch if comm else []),
        ],
        compiler_params=pltpu.CompilerParams(vmem_limit_bytes=VMEM_LIMIT, **extra),
        name="middle",
    )(drop, att, x, cot, cot_rows, wo, w, w, *vecs, bias_in)


def columns(p, start=0):
    return pl.ds(pl.multiple_of(start + p * LANES, LANES), LANES)


def assemble(mix, nz, wqkv_ref, wo_ref):
    d = wo_ref.shape[0]
    wl = d // nz
    for j in range(4):
        whole = jnp.concatenate([mix(t)[:, j * wl : (j + 1) * wl] for t in range(nz)], axis=1)
        if j < 3:
            wqkv_ref[:, j * d : (j + 1) * d] = whole
        else:
            wo_ref[...] = whole


def first_kernel(
    tok_ref, cot_ref, qkvw_ref, wow_ref, upw_ref, dnw_ref, bias_ref, seg_ref,
    x_out, cot_out, wud_out, qkv_out, wqkv_out, xt_out, wo_ref, att_ref, lse_ref, ext_ref,
    sh_ref, mix_s, x_s, qkv_s, wqkv_s, xt_s, kx_s, qx_s, vt_s,
    out_sem, send, recv, local, tsend, trecv, csend, crecv,
):
    nz = mix_s.shape[1]
    length, d = att_ref.shape
    pairs = d // LANES
    blk = length // nz
    here = Here(nz)
    mix = Gather(here, mix_s, sh_ref, 0, 1, send, recv, local)
    rest = Gather(here, wud_out, sh_ref, 1, 2, send, recv, local)
    tokens = Exchange(here, tok_ref, x_s, tsend, trecv)
    cots = Exchange(here, cot_ref, cot_out, csend, crecv, (1, 2))
    sh_ref[0] = jnp.concatenate(
        (qkvw_ref[0], qkvw_ref[1], qkvw_ref[2], wow_ref[...]), axis=1
    )
    here.greet()
    mix.stage1(0)
    sh_ref[1] = upw_ref[...]
    sh_ref[2] = dnw_ref[...]
    seg = jnp.transpose(jnp.broadcast_to(seg_ref[pl.ds(here.z, 1), :], (LANES, length)))
    doc_lanes(seg, kx_s, qx_s)
    ext_ref[:, :LANES] = kx_s[:, LANES:]
    ext_ref[:, LANES:] = qx_s[:, LANES:]
    vt_s[:, HD:, :] = jnp.ones((2, vt_s.shape[1] - HD, length), BF)
    rest.stage1(0)
    mix.stage1(1)
    mix.stage1(2)
    rest.stage1(1)
    mix.stage1(3)
    tokens.start()
    mix.stage2(0)
    mix.stage2(1)
    mix.stage3(0)
    mix.stage2(2)
    mix.stage3(1)
    mix.stage2(3)
    mix.stage3(2)
    mix.stage3(3)
    rest.stage2(0)
    rest.stage1(2)
    mix.drain()
    assemble(lambda t: mix_s[0, t].reshape(d, -1), nz, wqkv_s, wo_ref)
    rest.stage2(1)
    rest.stage3(0)
    tokens.wait_recv()
    rest.stage1(3)
    cots.start()
    between = [
        [lambda: rest.stage2(2), lambda: rest.stage3(1)],
        [lambda: rest.stage2(3), lambda: rest.stage3(2)],
        [lambda: rest.stage3(3)],
    ]
    out_x = pltpu.make_async_copy(x_s, x_out, out_sem.at[0])
    out_qkv = pltpu.make_async_copy(qkv_s, qkv_out, out_sem.at[1])
    out_w = pltpu.make_async_copy(wqkv_s, wqkv_out, out_sem.at[2])
    out_xt = pltpu.make_async_copy(xt_s, xt_out, out_sem.at[3])
    out_x.start()
    out_w.start()
    bias = jnp.concatenate(
        (bias_ref[0:1, :], jnp.zeros((1, d), F32), bias_ref[1:2, :]), axis=1
    )

    def body(i, carry):
        at = pl.ds(pl.multiple_of(i * blk, blk), blk)
        qkv_s[at, :] = (dot_nn(x_s[i], wqkv_s[...]) + bias).astype(BF)
        return carry

    lax.fori_loop(0, nz, body, 0)
    out_qkv.start()
    for i in range(nz):
        xt_s[:, i * blk : (i + 1) * blk] = jnp.transpose(x_s[i])
    out_xt.start()

    def work(p):
        o, lse = attend_pair(
            qkv_s[:, columns(p)], qkv_s[:, columns(p, d)], qkv_s[:, columns(p, 2 * d)], kx_s, qx_s, vt_s
        )
        att_ref[:, columns(p)] = o
        lse_ref[p] = lse

    every_pair(pairs, work, between)
    rest.drain()
    tokens.wait_send()
    cots.wait_recv()
    cots.wait_send()
    for copy in (out_x, out_qkv, out_w, out_xt):
        copy.wait()


def first(tokens, cot, qkv_w, wo_w, up_w, dn_w, qv_b, segment_ids):
    nz, nd = lax.axis_size("tensor"), lax.axis_size("dp")
    na, (rw, wide) = 3, up_w.shape
    _, blk, d = tokens.shape
    length = segment_ids.shape[1]
    pairs = d // LANES
    any_ = pl.BlockSpec(memory_space=pl.ANY)
    vmem = pl.BlockSpec(memory_space=pltpu.VMEM)
    dma = pltpu.SemaphoreType.DMA
    s = jax.ShapeDtypeStruct
    unit = (nz, nd // 2, 2, rw, wide)
    return pl.pallas_call(
        first_kernel,
        out_shape=(
            s(tokens.shape, BF),
            s(tokens.shape, BF),
            s((na - 1,) + unit, BF),
            s((length, 3 * d), BF),
            s((d, 3 * d), BF),
            s((d, length), BF),
            s((d, d), BF),
            s((length, d), BF),
            s((pairs, 2, length), F32),
            s((length, 2 * LANES), BF),
        ),
        in_specs=[any_, any_] + [vmem] * 6,
        out_specs=(any_,) * 6 + (vmem,) * 4,
        scratch_shapes=[
            pltpu.VMEM((na, rw, wide), BF),
            pltpu.VMEM((1,) + unit, BF),
            pltpu.VMEM((nz, blk, d), BF),
            pltpu.VMEM((length, 3 * d), BF),
            pltpu.VMEM((d, 3 * d), BF),
            pltpu.VMEM((d, length), BF),
            pltpu.VMEM((length, 2 * LANES), BF),
            pltpu.VMEM((length, 2 * LANES), BF),
            pltpu.VMEM((2, HD + 16, length), BF),
            dma((4,)),
            dma((na, nz, 10)),
            dma((na, nz, 6)),
            dma((na,)),
            dma((nz,)),
            dma((nz,)),
            dma((nz,)),
            dma((nz,)),
        ],
        compiler_params=pltpu.CompilerParams(
            collective_id=0, has_side_effects=True, vmem_limit_bytes=VMEM_LIMIT
        ),
        name="first",
    )(tokens, cot, qkv_w, wo_w, up_w, dn_w, qv_b, segment_ids)


def last_kernel(
    gup_ref, gdn_ref, gwo_ref, ghpre_ref, qkv_ref, att_ref, gatt_ref, wqkv_ref, xt_ref,
    lse_ref, ext_ref, vecg_ref, bing_ref,
    grows_ref, out_ref, vsum_ref,
    pair_s, g_s, w_s, xt_s, hpre_s, gwo_s, gx_s, kx_s, qx_s, kt_s, delta_s, dk_s, dv_s, vbuf,
    u0, u1, u2, u3, u4, u5, u6, m0, m1, m2, m3, m4, m5, m6,
    psem, hsem, load, uload, send, recv, xsend, xrecv, vsend, vrecv,
):
    nz = u0.shape[1]
    length, d = g_s.shape[1:]
    pairs = d // LANES
    blk = length // nz
    wl = d // nz
    here = Here(nz)
    z = here.z
    ud = Scatter(here, u0, u1, u2, u3, u4, u5, u6, 1, send, recv)
    mx = Scatter(here, m0, m1, m2, m3, m4, m5, m6, 0, send, recv)
    rows = Exchange(here, gx_s, grows_ref, xsend, xrecv)

    def pair_loads(p, slot):
        srcs = (
            qkv_ref.at[:, columns(p)], qkv_ref.at[:, columns(p, d)], qkv_ref.at[:, columns(p, 2 * d)],
            att_ref.at[:, columns(p)], gatt_ref.at[:, columns(p)],
        )
        return [
            pltpu.make_async_copy(src, pair_s.at[slot, j], psem.at[slot, j])
            for j, src in enumerate(srcs)
        ]

    def ud_loads(k):
        t = ud.order[k]
        return [
            pltpu.make_async_copy(g.at[t], u0.at[a, t], uload.at[a, t])
            for a, g in enumerate((gup_ref, gdn_ref))
        ]

    later = [
        pltpu.make_async_copy(src, dst, load.at[i])
        for i, (src, dst) in enumerate(((wqkv_ref, w_s), (xt_ref, xt_s), (gwo_ref, gwo_s)))
    ]

    def hpre_load(i, slot):
        return pltpu.make_async_copy(ghpre_ref.at[i], hpre_s.at[slot], hsem.at[slot])

    for copy in pair_loads(0, 0):
        copy.start()
    for k in range(nz):
        for copy in ud_loads(k):
            copy.start()
    here.greet()
    kx_s[:, LANES:] = ext_ref[:, :LANES]
    qx_s[:, LANES:] = ext_ref[:, LANES:]
    for k in range(nz):
        for copy in ud_loads(k):
            copy.wait()
        ud.stage1(k)

    def work(p):
        slot = p % 2

        @pl.when(p + 1 < pairs)
        def _():
            for copy in pair_loads(p + 1, 1 - slot):
                copy.start()

        for copy in pair_loads(p, slot):
            copy.wait()
        q, k, v, att, g = [pair_s.at[slot, j] for j in range(5)]

        def put_q(at, value):
            g_s[0, at, columns(p)] = value

        attend_pair_back(q, k, v, att, g, lse_ref[p], kx_s, qx_s, kt_s, delta_s, dk_s, dv_s, put_q)
        g_s[1, :, columns(p)] = dk_s[...].astype(BF)
        g_s[2, :, columns(p)] = dv_s[...].astype(BF)

    def start_later():
        for copy in later:
            copy.start()

    def run(*names):
        return [lambda name=name, k=k: getattr(ud, name)(k) for name, k in names]

    between = [
        run(("stage2", 0), ("stage2", 1)),
        run(("stage2", 2), ("stage3", 0), ("stage2", 3)),
        run(("stage3", 1),) + [start_later],
        run(("stage4", 0), ("stage5", 0), ("stage3", 2)),
        run(("stage3", 3), ("stage4", 1), ("stage5", 1)),
    ]
    every_pair(pairs, work, between)

    place_of = [flip(z, k) for k in (2, 3, 1, 0)]
    hpre_load(place_of[0], 0).start()
    for copy in later:
        copy.wait()
    for i, to in enumerate(place_of):
        if i + 1 < nz:
            hpre_load(place_of[i + 1], (i + 1) % 2).start()
        hpre_load(to, i % 2).wait()
        at = pl.ds(pl.multiple_of(to * blk, blk), blk)
        total = hpre_s[i % 2]
        for j in range(3):
            total = total + dot_nt(g_s[j, at, :], w_s[:, j * d : (j + 1) * d])
        gx_s[to] = total.astype(BF)
        if i + 1 < nz:
            rows.copy((2, 3, 1)[i]).start()
        else:
            rows.own().start()

    ud.stage4(2)
    ud.stage5(2)

    vsum_ref[...] = jnp.zeros_like(vsum_ref)
    vsum_ref[0:8, :] = vecg_ref[...]
    for i in range(bing_ref.shape[1] // d):
        vsum_ref[8 + i : 9 + i, :] = bing_ref[:, i * d : (i + 1) * d]
    xt = xt_s[...]
    for j in range(3):
        grad = dot_nn(xt, g_s[j]).astype(BF)
        for t in range(nz):
            part = grad[:, t * wl : (t + 1) * wl]
            m0[0, t, :, :, :, j * wl : (j + 1) * wl] = part.reshape(m0.shape[2:5] + (wl,))
        if j != 1:
            sums = jnp.sum(g_s[j].astype(F32), axis=0, keepdims=True)
            r = vsum_ref.shape[0] - 2 + j // 2
            vsum_ref[r : r + 1, :] = sums
    for t in range(nz):
        part = gwo_s[:, t * wl : (t + 1) * wl]
        m0[0, t, :, :, :, 3 * wl :] = part.reshape(m0.shape[2:5] + (wl,))

    partners = [(here.dev_c, z), (here.dev_x, z), (here.dev_y, z)]
    partners += [(here.dp, z + 1 - 2 * (z % 2)), (here.dp, (z + 2) % nz)]

    def vec_copy(k):
        return remote(vbuf.at[0, k], vbuf.at[1, k], vsend.at[k], vrecv.at[k], *partners[k])

    def vec_start(k):
        vbuf[0, k] = vsum_ref[...]
        vec_copy(k).start()

    def vec_finish(k):
        landed(vbuf.at[1, k], vrecv.at[k])
        vsum_ref[...] += vbuf[1, k]

    for k in range(nz):
        mx.stage1(k)
    vec_start(0)
    for k in range(nz + 3):
        if k < nz:
            mx.stage2(k)
        if 1 <= k <= nz:
            mx.stage3(k - 1)
        if k < len(partners):
            vec_finish(k)
            if k + 1 < len(partners):
                vec_start(k + 1)
        if 2 <= k <= nz + 1:
            mx.stage4(k - 2)
        if 3 <= k <= nz + 1:
            mx.stage5(k - 3)
    ud.stage4(3)
    ud.finish(out_ref)
    mx.finish(out_ref)
    ud.drain()
    mx.drain()
    for k in range(len(partners)):
        vec_copy(k).wait_send()
    rows.wait_recv()
    rows.wait_send()


def last(gup, gdn, gwo, ghpre, qkv, att, gatt, wqkv, xt, lse, ext, vecg, bing):
    nz, nd = lax.axis_size("tensor"), lax.axis_size("dp")
    length, d = att.shape
    rw, wide = d // nd, gup.shape[2]
    blk = length // nz
    unit = (nz, nd // 2, 2, rw, wide)
    any_ = pl.BlockSpec(memory_space=pl.ANY)
    vmem = pl.BlockSpec(memory_space=pltpu.VMEM)
    dma = pltpu.SemaphoreType.DMA
    s = jax.ShapeDtypeStruct
    steps = 5
    vec_shape = (16, d)
    return pl.pallas_call(
        last_kernel,
        out_shape=(
            s((nz, blk, d), BF),
            s((3, rw, wide), F32),
            s(vec_shape, F32),
        ),
        in_specs=[any_] * 9 + [vmem] * 4,
        out_specs=(any_, vmem, vmem),
        scratch_shapes=[
            pltpu.VMEM((2, 5, length, LANES), BF),
            pltpu.VMEM((3, length, d), BF),
            pltpu.VMEM((d, 3 * d), BF),
            pltpu.VMEM((d, length), BF),
            pltpu.VMEM((2, blk, d), F32),
            pltpu.VMEM((d, d), BF),
            pltpu.VMEM((nz, blk, d), BF),
            pltpu.VMEM((length, 2 * LANES), BF),
            pltpu.VMEM((length, 2 * LANES), BF),
            pltpu.VMEM((LANES, length), BF),
            pltpu.VMEM((8, length), F32),
            pltpu.VMEM((length, LANES), F32),
            pltpu.VMEM((length, LANES), F32),
            pltpu.VMEM((2, steps) + vec_shape, F32),
        ]
        + scatter_scratch(2, nz, nd, rw, wide)
        + scatter_scratch(1, nz, nd, rw, wide)
        + [
            dma((2, 5)),
            dma((2,)),
            dma((3,)),
            dma((2, nz)),
            dma((3, nz, 7)),
            dma((3, nz, 7)),
            dma((nz,)),
            dma((nz,)),
            dma((steps,)),
            dma((steps,)),
        ],
        compiler_params=pltpu.CompilerParams(
            collective_id=1, has_side_effects=True, vmem_limit_bytes=LAST_LIMIT
        ),
        name="last",
    )(
        gup.reshape(unit), gdn.reshape(unit), gwo, ghpre.reshape(nz, blk, d),
        qkv, att, gatt, wqkv, xt, lse, ext, vecg, bing,
    )


LAST_LIMIT = 61 * 1024 * 1024


def plain_attend_kernel(q_ref, k_ref, v_ref, segc_ref, o_ref, lse_ref, kx_s, qx_s, vt_s):
    doc_lanes(segc_ref[...], kx_s, qx_s)
    vt_s[:, HD:, :] = jnp.ones((2, vt_s.shape[1] - HD, vt_s.shape[2]), BF)
    o_ref[...], lse_ref[...] = attend_pair(q_ref[...], k_ref[...], v_ref[...], kx_s, qx_s, vt_s)


def plain_attend_back_kernel(
    q_ref, k_ref, v_ref, att_ref, g_ref, lse_ref, segc_ref, gq_ref, gk_ref, gv_ref,
    kx_s, qx_s, kt_s, delta_s, dk_s, dv_s,
):
    doc_lanes(segc_ref[...], kx_s, qx_s)

    def put_q(at, value):
        gq_ref[at, :] = value

    attend_pair_back(
        q_ref, k_ref, v_ref, att_ref, g_ref, lse_ref[...], kx_s, qx_s, kt_s, delta_s, dk_s, dv_s, put_q
    )
    gk_ref[...] = dk_s[...].astype(BF)
    gv_ref[...] = dv_s[...].astype(BF)


def plain_specs(length, d):
    col = lambda off: pl.BlockSpec((length, LANES), lambda p: (0, off + p))
    seg = pl.BlockSpec((length, LANES), lambda p: (0, 0))
    lse = pl.BlockSpec((None, 2, length), lambda p: (p, 0, 0))
    wide = pltpu.VMEM((length, 2 * LANES), BF)
    return d // LANES, col, seg, lse, wide


def plain_first(tokens, cot, qkv_w, wo_w, up_w, dn_w, qv_b, segment_ids):
    axes = ("tensor", "dp")
    nz = lax.axis_size("tensor")
    length, d = segment_ids.shape[1], tokens.shape[2]
    pairs, col, seg, lse_spec, wide = plain_specs(length, d)
    mix = jnp.concatenate((qkv_w[0], qkv_w[1], qkv_w[2], wo_w), axis=1)
    shards = jnp.stack((mix, up_w, dn_w))
    ids = lax.dynamic_index_in_dim(segment_ids, lax.axis_index("tensor"), 0, keepdims=False)
    segc = jnp.broadcast_to(ids[:, None], (length, LANES))
    bias = jnp.concatenate((qv_b[0], jnp.zeros((d,), F32), qv_b[1]))
    x = lax.all_to_all(tokens, "tensor", 0, 0)
    cot = lax.all_to_all(cot, "tensor", 0, 0)
    w = lax.all_gather(shards, axes, axis=1, tiled=True).reshape(3, nz, d, shards.shape[2])
    parts = w[0].reshape(nz, d, 4, d // nz).transpose(1, 2, 0, 3).reshape(d, 4 * d)
    wqkv, wo = parts[:, : 3 * d], parts[:, 3 * d :]
    rows = x.reshape(length, d)
    qkv = (dot_nn(rows, wqkv) + bias).astype(BF)
    att, lse = pl.pallas_call(
        plain_attend_kernel,
        grid=(pairs,),
        out_shape=(
            jax.ShapeDtypeStruct((length, d), BF),
            jax.ShapeDtypeStruct((pairs, 2, length), F32),
        ),
        in_specs=[col(0), col(pairs), col(2 * pairs), seg],
        out_specs=(col(0), lse_spec),
        scratch_shapes=[wide, wide, pltpu.VMEM((2, HD + 16, length), BF)],
        compiler_params=pltpu.CompilerParams(vmem_limit_bytes=VMEM_LIMIT),
        name="plain_attend",
    )(qkv, qkv, qkv, segc)
    return x, cot, w[1:], qkv, wqkv, rows.T, wo, att, lse, segc


def plain_last(gup, gdn, gwo, ghpre, qkv, att, gatt, wqkv, xt, lse, segc, vecg, bing):
    axes = ("tensor", "dp")
    nz = lax.axis_size("tensor")
    length, d = att.shape
    pairs, col, seg, lse_spec, wide = plain_specs(length, d)
    f32_wide = pltpu.VMEM((length, LANES), F32)
    grads = pl.pallas_call(
        plain_attend_back_kernel,
        grid=(pairs,),
        out_shape=[jax.ShapeDtypeStruct((length, d), BF)] * 3,
        in_specs=[col(0), col(pairs), col(2 * pairs), col(0), col(0), lse_spec, seg],
        out_specs=[col(0)] * 3,
        scratch_shapes=[
            wide, wide, pltpu.VMEM((LANES, length), BF), pltpu.VMEM((8, length), F32), f32_wide, f32_wide,
        ],
        compiler_params=pltpu.CompilerParams(vmem_limit_bytes=VMEM_LIMIT),
        name="plain_attend_back",
    )(qkv, qkv, qkv, att, gatt, lse, segc)
    g = jnp.concatenate(grads, axis=1)
    gx = (ghpre + dot_nt(g, wqkv)).astype(BF)
    gmix = jnp.concatenate((dot_nn(xt, g).astype(BF), gwo), axis=1)
    gmix = gmix.reshape(d, 4, nz, d // nz).transpose(2, 0, 1, 3).reshape(nz, d, -1)
    split = lambda a: a.reshape(nz, length // nz, d)
    parts = [
        lax.psum_scatter(p.reshape(nz * d, -1), axes, scatter_dimension=0, tiled=True)
        for p in (gmix, gup, gdn)
    ]
    sums = [jnp.sum(grads[j].astype(F32), axis=0, keepdims=True) for j in (0, 2)]
    bing = bing.reshape(-1, d)
    gap = jnp.zeros((6 - bing.shape[0], d), F32)
    vec = jnp.concatenate((vecg, bing, gap, *sums), axis=0)
    return (
        lax.all_to_all(split(gx), "tensor", 0, 0),
        jnp.stack(parts).astype(F32),
        lax.psum(vec, axes),
    )


def on_device(
    tokens, segment_ids, drop_flags, qkv_w, qv_b, wo_w, wo_b, gain1, shift1,
    up_w, up_b, dn_w, dn_b, gain2, shift2, cotangent,
):
    nt, nd = lax.axis_size("tensor"), lax.axis_size("dp")
    d = tokens.shape[2]
    length = segment_ids.shape[1]
    wl = qkv_w.shape[2]
    fl = up_w.shape[1]
    comm = (nt, nd) == (4, 8)
    begin, end = (first, last) if comm else (plain_first, plain_last)
    x, cot, wud, qkv, wqkv, xt, wo, att, lse, ext = begin(
        tokens, cotangent, qkv_w, wo_w.T, up_w, dn_w.T, qv_b, segment_ids
    )
    vecs = (wo_b, gain1, shift1, dn_b, gain2, shift2)
    layer_out, g_att, g_hpre, gup, gdn, gwo, vecg, bing = middle(
        comm, drop_flags, att, x.reshape(length, d), cot.reshape(length, d), cotangent, wo,
        wud.reshape(2, nt, d, fl), vecs, up_b,
    )
    if not comm:
        layer_out = lax.all_to_all(layer_out.reshape(nt, length // nt, d), "tensor", 0, 0)
    rows, grads, total = end(
        gup, gdn, gwo, g_hpre, qkv, att, g_att, wqkv, xt, lse, ext, vecg, bing
    )
    g_mix, g_up, g_dn = grads[0], grads[1], grads[2]
    n_bin = nt * fl // d
    return (
        layer_out,
        rows.astype(F32),
        jnp.stack([g_mix[:, j * wl : (j + 1) * wl] for j in range(3)]),
        total[-2:],
        g_mix[:, 3 * wl :].T,
        total[0],
        total[1],
        total[2],
        g_up,
        total[8 : 8 + n_bin].reshape(-1),
        g_dn.T,
        total[3],
        total[4],
        total[5],
    )


def solution(mesh):
    rows = P("dp", "tensor", None)
    return jax.shard_map(
        on_device,
        mesh=mesh,
        in_specs=(
            rows, P("dp", None), P("dp"), P(None, "dp", "tensor"), P(), P("tensor", "dp"), P(), P(), P(),
            P("dp", "tensor"), P(), P("tensor", "dp"), P(), P(), P(), rows,
        ),
        out_specs=(
            rows, rows, P(None, "dp", "tensor"), P(), P("tensor", "dp"), P(), P(), P(),
            P("dp", "tensor"), P(), P("tensor", "dp"), P(), P(), P(),
        ),
        check_vma=False,
    )
```

```python
import functools
import jax
import jax.numpy as jnp
from jax import lax
from jax.experimental import pallas as pl
from jax.experimental.pallas import tpu as pltpu
from jax.sharding import PartitionSpec as P

HD = 64
EPS = 1e-05
NEG = -1000000000.0
BF = jnp.bfloat16
F32 = jnp.float32
VMEM_LIMIT = 60 * 1024 * 1024
BLK = 256
LANES = 128


def dot_nn(a, b):
    return jnp.dot(a, b, preferred_element_type=F32)


def dot_nt(a, b):
    return lax.dot_general(a, b, (((1,), (1,)), ((), ())), preferred_element_type=F32)


def dot_tn(a, b):
    return lax.dot_general(a, b, (((0,), (0,)), ((), ())), preferred_element_type=F32)


def doc_lanes(seg, kx_s, qx_s):
    lane = lax.broadcasted_iota(jnp.int32, seg.shape, 1)
    same = (seg == lane).astype(F32)
    kx_s[:, LANES:] = same.astype(BF)
    qx_s[:, LANES:] = ((1.0 - same) * NEG).astype(BF)


def split_heads(pair):
    first = lax.broadcasted_iota(jnp.int32, pair.shape, 1) % (2 * HD) < HD
    zero = jnp.zeros((), pair.dtype)
    return jnp.where(first, pair, zero), jnp.where(first, zero, pair)


def attend_pair(q, k, v, kx_s, qx_s, vt_s):
    kx_s[:, :LANES] = k
    qx_s[:, :LANES] = (q.astype(F32) * 0.125).astype(BF)
    vt = jnp.transpose(v)
    vt_s[0, :HD, :] = vt[:HD, :]
    vt_s[1, :HD, :] = vt[HD:, :]
    kx = kx_s[...]
    ext = qx_s[:, LANES:]
    outs, lses = [], []
    scores = [
        dot_nt(kx, jnp.concatenate((h, ext), axis=1)) for h in split_heads(qx_s[:, :LANES])
    ]
    for h in range(2):
        top = jnp.max(scores[h], axis=0, keepdims=True)
        p = jnp.exp(scores[h] - top).astype(BF)
        o = dot_nn(vt_s[h], p)
        total = o[HD : HD + 1, :]
        outs.append(o[:HD, :] / total)
        lses.append(top + jnp.log(total))
    return jnp.transpose(jnp.concatenate(outs, axis=0)).astype(BF), jnp.concatenate(lses, axis=0)


def attend_pair_back(q_ref, k_ref, v_ref, att_ref, g_ref, lse, kx_s, qx_s, kt_s, delta_s, dk_s, dv_s, put_q):
    length = q_ref.shape[0]
    kx_s[:, :LANES] = k_ref[...]
    qx_s[:, :LANES] = (q_ref[...].astype(F32) * 0.125).astype(BF)
    kt_s[...] = jnp.transpose(k_ref[...])
    sub = lax.broadcasted_iota(jnp.int32, (8, LANES), 0)
    lane = lax.broadcasted_iota(jnp.int32, (8, LANES), 1)
    pick = jnp.where(lane // HD == sub, 1.0, 0.0).astype(F32)
    prod = g_ref[...].astype(F32) * att_ref[...].astype(F32)
    delta_s[...] = lax.dot_general(
        pick, prod, (((1,), (1,)), ((), ())),
        preferred_element_type=F32, precision=lax.Precision.HIGHEST,
    )
    for i in range(length // QB):
        at = slice(i * QB, (i + 1) * QB)
        kx = kx_s[...]
        v = v_ref[...]
        ext = qx_s[at, LANES:]
        qs = split_heads(qx_s[at, :LANES])
        gs = split_heads(g_ref[at, :])
        ps, ds, dq = [], [], []
        for h in range(2):
            s = dot_nt(kx, jnp.concatenate((qs[h], ext), axis=1))
            p = jnp.exp(s - lse[h : h + 1, at])
            dp = dot_nt(v, gs[h])
            d = (p * (dp - delta_s[h : h + 1, at])).astype(BF)
            ps.append(p.astype(BF))
            ds.append(d)
            dq.append(dot_nn(kt_s[h * HD : (h + 1) * HD, :], d))
        dv = dot_nn(jnp.concatenate(ps, axis=1), jnp.concatenate(gs, axis=0))
        dk = dot_nn(jnp.concatenate(ds, axis=1), jnp.concatenate(qs, axis=0))
        dv_s[...] = dv if i == 0 else dv_s[...] + dv
        dk_s[...] = dk if i == 0 else dk_s[...] + dk
        put_q(at, (jnp.transpose(jnp.concatenate(dq, axis=0)) * 0.125).astype(BF))


QB = 512


def place(dp):
    yx, core = dp // 2, dp % 2
    y, x = yx // 2, yx % 2
    return yx, core, y * 2 + 1 - x, (1 - y) * 2 + x, 3 - yx


def remote(src, dst, send, recv, dp, z):
    return pltpu.make_async_remote_copy(
        src_ref=src,
        dst_ref=dst,
        send_sem=send,
        recv_sem=recv,
        device_id=(dp, z),
        device_id_type=pl.DeviceIdType.MESH,
    )


def greet(dp, z, yx, core, yx_x, yx_y, nz):
    barrier = pltpu.get_barrier_semaphore()
    others = [(yx_x * 2 + core, z), (yx_y * 2 + core, z), (yx * 2 + 1 - core, z)]
    others += [(dp, (z + k) % nz) for k in range(1, nz)]
    for dev in others:
        pl.semaphore_signal(
            barrier, inc=1, device_id=dev, device_id_type=pl.DeviceIdType.MESH
        )
    pl.semaphore_wait(barrier, len(others))


def landed(ref, sem):
    pltpu.make_async_copy(ref, ref, sem).wait()


class Here:
    def __init__(self, nz):
        self.nz = nz
        self.dp, self.z = lax.axis_index("dp"), lax.axis_index("tensor")
        self.yx, self.core, self.yx_x, self.yx_y, self.yx_d = place(self.dp)
        self.dev_x = self.yx_x * 2 + self.core
        self.dev_y = self.yx_y * 2 + self.core
        self.dev_c = self.yx * 2 + 1 - self.core

    def greet(self):
        greet(self.dp, self.z, self.yx, self.core, self.yx_x, self.yx_y, self.nz)

    def sides(self, s, body):
        if s == 0:
            body(self.z, None)
            return

        @pl.when(self.z >= s)
        def _():
            body(self.z - s, True)

        @pl.when(self.z + s < self.nz)
        def _():
            body(self.z + s, False)


def flip(z, i):
    return (z % 2 + i % 2) % 2 + 2 * ((z // 2 + i // 2) % 2)


class Exchange:
    def __init__(self, here, src, dst, send, recv, ks=(1, 2, 3)):
        self.here, self.src, self.dst, self.send, self.recv, self.ks = here, src, dst, send, recv, ks

    def copy(self, k):
        h = self.here
        to = flip(h.z, k)
        return remote(
            self.src.at[to], self.dst.at[h.z], self.send.at[k], self.recv.at[k], h.dp, to
        )

    def own(self):
        z = self.here.z
        return pltpu.make_async_copy(self.src.at[z], self.dst.at[z], self.send.at[0])

    def start(self):
        for k in self.ks:
            self.copy(k).start()
        self.own().start()

    def got(self, k):
        landed(self.dst.at[flip(self.here.z, k)], self.recv.at[k])

    def wait_recv(self):
        self.own().wait()
        for k in self.ks:
            self.got(k)

    def wait_send(self):
        for k in self.ks:
            self.copy(k).wait_send()


class Gather:
    def __init__(self, here, w_ref, sh_ref, group, send, recv, line, local):
        self.here, self.w, self.sh = here, w_ref, sh_ref
        self.send = lambda kind: send.at[group, kind]
        self.recv = lambda t, kind: recv.at[group, t, kind]
        self.line = lambda t, kind: line.at[group, t, kind]
        self.all_cores = recv.at[group, 0, 5]
        self.local = local.at[group]
        half = w_ref.shape[4] // 2
        self.low, self.high = pl.ds(0, half), pl.ds(half, half)

    def blk(self, t, yx):
        return self.w.at[t, yx, self.here.core]

    def to_plane(self, t, own, kind):
        h = self.here
        dst = self.blk(t, h.yx)
        dev = (h.dev_x, h.dev_y, h.dev_c)[kind]
        arrived = self.all_cores if kind == 2 else self.recv(t, kind)
        return remote(self.sh if own else dst, dst, self.send(kind), arrived, dev, h.z)

    def to_line(self, t, own, kind):
        h = self.here
        dst = self.blk(t, h.yx)
        to = (h.z + 1) % h.nz if kind == 0 else (h.z + h.nz - 1) % h.nz
        return remote(self.sh if own else dst, dst, self.line(t, kind), self.recv(t, 4), h.dp, to)

    def own_copy(self):
        return pltpu.make_async_copy(self.sh, self.blk(self.here.z, self.here.yx), self.local)

    def half_y(self, t):
        b = self.w.at[t, self.here.yx_x, self.here.core, :, self.low]
        return remote(b, b, self.send(3), self.recv(t, 2), self.here.dev_y, self.here.z)

    def half_x(self, t):
        b = self.w.at[t, self.here.yx_y, self.here.core, :, self.high]
        return remote(b, b, self.send(4), self.recv(t, 3), self.here.dev_x, self.here.z)

    def to_core(self, t, yx, kind):
        b = self.blk(t, yx)
        return remote(b, b, self.send(kind), self.all_cores, self.here.dev_c, self.here.z)

    def along(self, s, from_left, right, left):
        h = self.here
        if s == 0 or from_left:
            pl.when(h.z < h.nz - 1)(right)
        if s == 0 or not from_left:
            pl.when(h.z > 0)(left)

    def stage1(self, s):
        own = s == 0

        def body(t, from_left):
            if own:
                self.own_copy().start()
            else:
                landed(self.blk(t, self.here.yx), self.recv(t, 4))
            self.along(
                s, from_left,
                lambda: self.to_line(t, own, 0).start(), lambda: self.to_line(t, own, 1).start(),
            )
            for kind in range(3):
                self.to_plane(t, own, kind).start()

        self.here.sides(s, body)

    def stage2(self, s):
        h = self.here

        def body(t, from_left):
            landed(self.blk(t, h.yx_x), self.recv(t, 0))
            self.half_y(t).start()
            self.to_core(t, h.yx_x, 5).start()
            landed(self.blk(t, h.yx_y), self.recv(t, 1))
            self.half_x(t).start()
            self.to_core(t, h.yx_y, 6).start()

        h.sides(s, body)

    def stage3(self, s):
        h = self.here

        def body(t, from_left):
            landed(self.w.at[t, h.yx_d, h.core, :, self.low], self.recv(t, 2))
            landed(self.w.at[t, h.yx_d, h.core, :, self.high], self.recv(t, 3))
            self.to_core(t, h.yx_d, 7).start()

        h.sides(s, body)

    def drain(self):
        h, w = self.here, self.w
        landed(w.at[:, :, 1 - h.core], self.all_cores)
        self.own_copy().wait()
        for kind in (0, 1, 2, 5, 6, 7):
            landed(w.at[:, h.yx, h.core], self.send(kind))
        landed(w.at[:, h.yx_x, h.core, :, self.low], self.send(3))
        landed(w.at[:, h.yx_y, h.core, :, self.high], self.send(4))
        for s in range(h.nz):

            def body(t, from_left):
                self.along(
                    s, from_left,
                    lambda: self.to_line(t, s == 0, 0).wait_send(),
                    lambda: self.to_line(t, s == 0, 1).wait_send(),
                )

            h.sides(s, body)


class Scatter:
    def __init__(self, here, own, rc, rda, rdb, rx, ry, rz, group, send, recv, order=None):
        self.here, self.own = here, own
        self.rc, self.rda, self.rdb, self.rx, self.ry, self.rz = rc, rda, rdb, rx, ry, rz
        self.send = lambda kind: send.at[group, kind]
        self.recv = lambda t, kind: recv.at[group, t, kind]
        half = own.shape[4] // 2
        self.low, self.high = pl.ds(0, half), pl.ds(half, half)
        z = here.z
        self.order = order or [3 * (1 - z // 2), (2 + 3 * z) % 5, 1 + z % 2, z]

    def copy(self, t, kind):
        h, own = self.here, self.own
        src, dst, dev, z = (
            lambda: (own.at[t, :, 1 - h.core], self.rc.at[t], h.dev_c, h.z),
            lambda: (own.at[t, h.yx_d, h.core, :, self.low], self.rda.at[t], h.dev_x, h.z),
            lambda: (own.at[t, h.yx_d, h.core, :, self.high], self.rdb.at[t], h.dev_y, h.z),
            lambda: (own.at[t, h.yx_x, h.core], self.rx.at[t], h.dev_x, h.z),
            lambda: (own.at[t, h.yx_y, h.core], self.ry.at[t], h.dev_y, h.z),
            lambda: (own.at[t, h.yx, h.core], self.rz.at[0, t], h.dp, (h.z + 1) % h.nz),
            lambda: (own.at[t, h.yx, h.core], self.rz.at[1, t], h.dp, (h.z + h.nz - 1) % h.nz),
        )[kind]()
        return remote(src, dst, self.send(min(kind, 5)), self.recv(t, kind), dev, z)

    def add(self, dst, *srcs):
        total = dst[...].astype(F32)
        for src in srcs:
            total = total + src[...].astype(F32)
        dst[...] = total.astype(BF)

    def stage1(self, k):
        self.copy(self.order[k], 0).start()

    def stage2(self, k):
        h, t = self.here, self.order[k]
        landed(self.rc.at[t], self.recv(t, 0))
        self.add(self.own.at[t, h.yx_d, h.core], self.rc.at[t, h.yx_d])
        self.copy(t, 1).start()
        self.copy(t, 2).start()
        for yx in (h.yx_x, h.yx_y, h.yx):
            self.add(self.own.at[t, yx, h.core], self.rc.at[t, yx])

    def stage3(self, k):
        h, t = self.here, self.order[k]
        landed(self.rda.at[t], self.recv(t, 1))
        self.add(self.own.at[t, h.yx_y, h.core, :, self.low], self.rda.at[t])
        self.copy(t, 4).start()
        landed(self.rdb.at[t], self.recv(t, 2))
        self.add(self.own.at[t, h.yx_x, h.core, :, self.high], self.rdb.at[t])
        self.copy(t, 3).start()

    def stage4(self, k):
        h, t = self.here, self.order[k]
        landed(self.rx.at[t], self.recv(t, 3))
        landed(self.ry.at[t], self.recv(t, 4))
        self.add(self.own.at[t, h.yx, h.core], self.rx.at[t], self.ry.at[t])

    def stage5(self, k):
        h, t = self.here, self.order[k]
        mine = self.own.at[t, h.yx, h.core]

        @pl.when(t > h.z)
        def _():
            @pl.when(h.z > 0)
            def _():
                landed(self.rz.at[0, t], self.recv(t, 5))
                self.add(mine, self.rz.at[0, t])

            self.copy(t, 5).start()

        @pl.when(t < h.z)
        def _():
            @pl.when(h.z < h.nz - 1)
            def _():
                landed(self.rz.at[1, t], self.recv(t, 6))
                self.add(mine, self.rz.at[1, t])

            self.copy(t, 6).start()

    def total(self):
        h, z = self.here, self.here.z
        mine = self.own.at[z, h.yx, h.core]

        @pl.when((z > 0) & (z < h.nz - 1))
        def _():
            landed(self.rz.at[0, z], self.recv(z, 5))
            landed(self.rz.at[1, z], self.recv(z, 6))
            self.add(mine, self.rz.at[0, z], self.rz.at[1, z])

        @pl.when(z == 0)
        def _():
            landed(self.rz.at[1, z], self.recv(z, 6))
            self.add(mine, self.rz.at[1, z])

        @pl.when(z == h.nz - 1)
        def _():
            landed(self.rz.at[0, z], self.recv(z, 5))
            self.add(mine, self.rz.at[0, z])

        return [mine[a].astype(F32) for a in range(mine.shape[0])]

    def drain(self):
        h, own = self.here, self.own
        landed(own.at[:, :, 1 - h.core], self.send(0))
        landed(own.at[:, h.yx_d, h.core, :, self.low], self.send(1))
        landed(own.at[:, h.yx_d, h.core, :, self.high], self.send(2))
        landed(own.at[:, h.yx_x, h.core], self.send(3))
        landed(own.at[:, h.yx_y, h.core], self.send(4))
        landed(self.rz.at[0, pl.ds(0, h.nz - 1)], self.send(5))


def scatter_scratch(na, nz, nd, rw, wide):
    return [
        pltpu.VMEM((nz, nd // 2, 2, na, rw, wide), BF),
        pltpu.VMEM((nz, nd // 2, na, rw, wide), BF),
        pltpu.VMEM((nz, na, rw // 2, wide), BF),
        pltpu.VMEM((nz, na, rw // 2, wide), BF),
        pltpu.VMEM((nz, na, rw, wide), BF),
        pltpu.VMEM((nz, na, rw, wide), BF),
        pltpu.VMEM((2, nz, na, rw, wide), BF),
    ]


def every_pair(pairs, work, between):
    def step(p, carry):
        work(p)
        for at, steps in enumerate(between):

            @pl.when(p == at)
            def _():
                for run in steps:
                    run()

        return carry

    lax.fori_loop(0, pairs, step, 0)


def gelu_parts(u):
    cdf = 0.5 + 0.5 * lax.erf(u * 0.7071067811865476)
    return u * cdf, cdf + u * jnp.exp(-0.5 * u * u) * 0.3989422804014327


def norm_rows(v):
    mean = jnp.mean(v, axis=-1, keepdims=True)
    c = v - mean
    inv = lax.rsqrt(jnp.mean(c * c, axis=-1, keepdims=True) + EPS)
    return c * inv, inv


def norm_back(g, normed, inv, gain):
    gn = g * gain
    return inv * (
        gn
        - jnp.mean(gn, axis=-1, keepdims=True)
        - normed * jnp.mean(gn * normed, axis=-1, keepdims=True)
    )


def partner_at(step):
    return (6 - step) % 4


def middle_kernel(comm, row_steps, *refs):
    drop_ref, att_ref, x_ref, cot_ref, crows_ref, wo_ref, up_ref, dn_ref = refs[:8]
    vecs, bin_ref = refs[8:14], refs[14]
    lo_ref, gatt_ref, ghpre_ref, gup_ref, gdn_ref, gwo_ref, vecg_ref, bing_ref = refs[15:23]
    att_s, act_s, gpre_s, slope_s, ht_s, gb2t_s, gbt_s = refs[23:30]
    step = pl.program_id(0)
    parts, d, fl = up_ref.shape[0], att_ref.shape[1], up_ref.shape[3]
    up = lambda t: up_ref[t].reshape(d, fl)
    dn = lambda t: dn_ref[t].reshape(d, fl)
    vec = lambda r: vecs[r][...][None, :]
    if comm:
        cot_s, c3_s, l_s, lsend, lrecv, csend, crecv = refs[30:]
        here = Here(row_steps)
        z = here.z
        layer = Exchange(here, l_s, lo_ref, lsend, lrecv)
        last_cot = lambda: remote(
            crows_ref.at[flip(z, 3)], c3_s, csend.at[0], crecv.at[0], here.dp, flip(z, 3)
        )

    @pl.when(step == 0)
    def _():
        if comm:
            barrier = pltpu.get_barrier_semaphore()
            for k in range(1, row_steps):
                pl.semaphore_signal(
                    barrier, inc=1, device_id=(here.dp, flip(z, k)), device_id_type=pl.DeviceIdType.MESH
                )
            pl.semaphore_wait(barrier, row_steps - 1)
            last_cot().start()
        vecg_ref[...] = jnp.zeros_like(vecg_ref)
        bing_ref[...] = jnp.zeros_like(bing_ref)

    if comm:

        @pl.when(step < row_steps - 1)
        def _():
            cot_s[...] = cot_ref[...]

        @pl.when(step == row_steps - 1)
        def _():
            landed(c3_s, crecv.at[0])
            cot_s[...] = c3_s[...]

    @pl.when(step < row_steps)
    def _():
        at = pl.ds(pl.multiple_of(step * BLK, BLK), BLK)
        dropped = drop_ref[lax.axis_index("tensor")] == 1
        cot = (cot_s if comm else cot_ref)[...].astype(F32)
        att = att_ref[...]
        att_s[at, :] = att
        x = x_ref[...].astype(F32)
        branch = dot_nt(att, wo_ref[...]) + vec(0)
        n1, inv1 = norm_rows(x + branch)
        hidden = n1 * vec(1) + vec(2)
        low = hidden.astype(BF)
        ht_s[:, at] = jnp.transpose(low)
        ffn = hidden + vec(3)
        for t in range(parts):
            pre = dot_nn(low, up(t)) + bin_ref[t * fl : (t + 1) * fl][None, :]
            act, slope = gelu_parts(pre)
            act = act.astype(BF)
            act_s[t, at, :] = act
            slope_s[t] = slope
            ffn = ffn + dot_nt(act, dn(t))
        n2, inv2 = norm_rows(ffn)
        final = n2 * vec(4) + vec(5)
        layer_rows = jnp.where(dropped, x, final).astype(BF)
        if comm:
            l_s[flip(z, partner_at(step))] = layer_rows
        else:
            lo_ref[...] = layer_rows
        g_final = jnp.where(dropped, 0.0, cot)
        g_fpre = norm_back(g_final, n2, inv2, vec(4))
        gb2 = g_fpre.astype(BF)
        gb2t_s[:, at] = jnp.transpose(gb2)
        g_hidden = g_fpre
        for t in range(parts):
            gpre = (dot_nn(gb2, dn(t)) * slope_s[t]).astype(BF)
            gpre_s[t, at, :] = gpre
            bing_ref[:, t * fl : (t + 1) * fl] += jnp.sum(gpre.astype(F32), axis=0, keepdims=True)
            g_hidden = g_hidden + dot_nt(gpre, up(t))
        g_hpre = norm_back(g_hidden, n1, inv1, vec(1))
        gb = g_hpre.astype(BF)
        gbt_s[:, at] = jnp.transpose(gb)
        gatt_ref[...] = dot_nn(gb, wo_ref[...]).astype(BF)
        ghpre_ref[...] = g_hpre + jnp.where(dropped, cot, 0.0)
        for r, v in enumerate(
            (gb.astype(F32), g_hidden * n1, g_hidden, gb2.astype(F32), g_final * n2, g_final)
        ):
            vecg_ref[r : r + 1, :] += jnp.sum(v, axis=0, keepdims=True)

    if comm:
        for k in range(row_steps):

            @pl.when(step == k)
            def _():
                if partner_at(k) == 0:
                    layer.own().start()
                else:
                    layer.copy(partner_at(k)).start()

    @pl.when((step >= row_steps) & (step < row_steps + parts))
    def _():
        t = step - row_steps
        gup_ref[...] = dot_nn(ht_s[...], gpre_s[t]).astype(BF)
        gdn_ref[...] = dot_nn(gb2t_s[...], act_s[t]).astype(BF)

    @pl.when(step == row_steps + parts)
    def _():
        gwo_ref[...] = dot_nn(gbt_s[...], att_s[...]).astype(BF)
        if comm:
            last_cot().wait_send()
            layer.wait_recv()
            layer.wait_send()


def middle(comm, drop, att, x, cot, cot_rows, wo, w, vecs, bias_in):
    length, d = att.shape
    parts, groups, _, group, fl = w.shape
    nr = length // BLK

    def place_of(i):
        return flip(lax.axis_index("tensor"), partner_at(i)) if comm else i

    rows = pl.BlockSpec((BLK, d), lambda i: (place_of(jnp.minimum(i, nr - 1)), 0))
    cot_spec = pl.BlockSpec((BLK, d), lambda i: (place_of(jnp.minimum(i, nr - 1 - comm)), 0))
    any_ = pl.BlockSpec(memory_space=pl.ANY)
    once = lambda shape: pl.BlockSpec(
        shape, lambda i: (0,) * len(shape), pipeline_mode=pl.Buffered(1)
    )
    weight = lambda a: pl.BlockSpec(
        (parts, groups, None, group, fl), lambda i: (0, 0, a, 0, 0), pipeline_mode=pl.Buffered(1)
    )
    part = pl.BlockSpec((None, d, fl), lambda i: (jnp.clip(i - nr, 0, parts - 1), 0, 0))
    whole = lambda shape: pl.BlockSpec(shape, lambda i: (0,) * len(shape))
    dma = pltpu.SemaphoreType.DMA
    comm_scratch = [
        pltpu.VMEM((BLK, d), BF),
        pltpu.VMEM((BLK, d), BF),
        pltpu.VMEM((nr, BLK, d), BF),
        dma((nr,)),
        dma((nr,)),
        dma((1,)),
        dma((1,)),
    ]
    extra = dict(collective_id=2, has_side_effects=True) if comm else {}
    return pl.pallas_call(
        functools.partial(middle_kernel, comm, nr),
        grid=(nr + parts + 1,),
        out_shape=(
            jax.ShapeDtypeStruct((nr, BLK, d) if comm else (length, d), BF),
            jax.ShapeDtypeStruct((length, d), BF),
            jax.ShapeDtypeStruct((length, d), F32),
            jax.ShapeDtypeStruct((parts, d, fl), BF),
            jax.ShapeDtypeStruct((parts, d, fl), BF),
            jax.ShapeDtypeStruct((d, d), BF),
            jax.ShapeDtypeStruct((8, d), F32),
            jax.ShapeDtypeStruct((1, parts * fl), F32),
        ),
        in_specs=[
            pl.BlockSpec(memory_space=pltpu.SMEM),
            rows,
            rows,
            cot_spec,
            any_,
            once((d, d)),
            weight(0),
            weight(1),
            *[once((d,))] * 6,
            once((parts * fl,)),
        ],
        out_specs=(
            any_ if comm else rows, rows, rows, part, part, whole((d, d)), whole((8, d)), whole((1, parts * fl)),
        ),
        scratch_shapes=[
            pltpu.VMEM((length, d), BF),
            pltpu.VMEM((parts, length, fl), BF),
            pltpu.VMEM((parts, length, fl), BF),
            pltpu.VMEM((parts, BLK, fl), F32),
            pltpu.VMEM((d, length), BF),
            pltpu.VMEM((d, length), BF),
            pltpu.VMEM((d, length), BF),
            *(comm_scratch if comm else []),
        ],
        compiler_params=pltpu.CompilerParams(vmem_limit_bytes=VMEM_LIMIT, **extra),
        name="middle",
    )(drop, att, x, cot, cot_rows, wo, w, w, *vecs, bias_in)


def columns(p, start=0):
    return pl.ds(pl.multiple_of(start + p * LANES, LANES), LANES)


def assemble(mix, nz, wqkv_ref, wo_ref):
    d = wo_ref.shape[0]
    wl = d // nz
    for j in range(4):
        whole = jnp.concatenate([mix(t)[:, j * wl : (j + 1) * wl] for t in range(nz)], axis=1)
        if j < 3:
            wqkv_ref[:, j * d : (j + 1) * d] = whole
        else:
            wo_ref[...] = whole


def first_kernel(
    tok_ref, cot_ref, qkvw_ref, wow_ref, upw_ref, dnw_ref, bias_ref, seg_ref,
    x_out, cot_out, wud_out, qkv_out, wqkv_out, xt_out, wo_ref, att_ref, lse_ref, ext_ref,
    sh_ref, mix_s, x_s, qkv_s, wqkv_s, xt_s, kx_s, qx_s, vt_s,
    out_sem, send, recv, line, local, tsend, trecv, csend, crecv,
):
    nz = mix_s.shape[0]
    length, d = att_ref.shape
    pairs = d // LANES
    blk = length // nz
    here = Here(nz)
    mix = Gather(here, mix_s, sh_ref.at[0:1], 0, send, recv, line, local)
    rest = Gather(here, wud_out, sh_ref.at[1:3], 1, send, recv, line, local)
    tokens = Exchange(here, tok_ref, x_s, tsend, trecv)
    cots = Exchange(here, cot_ref, cot_out, csend, crecv, (1, 2))
    sh_ref[0] = jnp.concatenate(
        (qkvw_ref[0], qkvw_ref[1], qkvw_ref[2], jnp.transpose(wow_ref[...])), axis=1
    )
    out_x = pltpu.make_async_copy(x_s, x_out, out_sem.at[0])
    out_qkv = pltpu.make_async_copy(qkv_s, qkv_out, out_sem.at[1])
    out_w = pltpu.make_async_copy(wqkv_s, wqkv_out, out_sem.at[2])
    out_xt = pltpu.make_async_copy(xt_s, xt_out, out_sem.at[3])
    here.greet()
    mix.stage1(0)
    sh_ref[1] = upw_ref[...]
    sh_ref[2] = dnw_ref[...]
    seg = jnp.transpose(jnp.broadcast_to(seg_ref[pl.ds(here.z, 1), :], (LANES, length)))
    doc_lanes(seg, kx_s, qx_s)
    ext_ref[:, :LANES] = kx_s[:, LANES:]
    ext_ref[:, LANES:] = qx_s[:, LANES:]
    vt_s[:, HD:, :] = jnp.ones((2, vt_s.shape[1] - HD, length), BF)
    rest.stage1(0)
    mix.stage1(1)
    mix.stage1(2)
    rest.stage1(1)
    mix.stage1(3)
    tokens.start()
    mix.stage2(0)
    mix.stage2(1)
    mix.stage3(0)
    mix.stage2(2)
    mix.stage3(1)
    mix.stage2(3)
    mix.stage3(2)
    mix.stage3(3)
    rest.stage2(0)
    rest.stage1(2)
    mix.drain()
    assemble(lambda t: mix_s[t].reshape(d, -1), nz, wqkv_s, wo_ref)
    out_w.start()
    bias = jnp.concatenate(
        (bias_ref[0:1, :], jnp.zeros((1, d), F32), bias_ref[1:2, :]), axis=1
    )
    tokens.own().wait()

    def project(k, carry):
        @pl.when(k > 0)
        def _():
            tokens.got(k)

        block = flip(here.z, k)
        at = pl.ds(pl.multiple_of(block * blk, blk), blk)
        qkv_s[at, :] = (dot_nn(x_s[block], wqkv_s[...]) + bias).astype(BF)
        xt_s[:, at] = jnp.transpose(x_s[block])

        @pl.when(k == 0)
        def _():
            rest.stage2(1)
            rest.stage3(0)

        @pl.when(k == 2)
        def _():
            rest.stage1(3)

        return carry

    lax.fori_loop(0, nz, project, 0)
    out_x.start()
    out_qkv.start()
    out_xt.start()
    cots.start()
    between = [
        [lambda: rest.stage2(2), lambda: rest.stage3(1)],
        [lambda: rest.stage2(3), lambda: rest.stage3(2)],
        [lambda: rest.stage3(3)],
    ]

    def work(p):
        o, lse = attend_pair(
            qkv_s[:, columns(p)], qkv_s[:, columns(p, d)], qkv_s[:, columns(p, 2 * d)], kx_s, qx_s, vt_s
        )
        att_ref[:, columns(p)] = o
        lse_ref[p] = lse

    every_pair(pairs, work, between)
    rest.drain()
    tokens.wait_send()
    cots.wait_recv()
    cots.wait_send()
    for copy in (out_x, out_qkv, out_w, out_xt):
        copy.wait()


def first(tokens, cot, qkv_w, wo_w, up_w, dn_w, qv_b, segment_ids):
    nz, nd = lax.axis_size("tensor"), lax.axis_size("dp")
    na, (rw, wide) = 3, up_w.shape
    _, blk, d = tokens.shape
    length = segment_ids.shape[1]
    pairs = d // LANES
    any_ = pl.BlockSpec(memory_space=pl.ANY)
    vmem = pl.BlockSpec(memory_space=pltpu.VMEM)
    dma = pltpu.SemaphoreType.DMA
    s = jax.ShapeDtypeStruct
    unit = lambda count: (nz, nd // 2, 2, count, rw, wide)
    return pl.pallas_call(
        first_kernel,
        out_shape=(
            s(tokens.shape, BF),
            s(tokens.shape, BF),
            s(unit(na - 1), BF),
            s((length, 3 * d), BF),
            s((d, 3 * d), BF),
            s((d, length), BF),
            s((d, d), BF),
            s((length, d), BF),
            s((pairs, 2, length), F32),
            s((length, 2 * LANES), BF),
        ),
        in_specs=[any_, any_] + [vmem] * 6,
        out_specs=(any_,) * 6 + (vmem,) * 4,
        scratch_shapes=[
            pltpu.VMEM((na, rw, wide), BF),
            pltpu.VMEM(unit(1), BF),
            pltpu.VMEM((nz, blk, d), BF),
            pltpu.VMEM((length, 3 * d), BF),
            pltpu.VMEM((d, 3 * d), BF),
            pltpu.VMEM((d, length), BF),
            pltpu.VMEM((length, 2 * LANES), BF),
            pltpu.VMEM((length, 2 * LANES), BF),
            pltpu.VMEM((2, HD + 16, length), BF),
            dma((4,)),
            dma((2, 8)),
            dma((2, nz, 6)),
            dma((2, nz, 2)),
            dma((2,)),
            dma((nz,)),
            dma((nz,)),
            dma((nz,)),
            dma((nz,)),
        ],
        compiler_params=pltpu.CompilerParams(
            collective_id=0, has_side_effects=True, vmem_limit_bytes=VMEM_LIMIT
        ),
        name="first",
    )(tokens, cot, qkv_w, wo_w, up_w, dn_w, qv_b, segment_ids)


def last_kernel(
    gup_ref, gdn_ref, gwo_ref, ghpre_ref, qkv_ref, att_ref, gatt_ref, wqkv_ref, xt_ref,
    lse_ref, ext_ref, vecg_ref, bing_ref,
    grows_ref, gqkv_ref, gout_ref, gup_out, gdn_out, vsum_ref,
    pair_s, g_s, w_s, xt_s, hpre_s, gwo_s, gx_s, kx_s, qx_s, kt_s, delta_s, dk_s, dv_s, vbuf,
    u0, u1, u2, u3, u4, u5, u6, m0, m1, m2, m3, m4, m5, m6,
    psem, hsem, load, uload, send, recv, xsend, xrecv, vsend, vrecv,
):
    nz = u0.shape[0]
    length, d = g_s.shape[1:]
    pairs = d // LANES
    blk = length // nz
    wl = d // nz
    here = Here(nz)
    z = here.z
    ud = Scatter(here, u0, u1, u2, u3, u4, u5, u6, 1, send, recv)
    mx = Scatter(here, m0, m1, m2, m3, m4, m5, m6, 0, send, recv)
    rows = Exchange(here, gx_s, grows_ref, xsend, xrecv)

    def pair_loads(p, slot):
        srcs = (
            qkv_ref.at[:, columns(p)], qkv_ref.at[:, columns(p, d)], qkv_ref.at[:, columns(p, 2 * d)],
            att_ref.at[:, columns(p)], gatt_ref.at[:, columns(p)],
        )
        return [
            pltpu.make_async_copy(src, pair_s.at[slot, j], psem.at[slot, j])
            for j, src in enumerate(srcs)
        ]

    def ud_loads(k):
        t = ud.order[k]
        return [
            pltpu.make_async_copy(
                g.at[t, :, here.core], u0.at[t, :, here.core, a], uload.at[a, t]
            )
            for a, g in enumerate((gup_ref, gdn_ref))
        ]

    def ud_core(k):
        t = ud.order[k]
        for a, g in enumerate((gup_ref, gdn_ref)):
            remote(
                g.at[t, :, 1 - here.core], u1.at[t, :, a], ud.send(0), ud.recv(t, 0), here.dev_c, z
            ).start()

    later = [
        pltpu.make_async_copy(src, dst, load.at[i])
        for i, (src, dst) in enumerate(((wqkv_ref, w_s), (xt_ref, xt_s), (gwo_ref, gwo_s)))
    ]

    def hpre_load(i, slot):
        return pltpu.make_async_copy(ghpre_ref.at[i], hpre_s.at[slot], hsem.at[slot])

    for copy in pair_loads(0, 0):
        copy.start()
    for k in range(nz):
        for copy in ud_loads(k):
            copy.start()
    here.greet()
    for k in range(nz):
        ud_core(k)
    kx_s[:, LANES:] = ext_ref[:, :LANES]
    qx_s[:, LANES:] = ext_ref[:, LANES:]

    def work(p):
        slot = p % 2

        @pl.when(p + 1 < pairs)
        def _():
            for copy in pair_loads(p + 1, 1 - slot):
                copy.start()

        for copy in pair_loads(p, slot):
            copy.wait()
        q, k, v, att, g = [pair_s.at[slot, j] for j in range(5)]

        def put_q(at, value):
            g_s[0, at, columns(p)] = value

        attend_pair_back(q, k, v, att, g, lse_ref[p], kx_s, qx_s, kt_s, delta_s, dk_s, dv_s, put_q)
        g_s[1, :, columns(p)] = dk_s[...].astype(BF)
        g_s[2, :, columns(p)] = dv_s[...].astype(BF)

    def start_later():
        for copy in later:
            copy.start()

    def run(*names):
        return [lambda name=name, k=k: getattr(ud, name)(k) for name, k in names]

    def halves_here():
        for k in range(nz):
            for copy in ud_loads(k):
                copy.wait()

    between = [
        [halves_here] + run(("stage2", 0), ("stage2", 1)),
        run(("stage2", 2), ("stage3", 0), ("stage2", 3)),
        run(("stage3", 1),) + [start_later],
        run(("stage4", 0), ("stage5", 0), ("stage3", 2)),
        run(("stage3", 3), ("stage4", 1), ("stage5", 1)),
    ]
    every_pair(pairs, work, between)

    place_of = [flip(z, k) for k in (2, 3, 1, 0)]
    hpre_load(place_of[0], 0).start()
    for copy in later:
        copy.wait()
    for i, to in enumerate(place_of):
        if i + 1 < nz:
            hpre_load(place_of[i + 1], (i + 1) % 2).start()
        hpre_load(to, i % 2).wait()
        at = pl.ds(pl.multiple_of(to * blk, blk), blk)
        total = hpre_s[i % 2]
        for j in range(3):
            total = total + dot_nt(g_s[j, at, :], w_s[:, j * d : (j + 1) * d])
        gx_s[to] = total.astype(BF)
        if i + 1 < nz:
            rows.copy((2, 3, 1)[i]).start()
        else:
            rows.own().start()

    ud.stage4(2)
    ud.stage5(2)

    vsum_ref[...] = jnp.zeros_like(vsum_ref)
    vsum_ref[0:8, :] = vecg_ref[...]
    for i in range(bing_ref.shape[1] // d):
        vsum_ref[8 + i : 9 + i, :] = bing_ref[:, i * d : (i + 1) * d]
    xt = xt_s[...]
    for j in range(3):
        grad = dot_nn(xt, g_s[j]).astype(BF)
        for t in range(nz):
            part = grad[:, t * wl : (t + 1) * wl]
            m0[t, :, :, 0, :, j * wl : (j + 1) * wl] = part.reshape(m0.shape[1:3] + (m0.shape[4], wl))
        if j != 1:
            sums = jnp.sum(g_s[j].astype(F32), axis=0, keepdims=True)
            r = vsum_ref.shape[0] - 2 + j // 2
            vsum_ref[r : r + 1, :] = sums
    for t in range(nz):
        part = gwo_s[:, t * wl : (t + 1) * wl]
        m0[t, :, :, 0, :, 3 * wl :] = part.reshape(m0.shape[1:3] + (m0.shape[4], wl))

    partners = [(here.dev_c, z), (here.dev_x, z), (here.dev_y, z)]
    partners += [(here.dp, z + 1 - 2 * (z % 2)), (here.dp, (z + 2) % nz)]

    def vec_copy(k):
        return remote(vbuf.at[0, k], vbuf.at[1, k], vsend.at[k], vrecv.at[k], *partners[k])

    def vec_start(k):
        vbuf[0, k] = vsum_ref[...]
        vec_copy(k).start()

    def vec_finish(k):
        landed(vbuf.at[1, k], vrecv.at[k])
        vsum_ref[...] += vbuf[1, k]

    for k in range(nz):
        mx.stage1(k)
    vec_start(0)
    for k in range(nz + 3):
        if k < nz:
            mx.stage2(k)
        if 1 <= k <= nz:
            mx.stage3(k - 1)
        if k < len(partners):
            vec_finish(k)
            if k + 1 < len(partners):
                vec_start(k + 1)
        if 2 <= k <= nz + 1:
            mx.stage4(k - 2)
        if 3 <= k <= nz + 1:
            mx.stage5(k - 3)
    ud.stage4(3)
    up_sum, dn_sum = ud.total()
    gup_out[...] = up_sum
    gdn_out[...] = dn_sum
    (mix_sum,) = mx.total()
    for j in range(3):
        gqkv_ref[j] = mix_sum[:, j * wl : (j + 1) * wl]
    gout_ref[...] = jnp.transpose(mix_sum[:, 3 * wl :])
    ud.drain()
    mx.drain()
    for k in range(len(partners)):
        vec_copy(k).wait_send()
    rows.wait_recv()
    rows.wait_send()


def last(gup, gdn, gwo, ghpre, qkv, att, gatt, wqkv, xt, lse, ext, vecg, bing):
    nz, nd = lax.axis_size("tensor"), lax.axis_size("dp")
    length, d = att.shape
    rw, wide, wl = d // nd, gup.shape[2], d // nz
    blk = length // nz
    unit = (nz, nd // 2, 2, rw, wide)
    any_ = pl.BlockSpec(memory_space=pl.ANY)
    vmem = pl.BlockSpec(memory_space=pltpu.VMEM)
    dma = pltpu.SemaphoreType.DMA
    s = jax.ShapeDtypeStruct
    steps = 5
    vec_shape = (16, d)
    return pl.pallas_call(
        last_kernel,
        out_shape=(
            s((nz, blk, d), BF),
            s((3, rw, wl), F32),
            s((wl, rw), F32),
            s((rw, wide), F32),
            s((rw, wide), F32),
            s(vec_shape, F32),
        ),
        in_specs=[any_] * 9 + [vmem] * 4,
        out_specs=(any_,) + (vmem,) * 5,
        scratch_shapes=[
            pltpu.VMEM((2, 5, length, LANES), BF),
            pltpu.VMEM((3, length, d), BF),
            pltpu.VMEM((d, 3 * d), BF),
            pltpu.VMEM((d, length), BF),
            pltpu.VMEM((2, blk, d), F32),
            pltpu.VMEM((d, d), BF),
            pltpu.VMEM((nz, blk, d), BF),
            pltpu.VMEM((length, 2 * LANES), BF),
            pltpu.VMEM((length, 2 * LANES), BF),
            pltpu.VMEM((LANES, length), BF),
            pltpu.VMEM((8, length), F32),
            pltpu.VMEM((length, LANES), F32),
            pltpu.VMEM((length, LANES), F32),
            pltpu.VMEM((2, steps) + vec_shape, F32),
        ]
        + scatter_scratch(2, nz, nd, rw, wide)
        + scatter_scratch(1, nz, nd, rw, wide)
        + [
            dma((2, 5)),
            dma((2,)),
            dma((3,)),
            dma((2, nz)),
            dma((2, 6)),
            dma((2, nz, 7)),
            dma((nz,)),
            dma((nz,)),
            dma((steps,)),
            dma((steps,)),
        ],
        compiler_params=pltpu.CompilerParams(
            collective_id=1, has_side_effects=True, vmem_limit_bytes=LAST_LIMIT
        ),
        name="last",
    )(
        gup.reshape(unit), gdn.reshape(unit), gwo, ghpre.reshape(nz, blk, d),
        qkv, att, gatt, wqkv, xt, lse, ext, vecg, bing,
    )


LAST_LIMIT = 61 * 1024 * 1024


def finish_kernel(lrows, grows, gqkv, gout, gup, gdn, sums, *outs):
    (
        layer_out, grad_tokens, o_qkv, o_qvb, o_out, o_outb, o_gain1, o_shift1,
        o_up, o_upb, o_dn, o_dnb, o_gain2, o_shift2,
    ) = outs
    layer_out[...] = lrows[...]
    grad_tokens[...] = grows[...].astype(F32)

    @pl.when(pl.program_id(0) == 0)
    def _():
        d = sums.shape[1]
        for dst, src in ((o_qkv, gqkv), (o_out, gout), (o_up, gup), (o_dn, gdn)):
            dst[...] = src[...]
        for r, dst in enumerate((o_outb, o_gain1, o_shift1, o_dnb, o_gain2, o_shift2)):
            dst[...] = sums[r, :]
        for r in range(o_upb.shape[0] // d):
            o_upb[r * d : (r + 1) * d] = sums[8 + r, :]
        o_qvb[...] = sums[sums.shape[0] - 2 :, :]


def finish(lrows, grows, gqkv, gout, gup, gdn, sums, hidden):
    nz, blk, d = lrows.shape
    rows = pl.BlockSpec((1, blk, d), lambda i: (i, 0, 0))
    s = jax.ShapeDtypeStruct
    same = lambda a: s(a.shape, a.dtype)
    vector = s((d,), F32)
    outs = (
        same(lrows), s(grows.shape, F32), same(gqkv), s((2, d), F32), same(gout), vector, vector, vector,
        same(gup), s((hidden,), F32), same(gdn), vector, vector, vector,
    )
    whole = lambda a: pl.BlockSpec(a.shape, lambda i: (0,) * len(a.shape))
    return pl.pallas_call(
        finish_kernel,
        grid=(nz,),
        out_shape=outs,
        in_specs=[rows, rows] + [whole(a) for a in (gqkv, gout, gup, gdn, sums)],
        out_specs=[rows, rows] + [whole(a) for a in outs[2:]],
        compiler_params=pltpu.CompilerParams(vmem_limit_bytes=VMEM_LIMIT),
        name="finish",
    )(lrows, grows, gqkv, gout, gup, gdn, sums)


def plain_attend_kernel(q_ref, k_ref, v_ref, segc_ref, o_ref, lse_ref, kx_s, qx_s, vt_s):
    doc_lanes(segc_ref[...], kx_s, qx_s)
    vt_s[:, HD:, :] = jnp.ones((2, vt_s.shape[1] - HD, vt_s.shape[2]), BF)
    o_ref[...], lse_ref[...] = attend_pair(q_ref[...], k_ref[...], v_ref[...], kx_s, qx_s, vt_s)


def plain_attend_back_kernel(
    q_ref, k_ref, v_ref, att_ref, g_ref, lse_ref, segc_ref, gq_ref, gk_ref, gv_ref,
    kx_s, qx_s, kt_s, delta_s, dk_s, dv_s,
):
    doc_lanes(segc_ref[...], kx_s, qx_s)

    def put_q(at, value):
        gq_ref[at, :] = value

    attend_pair_back(
        q_ref, k_ref, v_ref, att_ref, g_ref, lse_ref[...], kx_s, qx_s, kt_s, delta_s, dk_s, dv_s, put_q
    )
    gk_ref[...] = dk_s[...].astype(BF)
    gv_ref[...] = dv_s[...].astype(BF)


def plain_specs(length, d):
    col = lambda off: pl.BlockSpec((length, LANES), lambda p: (0, off + p))
    seg = pl.BlockSpec((length, LANES), lambda p: (0, 0))
    lse = pl.BlockSpec((None, 2, length), lambda p: (p, 0, 0))
    wide = pltpu.VMEM((length, 2 * LANES), BF)
    return d // LANES, col, seg, lse, wide


def plain_first(tokens, cot, qkv_w, wo_w, up_w, dn_w, qv_b, segment_ids):
    axes = ("tensor", "dp")
    nz = lax.axis_size("tensor")
    length, d = segment_ids.shape[1], tokens.shape[2]
    pairs, col, seg, lse_spec, wide = plain_specs(length, d)
    mix = jnp.concatenate((qkv_w[0], qkv_w[1], qkv_w[2], wo_w.T), axis=1)
    shards = jnp.stack((mix, up_w, dn_w))
    ids = lax.dynamic_index_in_dim(segment_ids, lax.axis_index("tensor"), 0, keepdims=False)
    segc = jnp.broadcast_to(ids[:, None], (length, LANES))
    bias = jnp.concatenate((qv_b[0], jnp.zeros((d,), F32), qv_b[1]))
    x = lax.all_to_all(tokens, "tensor", 0, 0)
    cot = lax.all_to_all(cot, "tensor", 0, 0)
    w = lax.all_gather(shards, axes, axis=1, tiled=True).reshape(3, nz, d, shards.shape[2])
    parts = w[0].reshape(nz, d, 4, d // nz).transpose(1, 2, 0, 3).reshape(d, 4 * d)
    wqkv, wo = parts[:, : 3 * d], parts[:, 3 * d :]
    rows = x.reshape(length, d)
    qkv = (dot_nn(rows, wqkv) + bias).astype(BF)
    att, lse = pl.pallas_call(
        plain_attend_kernel,
        grid=(pairs,),
        out_shape=(
            jax.ShapeDtypeStruct((length, d), BF),
            jax.ShapeDtypeStruct((pairs, 2, length), F32),
        ),
        in_specs=[col(0), col(pairs), col(2 * pairs), seg],
        out_specs=(col(0), lse_spec),
        scratch_shapes=[wide, wide, pltpu.VMEM((2, HD + 16, length), BF)],
        compiler_params=pltpu.CompilerParams(vmem_limit_bytes=VMEM_LIMIT),
        name="plain_attend",
    )(qkv, qkv, qkv, segc)
    wud = w[1:].reshape(2, nz, 8, d // 8, -1).transpose(1, 2, 0, 3, 4)
    return x, cot, wud, qkv, wqkv, rows.T, wo, att, lse, segc


def plain_last(gup, gdn, gwo, ghpre, qkv, att, gatt, wqkv, xt, lse, segc, vecg, bing):
    axes = ("tensor", "dp")
    nz = lax.axis_size("tensor")
    length, d = att.shape
    pairs, col, seg, lse_spec, wide = plain_specs(length, d)
    f32_wide = pltpu.VMEM((length, LANES), F32)
    grads = pl.pallas_call(
        plain_attend_back_kernel,
        grid=(pairs,),
        out_shape=[jax.ShapeDtypeStruct((length, d), BF)] * 3,
        in_specs=[col(0), col(pairs), col(2 * pairs), col(0), col(0), lse_spec, seg],
        out_specs=[col(0)] * 3,
        scratch_shapes=[
            wide, wide, pltpu.VMEM((LANES, length), BF), pltpu.VMEM((8, length), F32), f32_wide, f32_wide,
        ],
        compiler_params=pltpu.CompilerParams(vmem_limit_bytes=VMEM_LIMIT),
        name="plain_attend_back",
    )(qkv, qkv, qkv, att, gatt, lse, segc)
    g = jnp.concatenate(grads, axis=1)
    gx = (ghpre + dot_nt(g, wqkv)).astype(BF)
    gmix = jnp.concatenate((dot_nn(xt, g).astype(BF), gwo), axis=1)
    gmix = gmix.reshape(d, 4, nz, d // nz).transpose(2, 0, 1, 3).reshape(nz, d, -1)
    split = lambda a: a.reshape(nz, length // nz, d)
    parts = [
        lax.psum_scatter(p.reshape(nz * d, -1), axes, scatter_dimension=0, tiled=True)
        for p in (gmix, gup, gdn)
    ]
    mix_sum, up_sum, dn_sum = [p.astype(F32) for p in parts]
    wl = d // nz
    sums = [jnp.sum(grads[j].astype(F32), axis=0, keepdims=True) for j in (0, 2)]
    bing = bing.reshape(-1, d)
    gap = jnp.zeros((6 - bing.shape[0], d), F32)
    vec = jnp.concatenate((vecg, bing, gap, *sums), axis=0)
    return (
        lax.all_to_all(split(gx), "tensor", 0, 0),
        jnp.stack([mix_sum[:, j * wl : (j + 1) * wl] for j in range(3)]),
        mix_sum[:, 3 * wl :].T,
        up_sum,
        dn_sum,
        lax.psum(vec, axes),
    )


def on_device(
    tokens, segment_ids, drop_flags, qkv_w, qv_b, wo_w, wo_b, gain1, shift1,
    up_w, up_b, dn_w, dn_b, gain2, shift2, cotangent,
):
    nt, nd = lax.axis_size("tensor"), lax.axis_size("dp")
    d = tokens.shape[2]
    length = segment_ids.shape[1]
    wl = qkv_w.shape[2]
    fl = up_w.shape[1]
    comm = (nt, nd) == (4, 8)
    begin, end = (first, last) if comm else (plain_first, plain_last)
    x, cot, wud, qkv, wqkv, xt, wo, att, lse, ext = begin(
        tokens, cotangent, qkv_w, wo_w, up_w, dn_w.T, qv_b, segment_ids
    )
    vecs = (wo_b, gain1, shift1, dn_b, gain2, shift2)
    layer_out, g_att, g_hpre, gup, gdn, gwo, vecg, bing = middle(
        comm, drop_flags, att, x.reshape(length, d), cot.reshape(length, d), cotangent, wo,
        wud.reshape(nt, -1, 2, *wud.shape[-2:]), vecs, up_b,
    )
    if not comm:
        layer_out = lax.all_to_all(layer_out.reshape(nt, length // nt, d), "tensor", 0, 0)
    rows, g_qkv, g_out, g_up, g_dn, total = end(
        gup, gdn, gwo, g_hpre, qkv, att, g_att, wqkv, xt, lse, ext, vecg, bing
    )
    outs = finish(layer_out, rows, g_qkv, g_out, g_up, g_dn, total, nt * fl)
    return (*outs[:10], outs[10].T, *outs[11:])


def solution(mesh):
    rows = P("dp", "tensor", None)
    return jax.shard_map(
        on_device,
        mesh=mesh,
        in_specs=(
            rows, P("dp", None), P("dp"), P(None, "dp", "tensor"), P(), P("tensor", "dp"), P(), P(), P(),
            P("dp", "tensor"), P(), P("tensor", "dp"), P(), P(), P(), rows,
        ),
        out_specs=(
            rows, rows, P(None, "dp", "tensor"), P(), P("tensor", "dp"), P(), P(), P(),
            P("dp", "tensor"), P(), P("tensor", "dp"), P(), P(), P(),
        ),
        check_vma=False,
    )
```

```python
import functools
import jax
import jax.numpy as jnp
from jax import lax
from jax.experimental import pallas as pl
from jax.experimental.pallas import tpu as pltpu
from jax.sharding import PartitionSpec as P

HD = 64
EPS = 1e-05
NEG = -1000000000.0
BF = jnp.bfloat16
F32 = jnp.float32
VMEM_LIMIT = 60 * 1024 * 1024
BLK = 256
LANES = 128


def dot_nn(a, b):
    return jnp.dot(a, b, preferred_element_type=F32)


def dot_nt(a, b):
    return lax.dot_general(a, b, (((1,), (1,)), ((), ())), preferred_element_type=F32)


def dot_tn(a, b):
    return lax.dot_general(a, b, (((0,), (0,)), ((), ())), preferred_element_type=F32)


def doc_lanes(seg, kx_s, qx_s):
    lane = lax.broadcasted_iota(jnp.int32, seg.shape, 1)
    same = (seg == lane).astype(F32)
    kx_s[:, LANES:] = same.astype(BF)
    qx_s[:, LANES:] = ((1.0 - same) * NEG).astype(BF)


def split_heads(pair):
    first = lax.broadcasted_iota(jnp.int32, pair.shape, 1) % (2 * HD) < HD
    zero = jnp.zeros((), pair.dtype)
    return jnp.where(first, pair, zero), jnp.where(first, zero, pair)


def attend_pair(q, k, v, kx_s, qx_s, vt_s):
    kx_s[:, :LANES] = k
    qx_s[:, :LANES] = (q.astype(F32) * 0.125).astype(BF)
    vt = jnp.transpose(v)
    vt_s[0, :HD, :] = vt[:HD, :]
    vt_s[1, :HD, :] = vt[HD:, :]
    kx = kx_s[...]
    ext = qx_s[:, LANES:]
    outs, lses = [], []
    scores = [
        dot_nt(kx, jnp.concatenate((h, ext), axis=1)) for h in split_heads(qx_s[:, :LANES])
    ]
    for h in range(2):
        top = jnp.max(scores[h], axis=0, keepdims=True)
        p = jnp.exp(scores[h] - top).astype(BF)
        o = dot_nn(vt_s[h], p)
        total = o[HD : HD + 1, :]
        outs.append(o[:HD, :] / total)
        lses.append(top + jnp.log(total))
    return jnp.transpose(jnp.concatenate(outs, axis=0)).astype(BF), jnp.concatenate(lses, axis=0)


def attend_pair_back(q_ref, k_ref, v_ref, att_ref, g_ref, lse, kx_s, qx_s, kt_s, delta_s, dk_s, dv_s, put_q):
    length = q_ref.shape[0]
    kx_s[:, :LANES] = k_ref[...]
    qx_s[:, :LANES] = (q_ref[...].astype(F32) * 0.125).astype(BF)
    kt_s[...] = jnp.transpose(k_ref[...])
    sub = lax.broadcasted_iota(jnp.int32, (8, LANES), 0)
    lane = lax.broadcasted_iota(jnp.int32, (8, LANES), 1)
    pick = jnp.where(lane // HD == sub, 1.0, 0.0).astype(BF)
    prod = g_ref[...].astype(F32) * att_ref[...].astype(F32)
    upper = prod.astype(BF)
    lower = (prod - upper.astype(F32)).astype(BF)
    delta_s[...] = dot_nt(pick, upper) + dot_nt(pick, lower)
    for i in range(length // QB):
        at = slice(i * QB, (i + 1) * QB)
        kx = kx_s[...]
        v = v_ref[...]
        ext = qx_s[at, LANES:]
        qs = split_heads(qx_s[at, :LANES])
        gs = split_heads(g_ref[at, :])
        ps, ds, dq = [], [], []
        for h in range(2):
            s = dot_nt(kx, jnp.concatenate((qs[h], ext), axis=1))
            p = jnp.exp(s - lse[h : h + 1, at])
            dp = dot_nt(v, gs[h])
            d = (p * (dp - delta_s[h : h + 1, at])).astype(BF)
            ps.append(p.astype(BF))
            ds.append(d)
            dq.append(dot_nn(kt_s[h * HD : (h + 1) * HD, :], d))
        dv = dot_nn(jnp.concatenate(ps, axis=1), jnp.concatenate(gs, axis=0))
        dk = dot_nn(jnp.concatenate(ds, axis=1), jnp.concatenate(qs, axis=0))
        dv_s[...] = dv if i == 0 else dv_s[...] + dv
        dk_s[...] = dk if i == 0 else dk_s[...] + dk
        put_q(at, (jnp.transpose(jnp.concatenate(dq, axis=0)) * 0.125).astype(BF))


QB = 512


def place(dp):
    yx, core = dp // 2, dp % 2
    y, x = yx // 2, yx % 2
    return yx, core, y * 2 + 1 - x, (1 - y) * 2 + x, 3 - yx


def remote(src, dst, send, recv, dp, z):
    return pltpu.make_async_remote_copy(
        src_ref=src,
        dst_ref=dst,
        send_sem=send,
        recv_sem=recv,
        device_id=(dp, z),
        device_id_type=pl.DeviceIdType.MESH,
    )


def greet(dp, z, yx, core, yx_x, yx_y, nz):
    barrier = pltpu.get_barrier_semaphore()
    others = [(yx_x * 2 + core, z), (yx_y * 2 + core, z), (yx * 2 + 1 - core, z)]
    others += [(dp, (z + k) % nz) for k in range(1, nz)]
    for dev in others:
        pl.semaphore_signal(
            barrier, inc=1, device_id=dev, device_id_type=pl.DeviceIdType.MESH
        )
    pl.semaphore_wait(barrier, len(others))


def landed(ref, sem):
    pltpu.make_async_copy(ref, ref, sem).wait()


class Here:
    def __init__(self, nz):
        self.nz = nz
        self.dp, self.z = lax.axis_index("dp"), lax.axis_index("tensor")
        self.yx, self.core, self.yx_x, self.yx_y, self.yx_d = place(self.dp)
        self.dev_x = self.yx_x * 2 + self.core
        self.dev_y = self.yx_y * 2 + self.core
        self.dev_c = self.yx * 2 + 1 - self.core

    def greet(self):
        greet(self.dp, self.z, self.yx, self.core, self.yx_x, self.yx_y, self.nz)

    def sides(self, s, body):
        if s == 0:
            body(self.z, None)
            return

        @pl.when(self.z >= s)
        def _():
            body(self.z - s, True)

        @pl.when(self.z + s < self.nz)
        def _():
            body(self.z + s, False)


def flip(z, i):
    return (z % 2 + i % 2) % 2 + 2 * ((z // 2 + i // 2) % 2)


class Exchange:
    def __init__(self, here, src, dst, send, recv, ks=(1, 2, 3)):
        self.here, self.src, self.dst, self.send, self.recv, self.ks = here, src, dst, send, recv, ks

    def copy(self, k):
        h = self.here
        to = flip(h.z, k)
        return remote(
            self.src.at[to], self.dst.at[h.z], self.send.at[k], self.recv.at[k], h.dp, to
        )

    def own(self):
        z = self.here.z
        return pltpu.make_async_copy(self.src.at[z], self.dst.at[z], self.send.at[0])

    def start(self):
        for k in self.ks:
            self.copy(k).start()
        self.own().start()

    def got(self, k):
        landed(self.dst.at[flip(self.here.z, k)], self.recv.at[k])

    def wait_recv(self):
        self.own().wait()
        for k in self.ks:
            self.got(k)

    def wait_send(self):
        for k in self.ks:
            self.copy(k).wait_send()


class Gather:
    def __init__(self, here, w_ref, sh_ref, group, send, recv, line, local):
        self.here, self.w, self.sh = here, w_ref, sh_ref
        self.send = lambda kind: send.at[group, kind]
        self.recv = lambda t, kind: recv.at[group, t, kind]
        self.line = lambda t, kind: line.at[group, t, kind]
        self.all_cores = recv.at[group, 0, 5]
        self.local = local.at[group]
        half = w_ref.shape[4] // 2
        self.low, self.high = pl.ds(0, half), pl.ds(half, half)

    def blk(self, t, yx):
        return self.w.at[t, yx, self.here.core]

    def to_plane(self, t, own, kind):
        h = self.here
        dst = self.blk(t, h.yx)
        dev = (h.dev_x, h.dev_y, h.dev_c)[kind]
        arrived = self.all_cores if kind == 2 else self.recv(t, kind)
        return remote(self.sh if own else dst, dst, self.send(kind), arrived, dev, h.z)

    def to_line(self, t, own, kind):
        h = self.here
        dst = self.blk(t, h.yx)
        to = (h.z + 1) % h.nz if kind == 0 else (h.z + h.nz - 1) % h.nz
        return remote(self.sh if own else dst, dst, self.line(t, kind), self.recv(t, 4), h.dp, to)

    def own_copy(self):
        return pltpu.make_async_copy(self.sh, self.blk(self.here.z, self.here.yx), self.local)

    def half_y(self, t):
        b = self.w.at[t, self.here.yx_x, self.here.core, :, self.low]
        return remote(b, b, self.send(3), self.recv(t, 2), self.here.dev_y, self.here.z)

    def half_x(self, t):
        b = self.w.at[t, self.here.yx_y, self.here.core, :, self.high]
        return remote(b, b, self.send(4), self.recv(t, 3), self.here.dev_x, self.here.z)

    def to_core(self, t, yx, kind):
        b = self.blk(t, yx)
        return remote(b, b, self.send(kind), self.all_cores, self.here.dev_c, self.here.z)

    def along(self, s, from_left, right, left):
        h = self.here
        if s == 0 or from_left:
            pl.when(h.z < h.nz - 1)(right)
        if s == 0 or not from_left:
            pl.when(h.z > 0)(left)

    def stage1(self, s):
        own = s == 0

        def body(t, from_left):
            if own:
                self.own_copy().start()
            else:
                landed(self.blk(t, self.here.yx), self.recv(t, 4))
            self.along(
                s, from_left,
                lambda: self.to_line(t, own, 0).start(), lambda: self.to_line(t, own, 1).start(),
            )
            for kind in range(3):
                self.to_plane(t, own, kind).start()

        self.here.sides(s, body)

    def stage2(self, s):
        h = self.here

        def body(t, from_left):
            landed(self.blk(t, h.yx_x), self.recv(t, 0))
            self.half_y(t).start()
            self.to_core(t, h.yx_x, 5).start()
            landed(self.blk(t, h.yx_y), self.recv(t, 1))
            self.half_x(t).start()
            self.to_core(t, h.yx_y, 6).start()

        h.sides(s, body)

    def stage3(self, s):
        h = self.here

        def body(t, from_left):
            landed(self.w.at[t, h.yx_d, h.core, :, self.low], self.recv(t, 2))
            landed(self.w.at[t, h.yx_d, h.core, :, self.high], self.recv(t, 3))
            self.to_core(t, h.yx_d, 7).start()

        h.sides(s, body)

    def drain(self):
        h, w = self.here, self.w
        landed(w.at[:, :, 1 - h.core], self.all_cores)
        self.own_copy().wait()
        for kind in (0, 1, 2, 5, 6, 7):
            landed(w.at[:, h.yx, h.core], self.send(kind))
        landed(w.at[:, h.yx_x, h.core, :, self.low], self.send(3))
        landed(w.at[:, h.yx_y, h.core, :, self.high], self.send(4))
        for s in range(h.nz):

            def body(t, from_left):
                self.along(
                    s, from_left,
                    lambda: self.to_line(t, s == 0, 0).wait_send(),
                    lambda: self.to_line(t, s == 0, 1).wait_send(),
                )

            h.sides(s, body)


class Scatter:
    def __init__(self, here, own, rc, rda, rdb, rx, ry, rz, group, send, recv, order=None):
        self.here, self.own = here, own
        self.rc, self.rda, self.rdb, self.rx, self.ry, self.rz = rc, rda, rdb, rx, ry, rz
        self.send = lambda kind: send.at[group, kind]
        self.recv = lambda t, kind: recv.at[group, t, kind]
        half = own.shape[4] // 2
        self.low, self.high = pl.ds(0, half), pl.ds(half, half)
        z = here.z
        self.order = order or [3 * (1 - z // 2), (2 + 3 * z) % 5, 1 + z % 2, z]

    def copy(self, t, kind):
        h, own = self.here, self.own
        src, dst, dev, z = (
            lambda: (own.at[t, :, 1 - h.core], self.rc.at[t], h.dev_c, h.z),
            lambda: (own.at[t, h.yx_d, h.core, :, self.low], self.rda.at[t], h.dev_x, h.z),
            lambda: (own.at[t, h.yx_d, h.core, :, self.high], self.rdb.at[t], h.dev_y, h.z),
            lambda: (own.at[t, h.yx_x, h.core], self.rx.at[t], h.dev_x, h.z),
            lambda: (own.at[t, h.yx_y, h.core], self.ry.at[t], h.dev_y, h.z),
            lambda: (own.at[t, h.yx, h.core], self.rz.at[0, t], h.dp, (h.z + 1) % h.nz),
            lambda: (own.at[t, h.yx, h.core], self.rz.at[1, t], h.dp, (h.z + h.nz - 1) % h.nz),
        )[kind]()
        return remote(src, dst, self.send(min(kind, 5)), self.recv(t, kind), dev, z)

    def add(self, dst, *srcs):
        total = dst[...].astype(F32)
        for src in srcs:
            total = total + src[...].astype(F32)
        dst[...] = total.astype(BF)

    def stage1(self, k):
        self.copy(self.order[k], 0).start()

    def stage2(self, k):
        h, t = self.here, self.order[k]
        landed(self.rc.at[t], self.recv(t, 0))
        self.add(self.own.at[t, h.yx_d, h.core], self.rc.at[t, h.yx_d])
        self.copy(t, 1).start()
        self.copy(t, 2).start()
        for yx in (h.yx_x, h.yx_y, h.yx):
            self.add(self.own.at[t, yx, h.core], self.rc.at[t, yx])

    def stage3(self, k):
        h, t = self.here, self.order[k]
        landed(self.rda.at[t], self.recv(t, 1))
        self.add(self.own.at[t, h.yx_y, h.core, :, self.low], self.rda.at[t])
        self.copy(t, 4).start()
        landed(self.rdb.at[t], self.recv(t, 2))
        self.add(self.own.at[t, h.yx_x, h.core, :, self.high], self.rdb.at[t])
        self.copy(t, 3).start()

    def stage4(self, k):
        h, t = self.here, self.order[k]
        landed(self.rx.at[t], self.recv(t, 3))
        landed(self.ry.at[t], self.recv(t, 4))
        self.add(self.own.at[t, h.yx, h.core], self.rx.at[t], self.ry.at[t])

    def stage5(self, k):
        h, t = self.here, self.order[k]
        mine = self.own.at[t, h.yx, h.core]

        @pl.when(t > h.z)
        def _():
            @pl.when(h.z > 0)
            def _():
                landed(self.rz.at[0, t], self.recv(t, 5))
                self.add(mine, self.rz.at[0, t])

            self.copy(t, 5).start()

        @pl.when(t < h.z)
        def _():
            @pl.when(h.z < h.nz - 1)
            def _():
                landed(self.rz.at[1, t], self.recv(t, 6))
                self.add(mine, self.rz.at[1, t])

            self.copy(t, 6).start()

    def total(self):
        h, z = self.here, self.here.z
        mine = self.own.at[z, h.yx, h.core]

        @pl.when((z > 0) & (z < h.nz - 1))
        def _():
            landed(self.rz.at[0, z], self.recv(z, 5))
            landed(self.rz.at[1, z], self.recv(z, 6))
            self.add(mine, self.rz.at[0, z], self.rz.at[1, z])

        @pl.when(z == 0)
        def _():
            landed(self.rz.at[1, z], self.recv(z, 6))
            self.add(mine, self.rz.at[1, z])

        @pl.when(z == h.nz - 1)
        def _():
            landed(self.rz.at[0, z], self.recv(z, 5))
            self.add(mine, self.rz.at[0, z])

        return [mine[a].astype(F32) for a in range(mine.shape[0])]

    def drain(self):
        h, own = self.here, self.own
        landed(own.at[:, :, 1 - h.core], self.send(0))
        landed(own.at[:, h.yx_d, h.core, :, self.low], self.send(1))
        landed(own.at[:, h.yx_d, h.core, :, self.high], self.send(2))
        landed(own.at[:, h.yx_x, h.core], self.send(3))
        landed(own.at[:, h.yx_y, h.core], self.send(4))
        landed(self.rz.at[0, pl.ds(0, h.nz - 1)], self.send(5))


def scatter_scratch(na, nz, nd, rw, wide):
    return [
        pltpu.VMEM((nz, nd // 2, 2, na, rw, wide), BF),
        pltpu.VMEM((nz, nd // 2, na, rw, wide), BF),
        pltpu.VMEM((nz, na, rw // 2, wide), BF),
        pltpu.VMEM((nz, na, rw // 2, wide), BF),
        pltpu.VMEM((nz, na, rw, wide), BF),
        pltpu.VMEM((nz, na, rw, wide), BF),
        pltpu.VMEM((2, nz, na, rw, wide), BF),
    ]


def every_pair(pairs, work, between):
    def step(p, carry):
        work(p)
        for at, steps in enumerate(between):

            @pl.when(p == at)
            def _():
                for run in steps:
                    run()

        return carry

    lax.fori_loop(0, pairs, step, 0)


def gelu_parts(u):
    cdf = 0.5 + 0.5 * lax.erf(u * 0.7071067811865476)
    return u * cdf, cdf + u * jnp.exp(-0.5 * u * u) * 0.3989422804014327


def norm_rows(v):
    mean = jnp.mean(v, axis=-1, keepdims=True)
    c = v - mean
    inv = lax.rsqrt(jnp.mean(c * c, axis=-1, keepdims=True) + EPS)
    return c * inv, inv


def norm_back(g, normed, inv, gain):
    gn = g * gain
    return inv * (
        gn
        - jnp.mean(gn, axis=-1, keepdims=True)
        - normed * jnp.mean(gn * normed, axis=-1, keepdims=True)
    )


def partner_at(step):
    return (6 - step) % 4


def middle_kernel(comm, row_steps, *refs):
    drop_ref, att_ref, x_ref, cot_ref, crows_ref, wo_ref, up_ref, dn_ref = refs[:8]
    vecs, bin_ref = refs[8:14], refs[14]
    lo_ref, gatt_ref, ghpre_ref, gup_ref, gdn_ref, gwo_ref, vecg_ref, bing_ref = refs[15:23]
    att_s, act_s, gpre_s, slope_s, ht_s, gb2t_s, gbt_s = refs[23:30]
    step = pl.program_id(0)
    parts, d, fl = up_ref.shape[0], att_ref.shape[1], up_ref.shape[3]
    up = lambda t: up_ref[t].reshape(d, fl)
    dn = lambda t: dn_ref[t].reshape(d, fl)
    vec = lambda r: vecs[r][...][None, :]
    if comm:
        cot_s, c3_s, l_s, lsend, lrecv, csend, crecv = refs[30:]
        here = Here(row_steps)
        z = here.z
        layer = Exchange(here, l_s, lo_ref, lsend, lrecv)
        last_cot = lambda: remote(
            crows_ref.at[flip(z, 3)], c3_s, csend.at[0], crecv.at[0], here.dp, flip(z, 3)
        )

    @pl.when(step == 0)
    def _():
        if comm:
            barrier = pltpu.get_barrier_semaphore()
            for k in range(1, row_steps):
                pl.semaphore_signal(
                    barrier, inc=1, device_id=(here.dp, flip(z, k)), device_id_type=pl.DeviceIdType.MESH
                )
            pl.semaphore_wait(barrier, row_steps - 1)
            last_cot().start()
        vecg_ref[...] = jnp.zeros_like(vecg_ref)
        bing_ref[...] = jnp.zeros_like(bing_ref)

    if comm:

        @pl.when(step < row_steps - 1)
        def _():
            cot_s[...] = cot_ref[...]

        @pl.when(step == row_steps - 1)
        def _():
            landed(c3_s, crecv.at[0])
            cot_s[...] = c3_s[...]

    @pl.when(step < row_steps)
    def _():
        at = pl.ds(pl.multiple_of(step * BLK, BLK), BLK)
        dropped = drop_ref[lax.axis_index("tensor")] == 1
        cot = (cot_s if comm else cot_ref)[...].astype(F32)
        att = att_ref[...]
        att_s[at, :] = att
        x = x_ref[...].astype(F32)
        branch = dot_nt(att, wo_ref[...]) + vec(0)
        n1, inv1 = norm_rows(x + branch)
        hidden = n1 * vec(1) + vec(2)
        low = hidden.astype(BF)
        ht_s[:, at] = jnp.transpose(low)
        ffn = hidden + vec(3)
        for t in range(parts):
            pre = dot_nn(low, up(t)) + bin_ref[t * fl : (t + 1) * fl][None, :]
            act, slope = gelu_parts(pre)
            act = act.astype(BF)
            act_s[t, at, :] = act
            slope_s[t] = slope
            ffn = ffn + dot_nt(act, dn(t))
        n2, inv2 = norm_rows(ffn)
        final = n2 * vec(4) + vec(5)
        layer_rows = jnp.where(dropped, x, final).astype(BF)
        if comm:
            l_s[flip(z, partner_at(step))] = layer_rows
        else:
            lo_ref[...] = layer_rows
        g_final = jnp.where(dropped, 0.0, cot)
        g_fpre = norm_back(g_final, n2, inv2, vec(4))
        gb2 = g_fpre.astype(BF)
        gb2t_s[:, at] = jnp.transpose(gb2)
        g_hidden = g_fpre
        for t in range(parts):
            gpre = (dot_nn(gb2, dn(t)) * slope_s[t]).astype(BF)
            gpre_s[t, at, :] = gpre
            bing_ref[:, t * fl : (t + 1) * fl] += jnp.sum(gpre.astype(F32), axis=0, keepdims=True)
            g_hidden = g_hidden + dot_nt(gpre, up(t))
        g_hpre = norm_back(g_hidden, n1, inv1, vec(1))
        gb = g_hpre.astype(BF)
        gbt_s[:, at] = jnp.transpose(gb)
        gatt_ref[...] = dot_nn(gb, wo_ref[...]).astype(BF)
        ghpre_ref[...] = g_hpre + jnp.where(dropped, cot, 0.0)
        for r, v in enumerate(
            (gb.astype(F32), g_hidden * n1, g_hidden, gb2.astype(F32), g_final * n2, g_final)
        ):
            vecg_ref[r : r + 1, :] += jnp.sum(v, axis=0, keepdims=True)

    if comm:
        for k in range(row_steps):

            @pl.when(step == k)
            def _():
                if partner_at(k) == 0:
                    layer.own().start()
                else:
                    layer.copy(partner_at(k)).start()

    @pl.when((step >= row_steps) & (step < row_steps + parts))
    def _():
        t = step - row_steps
        gup_ref[...] = dot_nn(ht_s[...], gpre_s[t]).astype(BF)
        gdn_ref[...] = dot_nn(gb2t_s[...], act_s[t]).astype(BF)

    @pl.when(step == row_steps + parts)
    def _():
        gwo_ref[...] = dot_nn(gbt_s[...], att_s[...]).astype(BF)
        if comm:
            last_cot().wait_send()
            layer.wait_recv()
            layer.wait_send()


def middle(comm, drop, att, x, cot, cot_rows, wo, w, vecs, bias_in):
    length, d = att.shape
    parts, groups, _, group, fl = w.shape
    nr = length // BLK

    def place_of(i):
        return flip(lax.axis_index("tensor"), partner_at(i)) if comm else i

    rows = pl.BlockSpec((BLK, d), lambda i: (place_of(jnp.minimum(i, nr - 1)), 0))
    cot_spec = pl.BlockSpec((BLK, d), lambda i: (place_of(jnp.minimum(i, nr - 1 - comm)), 0))
    any_ = pl.BlockSpec(memory_space=pl.ANY)
    once = lambda shape: pl.BlockSpec(
        shape, lambda i: (0,) * len(shape), pipeline_mode=pl.Buffered(1)
    )
    weight = lambda a: pl.BlockSpec(
        (parts, groups, None, group, fl), lambda i: (0, 0, a, 0, 0), pipeline_mode=pl.Buffered(1)
    )
    part = pl.BlockSpec((None, d, fl), lambda i: (jnp.clip(i - nr, 0, parts - 1), 0, 0))
    whole = lambda shape: pl.BlockSpec(shape, lambda i: (0,) * len(shape))
    dma = pltpu.SemaphoreType.DMA
    comm_scratch = [
        pltpu.VMEM((BLK, d), BF),
        pltpu.VMEM((BLK, d), BF),
        pltpu.VMEM((nr, BLK, d), BF),
        dma((nr,)),
        dma((nr,)),
        dma((1,)),
        dma((1,)),
    ]
    extra = dict(collective_id=2, has_side_effects=True) if comm else {}
    return pl.pallas_call(
        functools.partial(middle_kernel, comm, nr),
        grid=(nr + parts + 1,),
        out_shape=(
            jax.ShapeDtypeStruct((nr, BLK, d) if comm else (length, d), BF),
            jax.ShapeDtypeStruct((length, d), BF),
            jax.ShapeDtypeStruct((length, d), F32),
            jax.ShapeDtypeStruct((parts, d, fl), BF),
            jax.ShapeDtypeStruct((parts, d, fl), BF),
            jax.ShapeDtypeStruct((d, d), BF),
            jax.ShapeDtypeStruct((8, d), F32),
            jax.ShapeDtypeStruct((1, parts * fl), F32),
        ),
        in_specs=[
            pl.BlockSpec(memory_space=pltpu.SMEM),
            rows,
            rows,
            cot_spec,
            any_,
            once((d, d)),
            weight(0),
            weight(1),
            *[once((d,))] * 6,
            once((parts * fl,)),
        ],
        out_specs=(
            any_ if comm else rows, rows, rows, part, part, whole((d, d)), whole((8, d)), whole((1, parts * fl)),
        ),
        scratch_shapes=[
            pltpu.VMEM((length, d), BF),
            pltpu.VMEM((parts, length, fl), BF),
            pltpu.VMEM((parts, length, fl), BF),
            pltpu.VMEM((parts, BLK, fl), F32),
            pltpu.VMEM((d, length), BF),
            pltpu.VMEM((d, length), BF),
            pltpu.VMEM((d, length), BF),
            *(comm_scratch if comm else []),
        ],
        compiler_params=pltpu.CompilerParams(vmem_limit_bytes=VMEM_LIMIT, **extra),
        name="middle",
    )(drop, att, x, cot, cot_rows, wo, w, w, *vecs, bias_in)


def columns(p, start=0):
    return pl.ds(pl.multiple_of(start + p * LANES, LANES), LANES)


def assemble(mix, nz, wqkv_ref, wo_ref):
    d = wo_ref.shape[0]
    wl = d // nz
    for j in range(4):
        whole = jnp.concatenate([mix(t)[:, j * wl : (j + 1) * wl] for t in range(nz)], axis=1)
        if j < 3:
            wqkv_ref[:, j * d : (j + 1) * d] = whole
        else:
            wo_ref[...] = whole


def first_kernel(
    tok_ref, cot_ref, qkvw_ref, wow_ref, upw_ref, dnw_ref, bias_ref, seg_ref,
    x_out, cot_out, wud_out, qkv_out, wqkv_out, xt_out, wo_ref, att_ref, lse_ref, ext_ref,
    sh_ref, mix_s, x_s, qkv_s, wqkv_s, xt_s, kx_s, qx_s, vt_s,
    out_sem, send, recv, line, local, tsend, trecv, csend, crecv,
):
    nz = mix_s.shape[0]
    length, d = att_ref.shape
    pairs = d // LANES
    blk = length // nz
    here = Here(nz)
    mix = Gather(here, mix_s, sh_ref.at[0:1], 0, send, recv, line, local)
    rest = Gather(here, wud_out, sh_ref.at[1:3], 1, send, recv, line, local)
    tokens = Exchange(here, tok_ref, x_s, tsend, trecv)
    cots = Exchange(here, cot_ref, cot_out, csend, crecv, (1, 2))
    sh_ref[0] = jnp.concatenate(
        (qkvw_ref[0], qkvw_ref[1], qkvw_ref[2], jnp.transpose(wow_ref[...])), axis=1
    )
    out_x = pltpu.make_async_copy(x_s, x_out, out_sem.at[0])
    out_qkv = pltpu.make_async_copy(qkv_s, qkv_out, out_sem.at[1])
    out_w = pltpu.make_async_copy(wqkv_s, wqkv_out, out_sem.at[2])
    out_xt = pltpu.make_async_copy(xt_s, xt_out, out_sem.at[3])
    here.greet()
    mix.stage1(0)
    sh_ref[1] = upw_ref[...]
    sh_ref[2] = dnw_ref[...]
    seg = jnp.transpose(jnp.broadcast_to(seg_ref[pl.ds(here.z, 1), :], (LANES, length)))
    doc_lanes(seg, kx_s, qx_s)
    ext_ref[:, :LANES] = kx_s[:, LANES:]
    ext_ref[:, LANES:] = qx_s[:, LANES:]
    vt_s[:, HD:, :] = jnp.ones((2, vt_s.shape[1] - HD, length), BF)
    rest.stage1(0)
    mix.stage1(1)
    mix.stage1(2)
    rest.stage1(1)
    mix.stage1(3)
    tokens.start()
    mix.stage2(0)
    mix.stage2(1)
    mix.stage3(0)
    mix.stage2(2)
    mix.stage3(1)
    mix.stage2(3)
    mix.stage3(2)
    mix.stage3(3)
    rest.stage2(0)
    rest.stage1(2)
    mix.drain()
    assemble(lambda t: mix_s[t].reshape(d, -1), nz, wqkv_s, wo_ref)
    out_w.start()
    bias = jnp.concatenate(
        (bias_ref[0:1, :], jnp.zeros((1, d), F32), bias_ref[1:2, :]), axis=1
    )
    tokens.own().wait()

    def project(k, carry):
        @pl.when(k > 0)
        def _():
            tokens.got(k)

        block = flip(here.z, k)
        at = pl.ds(pl.multiple_of(block * blk, blk), blk)
        qkv_s[at, :] = (dot_nn(x_s[block], wqkv_s[...]) + bias).astype(BF)
        xt_s[:, at] = jnp.transpose(x_s[block])

        @pl.when(k == 0)
        def _():
            rest.stage2(1)
            rest.stage3(0)

        @pl.when(k == 2)
        def _():
            rest.stage1(3)

        return carry

    lax.fori_loop(0, nz, project, 0)
    out_x.start()
    out_qkv.start()
    out_xt.start()
    cots.start()
    between = [
        [lambda: rest.stage2(2), lambda: rest.stage3(1)],
        [lambda: rest.stage2(3), lambda: rest.stage3(2)],
        [lambda: rest.stage3(3)],
    ]

    def work(p):
        o, lse = attend_pair(
            qkv_s[:, columns(p)], qkv_s[:, columns(p, d)], qkv_s[:, columns(p, 2 * d)], kx_s, qx_s, vt_s
        )
        att_ref[:, columns(p)] = o
        lse_ref[p] = lse

    every_pair(pairs, work, between)
    rest.drain()
    tokens.wait_send()
    cots.wait_recv()
    cots.wait_send()
    for copy in (out_x, out_qkv, out_w, out_xt):
        copy.wait()


def first(tokens, cot, qkv_w, wo_w, up_w, dn_w, qv_b, segment_ids):
    nz, nd = lax.axis_size("tensor"), lax.axis_size("dp")
    na, (rw, wide) = 3, up_w.shape
    _, blk, d = tokens.shape
    length = segment_ids.shape[1]
    pairs = d // LANES
    any_ = pl.BlockSpec(memory_space=pl.ANY)
    vmem = pl.BlockSpec(memory_space=pltpu.VMEM)
    dma = pltpu.SemaphoreType.DMA
    s = jax.ShapeDtypeStruct
    unit = lambda count: (nz, nd // 2, 2, count, rw, wide)
    return pl.pallas_call(
        first_kernel,
        out_shape=(
            s(tokens.shape, BF),
            s(tokens.shape, BF),
            s(unit(na - 1), BF),
            s((length, 3 * d), BF),
            s((d, 3 * d), BF),
            s((d, length), BF),
            s((d, d), BF),
            s((length, d), BF),
            s((pairs, 2, length), F32),
            s((length, 2 * LANES), BF),
        ),
        in_specs=[any_, any_] + [vmem] * 6,
        out_specs=(any_,) * 6 + (vmem,) * 4,
        scratch_shapes=[
            pltpu.VMEM((na, rw, wide), BF),
            pltpu.VMEM(unit(1), BF),
            pltpu.VMEM((nz, blk, d), BF),
            pltpu.VMEM((length, 3 * d), BF),
            pltpu.VMEM((d, 3 * d), BF),
            pltpu.VMEM((d, length), BF),
            pltpu.VMEM((length, 2 * LANES), BF),
            pltpu.VMEM((length, 2 * LANES), BF),
            pltpu.VMEM((2, HD + 16, length), BF),
            dma((4,)),
            dma((2, 8)),
            dma((2, nz, 6)),
            dma((2, nz, 2)),
            dma((2,)),
            dma((nz,)),
            dma((nz,)),
            dma((nz,)),
            dma((nz,)),
        ],
        compiler_params=pltpu.CompilerParams(
            collective_id=0, has_side_effects=True, vmem_limit_bytes=VMEM_LIMIT
        ),
        name="first",
    )(tokens, cot, qkv_w, wo_w, up_w, dn_w, qv_b, segment_ids)


def last_kernel(
    gup_ref, gdn_ref, gwo_ref, ghpre_ref, qkv_ref, att_ref, gatt_ref, wqkv_ref, xt_ref,
    lse_ref, ext_ref, vecg_ref, bing_ref,
    grows_ref, gqkv_ref, gout_ref, gup_out, gdn_out, vsum_ref,
    pair_s, g_s, w_s, xt_s, hpre_s, gwo_s, gx_s, kx_s, qx_s, kt_s, delta_s, dk_s, dv_s, vbuf,
    u0, u1, u2, u3, u4, u5, u6, m0, m1, m2, m3, m4, m5, m6,
    psem, hsem, load, uload, send, recv, xsend, xrecv, vsend, vrecv,
):
    nz = u0.shape[0]
    length, d = g_s.shape[1:]
    pairs = d // LANES
    blk = length // nz
    wl = d // nz
    here = Here(nz)
    z = here.z
    ud = Scatter(here, u0, u1, u2, u3, u4, u5, u6, 1, send, recv)
    mx = Scatter(here, m0, m1, m2, m3, m4, m5, m6, 0, send, recv)
    rows = Exchange(here, gx_s, grows_ref, xsend, xrecv)

    def pair_loads(p, slot):
        srcs = (
            qkv_ref.at[:, columns(p)], qkv_ref.at[:, columns(p, d)], qkv_ref.at[:, columns(p, 2 * d)],
            att_ref.at[:, columns(p)], gatt_ref.at[:, columns(p)],
        )
        return [
            pltpu.make_async_copy(src, pair_s.at[slot, j], psem.at[slot, j])
            for j, src in enumerate(srcs)
        ]

    def ud_loads(k):
        t = ud.order[k]
        return [
            pltpu.make_async_copy(
                g.at[t, :, here.core], u0.at[t, :, here.core, a], uload.at[a, t]
            )
            for a, g in enumerate((gup_ref, gdn_ref))
        ]

    def ud_core(k):
        t = ud.order[k]
        for a, g in enumerate((gup_ref, gdn_ref)):
            remote(
                g.at[t, :, 1 - here.core], u1.at[t, :, a], ud.send(0), ud.recv(t, 0), here.dev_c, z
            ).start()

    later = [
        pltpu.make_async_copy(src, dst, load.at[i])
        for i, (src, dst) in enumerate(((wqkv_ref, w_s), (xt_ref, xt_s), (gwo_ref, gwo_s)))
    ]

    def hpre_load(i, slot):
        return pltpu.make_async_copy(ghpre_ref.at[i], hpre_s.at[slot], hsem.at[slot])

    for copy in pair_loads(0, 0):
        copy.start()
    for k in range(nz):
        for copy in ud_loads(k):
            copy.start()
    here.greet()
    for k in range(nz):
        ud_core(k)
    kx_s[:, LANES:] = ext_ref[:, :LANES]
    qx_s[:, LANES:] = ext_ref[:, LANES:]

    def work(p):
        slot = p % 2

        @pl.when(p + 1 < pairs)
        def _():
            for copy in pair_loads(p + 1, 1 - slot):
                copy.start()

        for copy in pair_loads(p, slot):
            copy.wait()
        q, k, v, att, g = [pair_s.at[slot, j] for j in range(5)]

        def put_q(at, value):
            g_s[0, at, columns(p)] = value

        attend_pair_back(q, k, v, att, g, lse_ref[p], kx_s, qx_s, kt_s, delta_s, dk_s, dv_s, put_q)
        g_s[1, :, columns(p)] = dk_s[...].astype(BF)
        g_s[2, :, columns(p)] = dv_s[...].astype(BF)

    def start_later():
        for copy in later:
            copy.start()

    def run(*names):
        return [lambda name=name, k=k: getattr(ud, name)(k) for name, k in names]

    def halves_here():
        for k in range(nz):
            for copy in ud_loads(k):
                copy.wait()

    between = [
        [halves_here] + run(("stage2", 0), ("stage2", 1)),
        run(("stage2", 2), ("stage3", 0), ("stage2", 3)),
        run(("stage3", 1),) + [start_later],
        run(("stage4", 0), ("stage5", 0), ("stage3", 2)),
        run(("stage3", 3), ("stage4", 1), ("stage5", 1)),
    ]
    every_pair(pairs, work, between)

    place_of = [flip(z, k) for k in (2, 3, 1, 0)]
    hpre_load(place_of[0], 0).start()
    for copy in later:
        copy.wait()
    for i, to in enumerate(place_of):
        if i + 1 < nz:
            hpre_load(place_of[i + 1], (i + 1) % 2).start()
        hpre_load(to, i % 2).wait()
        at = pl.ds(pl.multiple_of(to * blk, blk), blk)
        total = hpre_s[i % 2]
        for j in range(3):
            total = total + dot_nt(g_s[j, at, :], w_s[:, j * d : (j + 1) * d])
        gx_s[to] = total.astype(BF)
        if i + 1 < nz:
            rows.copy((2, 3, 1)[i]).start()
        else:
            rows.own().start()

    ud.stage4(2)
    ud.stage5(2)

    vsum_ref[...] = jnp.zeros_like(vsum_ref)
    vsum_ref[0:8, :] = vecg_ref[...]
    for i in range(bing_ref.shape[1] // d):
        vsum_ref[8 + i : 9 + i, :] = bing_ref[:, i * d : (i + 1) * d]
    xt = xt_s[...]
    for j in range(3):
        grad = dot_nn(xt, g_s[j]).astype(BF)
        for t in range(nz):
            part = grad[:, t * wl : (t + 1) * wl]
            m0[t, :, :, 0, :, j * wl : (j + 1) * wl] = part.reshape(m0.shape[1:3] + (m0.shape[4], wl))
        if j != 1:
            sums = jnp.sum(g_s[j].astype(F32), axis=0, keepdims=True)
            r = vsum_ref.shape[0] - 2 + j // 2
            vsum_ref[r : r + 1, :] = sums
    for t in range(nz):
        part = gwo_s[:, t * wl : (t + 1) * wl]
        m0[t, :, :, 0, :, 3 * wl :] = part.reshape(m0.shape[1:3] + (m0.shape[4], wl))

    partners = [(here.dev_c, z), (here.dev_x, z), (here.dev_y, z)]
    partners += [(here.dp, z + 1 - 2 * (z % 2)), (here.dp, (z + 2) % nz)]

    def vec_copy(k):
        return remote(vbuf.at[0, k], vbuf.at[1, k], vsend.at[k], vrecv.at[k], *partners[k])

    def vec_start(k):
        vbuf[0, k] = vsum_ref[...]
        vec_copy(k).start()

    def vec_finish(k):
        landed(vbuf.at[1, k], vrecv.at[k])
        vsum_ref[...] += vbuf[1, k]

    for k in range(nz):
        mx.stage1(k)
    vec_start(0)
    for k in range(nz + 3):
        if k < nz:
            mx.stage2(k)
        if 1 <= k <= nz:
            mx.stage3(k - 1)
        if k < len(partners):
            vec_finish(k)
            if k + 1 < len(partners):
                vec_start(k + 1)
        if 2 <= k <= nz + 1:
            mx.stage4(k - 2)
        if 3 <= k <= nz + 1:
            mx.stage5(k - 3)
    ud.stage4(3)
    up_sum, dn_sum = ud.total()
    gup_out[...] = up_sum
    gdn_out[...] = dn_sum
    (mix_sum,) = mx.total()
    for j in range(3):
        gqkv_ref[j] = mix_sum[:, j * wl : (j + 1) * wl]
    gout_ref[...] = jnp.transpose(mix_sum[:, 3 * wl :])
    ud.drain()
    mx.drain()
    for k in range(len(partners)):
        vec_copy(k).wait_send()
    rows.wait_recv()
    rows.wait_send()


def last(gup, gdn, gwo, ghpre, qkv, att, gatt, wqkv, xt, lse, ext, vecg, bing):
    nz, nd = lax.axis_size("tensor"), lax.axis_size("dp")
    length, d = att.shape
    rw, wide, wl = d // nd, gup.shape[2], d // nz
    blk = length // nz
    unit = (nz, nd // 2, 2, rw, wide)
    any_ = pl.BlockSpec(memory_space=pl.ANY)
    vmem = pl.BlockSpec(memory_space=pltpu.VMEM)
    dma = pltpu.SemaphoreType.DMA
    s = jax.ShapeDtypeStruct
    steps = 5
    vec_shape = (16, d)
    return pl.pallas_call(
        last_kernel,
        out_shape=(
            s((nz, blk, d), BF),
            s((3, rw, wl), F32),
            s((wl, rw), F32),
            s((rw, wide), F32),
            s((rw, wide), F32),
            s(vec_shape, F32),
        ),
        in_specs=[any_] * 9 + [vmem] * 4,
        out_specs=(any_,) + (vmem,) * 5,
        scratch_shapes=[
            pltpu.VMEM((2, 5, length, LANES), BF),
            pltpu.VMEM((3, length, d), BF),
            pltpu.VMEM((d, 3 * d), BF),
            pltpu.VMEM((d, length), BF),
            pltpu.VMEM((2, blk, d), F32),
            pltpu.VMEM((d, d), BF),
            pltpu.VMEM((nz, blk, d), BF),
            pltpu.VMEM((length, 2 * LANES), BF),
            pltpu.VMEM((length, 2 * LANES), BF),
            pltpu.VMEM((LANES, length), BF),
            pltpu.VMEM((8, length), F32),
            pltpu.VMEM((length, LANES), F32),
            pltpu.VMEM((length, LANES), F32),
            pltpu.VMEM((2, steps) + vec_shape, F32),
        ]
        + scatter_scratch(2, nz, nd, rw, wide)
        + scatter_scratch(1, nz, nd, rw, wide)
        + [
            dma((2, 5)),
            dma((2,)),
            dma((3,)),
            dma((2, nz)),
            dma((2, 6)),
            dma((2, nz, 7)),
            dma((nz,)),
            dma((nz,)),
            dma((steps,)),
            dma((steps,)),
        ],
        compiler_params=pltpu.CompilerParams(
            collective_id=1, has_side_effects=True, vmem_limit_bytes=LAST_LIMIT
        ),
        name="last",
    )(
        gup.reshape(unit), gdn.reshape(unit), gwo, ghpre.reshape(nz, blk, d),
        qkv, att, gatt, wqkv, xt, lse, ext, vecg, bing,
    )


LAST_LIMIT = 61 * 1024 * 1024


def finish_kernel(lrows, grows, gqkv, gout, gup, gdn, sums, *outs):
    (
        layer_out, grad_tokens, o_qkv, o_qvb, o_out, o_outb, o_gain1, o_shift1,
        o_up, o_upb, o_dn, o_dnb, o_gain2, o_shift2,
    ) = outs
    layer_out[...] = lrows[...]
    grad_tokens[...] = grows[...].astype(F32)

    @pl.when(pl.program_id(0) == 0)
    def _():
        d = sums.shape[1]
        for dst, src in ((o_qkv, gqkv), (o_out, gout), (o_up, gup), (o_dn, gdn)):
            dst[...] = src[...]
        for r, dst in enumerate((o_outb, o_gain1, o_shift1, o_dnb, o_gain2, o_shift2)):
            dst[...] = sums[r, :]
        for r in range(o_upb.shape[0] // d):
            o_upb[r * d : (r + 1) * d] = sums[8 + r, :]
        o_qvb[...] = sums[sums.shape[0] - 2 :, :]


def finish(lrows, grows, gqkv, gout, gup, gdn, sums, hidden):
    nz, blk, d = lrows.shape
    rows = pl.BlockSpec((nz // 2, blk, d), lambda i: (i, 0, 0))
    s = jax.ShapeDtypeStruct
    same = lambda a: s(a.shape, a.dtype)
    vector = s((d,), F32)
    outs = (
        same(lrows), s(grows.shape, F32), same(gqkv), s((2, d), F32), same(gout), vector, vector, vector,
        same(gup), s((hidden,), F32), same(gdn), vector, vector, vector,
    )
    whole = lambda a: pl.BlockSpec(a.shape, lambda i: (0,) * len(a.shape))
    return pl.pallas_call(
        finish_kernel,
        grid=(2,),
        out_shape=outs,
        in_specs=[rows, rows] + [whole(a) for a in (gqkv, gout, gup, gdn, sums)],
        out_specs=[rows, rows] + [whole(a) for a in outs[2:]],
        compiler_params=pltpu.CompilerParams(vmem_limit_bytes=VMEM_LIMIT),
        name="finish",
    )(lrows, grows, gqkv, gout, gup, gdn, sums)


def plain_attend_kernel(q_ref, k_ref, v_ref, segc_ref, o_ref, lse_ref, kx_s, qx_s, vt_s):
    doc_lanes(segc_ref[...], kx_s, qx_s)
    vt_s[:, HD:, :] = jnp.ones((2, vt_s.shape[1] - HD, vt_s.shape[2]), BF)
    o_ref[...], lse_ref[...] = attend_pair(q_ref[...], k_ref[...], v_ref[...], kx_s, qx_s, vt_s)


def plain_attend_back_kernel(
    q_ref, k_ref, v_ref, att_ref, g_ref, lse_ref, segc_ref, gq_ref, gk_ref, gv_ref,
    kx_s, qx_s, kt_s, delta_s, dk_s, dv_s,
):
    doc_lanes(segc_ref[...], kx_s, qx_s)

    def put_q(at, value):
        gq_ref[at, :] = value

    attend_pair_back(
        q_ref, k_ref, v_ref, att_ref, g_ref, lse_ref[...], kx_s, qx_s, kt_s, delta_s, dk_s, dv_s, put_q
    )
    gk_ref[...] = dk_s[...].astype(BF)
    gv_ref[...] = dv_s[...].astype(BF)


def plain_specs(length, d):
    col = lambda off: pl.BlockSpec((length, LANES), lambda p: (0, off + p))
    seg = pl.BlockSpec((length, LANES), lambda p: (0, 0))
    lse = pl.BlockSpec((None, 2, length), lambda p: (p, 0, 0))
    wide = pltpu.VMEM((length, 2 * LANES), BF)
    return d // LANES, col, seg, lse, wide


def plain_first(tokens, cot, qkv_w, wo_w, up_w, dn_w, qv_b, segment_ids):
    axes = ("tensor", "dp")
    nz = lax.axis_size("tensor")
    length, d = segment_ids.shape[1], tokens.shape[2]
    pairs, col, seg, lse_spec, wide = plain_specs(length, d)
    mix = jnp.concatenate((qkv_w[0], qkv_w[1], qkv_w[2], wo_w.T), axis=1)
    shards = jnp.stack((mix, up_w, dn_w))
    ids = lax.dynamic_index_in_dim(segment_ids, lax.axis_index("tensor"), 0, keepdims=False)
    segc = jnp.broadcast_to(ids[:, None], (length, LANES))
    bias = jnp.concatenate((qv_b[0], jnp.zeros((d,), F32), qv_b[1]))
    x = lax.all_to_all(tokens, "tensor", 0, 0)
    cot = lax.all_to_all(cot, "tensor", 0, 0)
    w = lax.all_gather(shards, axes, axis=1, tiled=True).reshape(3, nz, d, shards.shape[2])
    parts = w[0].reshape(nz, d, 4, d // nz).transpose(1, 2, 0, 3).reshape(d, 4 * d)
    wqkv, wo = parts[:, : 3 * d], parts[:, 3 * d :]
    rows = x.reshape(length, d)
    qkv = (dot_nn(rows, wqkv) + bias).astype(BF)
    att, lse = pl.pallas_call(
        plain_attend_kernel,
        grid=(pairs,),
        out_shape=(
            jax.ShapeDtypeStruct((length, d), BF),
            jax.ShapeDtypeStruct((pairs, 2, length), F32),
        ),
        in_specs=[col(0), col(pairs), col(2 * pairs), seg],
        out_specs=(col(0), lse_spec),
        scratch_shapes=[wide, wide, pltpu.VMEM((2, HD + 16, length), BF)],
        compiler_params=pltpu.CompilerParams(vmem_limit_bytes=VMEM_LIMIT),
        name="plain_attend",
    )(qkv, qkv, qkv, segc)
    wud = w[1:].reshape(2, nz, 8, d // 8, -1).transpose(1, 2, 0, 3, 4)
    return x, cot, wud, qkv, wqkv, rows.T, wo, att, lse, segc


def plain_last(gup, gdn, gwo, ghpre, qkv, att, gatt, wqkv, xt, lse, segc, vecg, bing):
    axes = ("tensor", "dp")
    nz = lax.axis_size("tensor")
    length, d = att.shape
    pairs, col, seg, lse_spec, wide = plain_specs(length, d)
    f32_wide = pltpu.VMEM((length, LANES), F32)
    grads = pl.pallas_call(
        plain_attend_back_kernel,
        grid=(pairs,),
        out_shape=[jax.ShapeDtypeStruct((length, d), BF)] * 3,
        in_specs=[col(0), col(pairs), col(2 * pairs), col(0), col(0), lse_spec, seg],
        out_specs=[col(0)] * 3,
        scratch_shapes=[
            wide, wide, pltpu.VMEM((LANES, length), BF), pltpu.VMEM((8, length), F32), f32_wide, f32_wide,
        ],
        compiler_params=pltpu.CompilerParams(vmem_limit_bytes=VMEM_LIMIT),
        name="plain_attend_back",
    )(qkv, qkv, qkv, att, gatt, lse, segc)
    g = jnp.concatenate(grads, axis=1)
    gx = (ghpre + dot_nt(g, wqkv)).astype(BF)
    gmix = jnp.concatenate((dot_nn(xt, g).astype(BF), gwo), axis=1)
    gmix = gmix.reshape(d, 4, nz, d // nz).transpose(2, 0, 1, 3).reshape(nz, d, -1)
    split = lambda a: a.reshape(nz, length // nz, d)
    parts = [
        lax.psum_scatter(p.reshape(nz * d, -1), axes, scatter_dimension=0, tiled=True)
        for p in (gmix, gup, gdn)
    ]
    mix_sum, up_sum, dn_sum = [p.astype(F32) for p in parts]
    wl = d // nz
    sums = [jnp.sum(grads[j].astype(F32), axis=0, keepdims=True) for j in (0, 2)]
    bing = bing.reshape(-1, d)
    gap = jnp.zeros((6 - bing.shape[0], d), F32)
    vec = jnp.concatenate((vecg, bing, gap, *sums), axis=0)
    return (
        lax.all_to_all(split(gx), "tensor", 0, 0),
        jnp.stack([mix_sum[:, j * wl : (j + 1) * wl] for j in range(3)]),
        mix_sum[:, 3 * wl :].T,
        up_sum,
        dn_sum,
        lax.psum(vec, axes),
    )


def on_device(
    tokens, segment_ids, drop_flags, qkv_w, qv_b, wo_w, wo_b, gain1, shift1,
    up_w, up_b, dn_w, dn_b, gain2, shift2, cotangent,
):
    nt, nd = lax.axis_size("tensor"), lax.axis_size("dp")
    d = tokens.shape[2]
    length = segment_ids.shape[1]
    wl = qkv_w.shape[2]
    fl = up_w.shape[1]
    comm = (nt, nd) == (4, 8)
    begin, end = (first, last) if comm else (plain_first, plain_last)
    x, cot, wud, qkv, wqkv, xt, wo, att, lse, ext = begin(
        tokens, cotangent, qkv_w, wo_w, up_w, dn_w.T, qv_b, segment_ids
    )
    vecs = (wo_b, gain1, shift1, dn_b, gain2, shift2)
    layer_out, g_att, g_hpre, gup, gdn, gwo, vecg, bing = middle(
        comm, drop_flags, att, x.reshape(length, d), cot.reshape(length, d), cotangent, wo,
        wud.reshape(nt, -1, 2, *wud.shape[-2:]), vecs, up_b,
    )
    if not comm:
        layer_out = lax.all_to_all(layer_out.reshape(nt, length // nt, d), "tensor", 0, 0)
    rows, g_qkv, g_out, g_up, g_dn, total = end(
        gup, gdn, gwo, g_hpre, qkv, att, g_att, wqkv, xt, lse, ext, vecg, bing
    )
    outs = finish(layer_out, rows, g_qkv, g_out, g_up, g_dn, total, nt * fl)
    return (*outs[:10], outs[10].T, *outs[11:])


def solution(mesh):
    rows = P("dp", "tensor", None)
    return jax.shard_map(
        on_device,
        mesh=mesh,
        in_specs=(
            rows, P("dp", None), P("dp"), P(None, "dp", "tensor"), P(), P("tensor", "dp"), P(), P(), P(),
            P("dp", "tensor"), P(), P("tensor", "dp"), P(), P(), P(), rows,
        ),
        out_specs=(
            rows, rows, P(None, "dp", "tensor"), P(), P("tensor", "dp"), P(), P(), P(),
            P("dp", "tensor"), P(), P("tensor", "dp"), P(), P(), P(),
        ),
        check_vma=False,
    )
```

```python
import functools
import jax
import jax.numpy as jnp
from jax import lax
from jax.experimental import pallas as pl
from jax.experimental.pallas import tpu as pltpu
from jax.sharding import PartitionSpec as P

HD = 64
EPS = 1e-05
NEG = -1000000000.0
BF = jnp.bfloat16
F32 = jnp.float32
VMEM_LIMIT = 60 * 1024 * 1024
BLK = 256
LANES = 128


def dot_nn(a, b):
    return jnp.dot(a, b, preferred_element_type=F32)


def dot_nt(a, b):
    return lax.dot_general(a, b, (((1,), (1,)), ((), ())), preferred_element_type=F32)


def dot_tn(a, b):
    return lax.dot_general(a, b, (((0,), (0,)), ((), ())), preferred_element_type=F32)


def doc_lanes(seg, kx_s, qx_s):
    lane = lax.broadcasted_iota(jnp.int32, seg.shape, 1)
    same = (seg == lane).astype(F32)
    kx_s[:, LANES:] = same.astype(BF)
    qx_s[:, LANES:] = ((1.0 - same) * NEG).astype(BF)


def split_heads(pair):
    first = lax.broadcasted_iota(jnp.int32, pair.shape, 1) % (2 * HD) < HD
    zero = jnp.zeros((), pair.dtype)
    return jnp.where(first, pair, zero), jnp.where(first, zero, pair)


def attend_pair(q, k, v, kx_s, qx_s, vt_s):
    kx_s[:, :LANES] = k
    qx_s[:, :LANES] = (q.astype(F32) * 0.125).astype(BF)
    vt = jnp.transpose(v)
    vt_s[0, :HD, :] = vt[:HD, :]
    vt_s[1, :HD, :] = vt[HD:, :]
    kx = kx_s[...]
    ext = qx_s[:, LANES:]
    outs, lses = [], []
    scores = [
        dot_nt(kx, jnp.concatenate((h, ext), axis=1)) for h in split_heads(qx_s[:, :LANES])
    ]
    for h in range(2):
        top = jnp.max(scores[h], axis=0, keepdims=True)
        p = jnp.exp(scores[h] - top).astype(BF)
        o = dot_nn(vt_s[h], p)
        total = o[HD : HD + 1, :]
        outs.append(o[:HD, :] / total)
        lses.append(top + jnp.log(total))
    return jnp.transpose(jnp.concatenate(outs, axis=0)).astype(BF), jnp.concatenate(lses, axis=0)


def attend_pair_back(q_ref, k_ref, v_ref, att_ref, g_ref, lse, kx_s, qx_s, kt_s, delta_s, dk_s, dv_s, put_q):
    length = q_ref.shape[0]
    kx_s[:, :LANES] = k_ref[...]
    qx_s[:, :LANES] = (q_ref[...].astype(F32) * 0.125).astype(BF)
    kt_s[...] = jnp.transpose(k_ref[...])
    sub = lax.broadcasted_iota(jnp.int32, (8, LANES), 0)
    lane = lax.broadcasted_iota(jnp.int32, (8, LANES), 1)
    pick = jnp.where(lane // HD == sub, 1.0, 0.0).astype(BF)
    prod = g_ref[...].astype(F32) * att_ref[...].astype(F32)
    upper = prod.astype(BF)
    lower = (prod - upper.astype(F32)).astype(BF)
    delta_s[...] = dot_nt(pick, upper) + dot_nt(pick, lower)
    for i in range(length // QB):
        at = slice(i * QB, (i + 1) * QB)
        kx = kx_s[...]
        v = v_ref[...]
        ext = qx_s[at, LANES:]
        qs = split_heads(qx_s[at, :LANES])
        gs = split_heads(g_ref[at, :])
        ps, ds, dq = [], [], []
        for h in range(2):
            s = dot_nt(kx, jnp.concatenate((qs[h], ext), axis=1))
            p = jnp.exp(s - lse[h : h + 1, at])
            dp = dot_nt(v, gs[h])
            d = (p * (dp - delta_s[h : h + 1, at])).astype(BF)
            ps.append(p.astype(BF))
            ds.append(d)
            dq.append(dot_nn(kt_s[h * HD : (h + 1) * HD, :], d))
        dv = dot_nn(jnp.concatenate(ps, axis=1), jnp.concatenate(gs, axis=0))
        dk = dot_nn(jnp.concatenate(ds, axis=1), jnp.concatenate(qs, axis=0))
        dv_s[...] = dv if i == 0 else dv_s[...] + dv
        dk_s[...] = dk if i == 0 else dk_s[...] + dk
        put_q(at, (jnp.transpose(jnp.concatenate(dq, axis=0)) * 0.125).astype(BF))


QB = 512


def place(dp):
    yx, core = dp // 2, dp % 2
    y, x = yx // 2, yx % 2
    return yx, core, y * 2 + 1 - x, (1 - y) * 2 + x, 3 - yx


def remote(src, dst, send, recv, dp, z):
    return pltpu.make_async_remote_copy(
        src_ref=src,
        dst_ref=dst,
        send_sem=send,
        recv_sem=recv,
        device_id=(dp, z),
        device_id_type=pl.DeviceIdType.MESH,
    )


def greet(dp, z, yx, core, yx_x, yx_y, nz):
    barrier = pltpu.get_barrier_semaphore()
    others = [(yx_x * 2 + core, z), (yx_y * 2 + core, z), (yx * 2 + 1 - core, z)]
    others += [(dp, (z + k) % nz) for k in range(1, nz)]
    for dev in others:
        pl.semaphore_signal(
            barrier, inc=1, device_id=dev, device_id_type=pl.DeviceIdType.MESH
        )
    pl.semaphore_wait(barrier, len(others))


def landed(ref, sem):
    pltpu.make_async_copy(ref, ref, sem).wait()


class Here:
    def __init__(self, nz):
        self.nz = nz
        self.dp, self.z = lax.axis_index("dp"), lax.axis_index("tensor")
        self.yx, self.core, self.yx_x, self.yx_y, self.yx_d = place(self.dp)
        self.dev_x = self.yx_x * 2 + self.core
        self.dev_y = self.yx_y * 2 + self.core
        self.dev_c = self.yx * 2 + 1 - self.core

    def greet(self):
        greet(self.dp, self.z, self.yx, self.core, self.yx_x, self.yx_y, self.nz)

    def sides(self, s, body):
        if s == 0:
            body(self.z, None)
            return

        @pl.when(self.z >= s)
        def _():
            body(self.z - s, True)

        @pl.when(self.z + s < self.nz)
        def _():
            body(self.z + s, False)


def flip(z, i):
    return (z % 2 + i % 2) % 2 + 2 * ((z // 2 + i // 2) % 2)


class Exchange:
    def __init__(self, here, src, dst, send, recv, ks=(1, 2, 3)):
        self.here, self.src, self.dst, self.send, self.recv, self.ks = here, src, dst, send, recv, ks

    def copy(self, k):
        h = self.here
        to = flip(h.z, k)
        return remote(
            self.src.at[to], self.dst.at[h.z], self.send.at[k], self.recv.at[k], h.dp, to
        )

    def own(self):
        z = self.here.z
        return pltpu.make_async_copy(self.src.at[z], self.dst.at[z], self.send.at[0])

    def start(self):
        for k in self.ks:
            self.copy(k).start()
        self.own().start()

    def got(self, k):
        landed(self.dst.at[flip(self.here.z, k)], self.recv.at[k])

    def wait_recv(self):
        self.own().wait()
        for k in self.ks:
            self.got(k)

    def wait_send(self):
        for k in self.ks:
            self.copy(k).wait_send()


class Gather:
    def __init__(self, here, w_ref, sh_ref, group, send, recv, line, local):
        self.here, self.w, self.sh = here, w_ref, sh_ref
        self.send = lambda kind: send.at[group, kind]
        self.recv = lambda t, kind: recv.at[group, t, kind]
        self.line = lambda t, kind: line.at[group, t, kind]
        self.all_cores = recv.at[group, 0, 5]
        self.local = local.at[group]
        half = w_ref.shape[4] // 2
        self.low, self.high = pl.ds(0, half), pl.ds(half, half)

    def blk(self, t, yx):
        return self.w.at[t, yx, self.here.core]

    def to_plane(self, t, own, kind):
        h = self.here
        dst = self.blk(t, h.yx)
        dev = (h.dev_x, h.dev_y, h.dev_c)[kind]
        arrived = self.all_cores if kind == 2 else self.recv(t, kind)
        return remote(self.sh if own else dst, dst, self.send(kind), arrived, dev, h.z)

    def to_line(self, t, own, kind):
        h = self.here
        dst = self.blk(t, h.yx)
        to = (h.z + 1) % h.nz if kind == 0 else (h.z + h.nz - 1) % h.nz
        return remote(self.sh if own else dst, dst, self.line(t, kind), self.recv(t, 4), h.dp, to)

    def own_copy(self):
        return pltpu.make_async_copy(self.sh, self.blk(self.here.z, self.here.yx), self.local)

    def half_y(self, t):
        b = self.w.at[t, self.here.yx_x, self.here.core, :, self.low]
        return remote(b, b, self.send(3), self.recv(t, 2), self.here.dev_y, self.here.z)

    def half_x(self, t):
        b = self.w.at[t, self.here.yx_y, self.here.core, :, self.high]
        return remote(b, b, self.send(4), self.recv(t, 3), self.here.dev_x, self.here.z)

    def to_core(self, t, yx, kind):
        b = self.blk(t, yx)
        return remote(b, b, self.send(kind), self.all_cores, self.here.dev_c, self.here.z)

    def along(self, s, from_left, right, left):
        h = self.here
        if s == 0 or from_left:
            pl.when(h.z < h.nz - 1)(right)
        if s == 0 or not from_left:
            pl.when(h.z > 0)(left)

    def stage1(self, s):
        own = s == 0

        def body(t, from_left):
            if own:
                self.own_copy().start()
            else:
                landed(self.blk(t, self.here.yx), self.recv(t, 4))
            self.along(
                s, from_left,
                lambda: self.to_line(t, own, 0).start(), lambda: self.to_line(t, own, 1).start(),
            )
            for kind in range(3):
                self.to_plane(t, own, kind).start()

        self.here.sides(s, body)

    def stage2(self, s):
        h = self.here

        def body(t, from_left):
            landed(self.blk(t, h.yx_x), self.recv(t, 0))
            self.half_y(t).start()
            self.to_core(t, h.yx_x, 5).start()
            landed(self.blk(t, h.yx_y), self.recv(t, 1))
            self.half_x(t).start()
            self.to_core(t, h.yx_y, 6).start()

        h.sides(s, body)

    def stage3(self, s):
        h = self.here

        def body(t, from_left):
            landed(self.w.at[t, h.yx_d, h.core, :, self.low], self.recv(t, 2))
            landed(self.w.at[t, h.yx_d, h.core, :, self.high], self.recv(t, 3))
            self.to_core(t, h.yx_d, 7).start()

        h.sides(s, body)

    def arrive(self):
        landed(self.w.at[:, :, 1 - self.here.core], self.all_cores)
        self.own_copy().wait()

    def sent(self):
        h, w = self.here, self.w
        for kind in (0, 1, 2, 5, 6, 7):
            landed(w.at[:, h.yx, h.core], self.send(kind))
        landed(w.at[:, h.yx_x, h.core, :, self.low], self.send(3))
        landed(w.at[:, h.yx_y, h.core, :, self.high], self.send(4))
        for s in range(h.nz):

            def body(t, from_left):
                self.along(
                    s, from_left,
                    lambda: self.to_line(t, s == 0, 0).wait_send(),
                    lambda: self.to_line(t, s == 0, 1).wait_send(),
                )

            h.sides(s, body)


class Scatter:
    def __init__(self, here, own, rc, rda, rdb, rx, ry, rz, group, send, recv, order=None):
        self.here, self.own = here, own
        self.rc, self.rda, self.rdb, self.rx, self.ry, self.rz = rc, rda, rdb, rx, ry, rz
        self.send = lambda kind: send.at[group, kind]
        self.recv = lambda t, kind: recv.at[group, t, kind]
        half = own.shape[4] // 2
        self.low, self.high = pl.ds(0, half), pl.ds(half, half)
        z = here.z
        self.order = order or [3 * (1 - z // 2), (2 + 3 * z) % 5, 1 + z % 2, z]

    def copy(self, t, kind):
        h, own = self.here, self.own
        src, dst, dev, z = (
            lambda: (own.at[t, :, 1 - h.core], self.rc.at[t], h.dev_c, h.z),
            lambda: (own.at[t, h.yx_d, h.core, :, self.low], self.rda.at[t], h.dev_x, h.z),
            lambda: (own.at[t, h.yx_d, h.core, :, self.high], self.rdb.at[t], h.dev_y, h.z),
            lambda: (own.at[t, h.yx_x, h.core], self.rx.at[t], h.dev_x, h.z),
            lambda: (own.at[t, h.yx_y, h.core], self.ry.at[t], h.dev_y, h.z),
            lambda: (own.at[t, h.yx, h.core], self.rz.at[0, t], h.dp, (h.z + 1) % h.nz),
            lambda: (own.at[t, h.yx, h.core], self.rz.at[1, t], h.dp, (h.z + h.nz - 1) % h.nz),
        )[kind]()
        return remote(src, dst, self.send(min(kind, 5)), self.recv(t, kind), dev, z)

    def add(self, dst, *srcs):
        total = dst[...].astype(F32)
        for src in srcs:
            total = total + src[...].astype(F32)
        dst[...] = total.astype(BF)

    def stage1(self, k):
        self.copy(self.order[k], 0).start()

    def stage2(self, k):
        h, t = self.here, self.order[k]
        landed(self.rc.at[t], self.recv(t, 0))
        self.add(self.own.at[t, h.yx_d, h.core], self.rc.at[t, h.yx_d])
        self.copy(t, 1).start()
        self.copy(t, 2).start()
        for yx in (h.yx_x, h.yx_y, h.yx):
            self.add(self.own.at[t, yx, h.core], self.rc.at[t, yx])

    def stage3(self, k):
        h, t = self.here, self.order[k]
        landed(self.rda.at[t], self.recv(t, 1))
        self.add(self.own.at[t, h.yx_y, h.core, :, self.low], self.rda.at[t])
        self.copy(t, 4).start()
        landed(self.rdb.at[t], self.recv(t, 2))
        self.add(self.own.at[t, h.yx_x, h.core, :, self.high], self.rdb.at[t])
        self.copy(t, 3).start()

    def stage4(self, k):
        h, t = self.here, self.order[k]
        landed(self.rx.at[t], self.recv(t, 3))
        landed(self.ry.at[t], self.recv(t, 4))
        self.add(self.own.at[t, h.yx, h.core], self.rx.at[t], self.ry.at[t])

    def stage5(self, k):
        h, t = self.here, self.order[k]
        mine = self.own.at[t, h.yx, h.core]

        @pl.when(t > h.z)
        def _():
            @pl.when(h.z > 0)
            def _():
                landed(self.rz.at[0, t], self.recv(t, 5))
                self.add(mine, self.rz.at[0, t])

            self.copy(t, 5).start()

        @pl.when(t < h.z)
        def _():
            @pl.when(h.z < h.nz - 1)
            def _():
                landed(self.rz.at[1, t], self.recv(t, 6))
                self.add(mine, self.rz.at[1, t])

            self.copy(t, 6).start()

    def total(self):
        h, z = self.here, self.here.z
        mine = self.own.at[z, h.yx, h.core]

        @pl.when((z > 0) & (z < h.nz - 1))
        def _():
            landed(self.rz.at[0, z], self.recv(z, 5))
            landed(self.rz.at[1, z], self.recv(z, 6))
            self.add(mine, self.rz.at[0, z], self.rz.at[1, z])

        @pl.when(z == 0)
        def _():
            landed(self.rz.at[1, z], self.recv(z, 6))
            self.add(mine, self.rz.at[1, z])

        @pl.when(z == h.nz - 1)
        def _():
            landed(self.rz.at[0, z], self.recv(z, 5))
            self.add(mine, self.rz.at[0, z])

        return [mine[a].astype(F32) for a in range(mine.shape[0])]

    def drain(self):
        h, own = self.here, self.own
        landed(own.at[:, :, 1 - h.core], self.send(0))
        landed(own.at[:, h.yx_d, h.core, :, self.low], self.send(1))
        landed(own.at[:, h.yx_d, h.core, :, self.high], self.send(2))
        landed(own.at[:, h.yx_x, h.core], self.send(3))
        landed(own.at[:, h.yx_y, h.core], self.send(4))
        landed(self.rz.at[0, pl.ds(0, h.nz - 1)], self.send(5))


def scatter_scratch(na, nz, nd, rw, wide):
    return [
        pltpu.VMEM((nz, nd // 2, 2, na, rw, wide), BF),
        pltpu.VMEM((nz, nd // 2, na, rw, wide), BF),
        pltpu.VMEM((nz, na, rw // 2, wide), BF),
        pltpu.VMEM((nz, na, rw // 2, wide), BF),
        pltpu.VMEM((nz, na, rw, wide), BF),
        pltpu.VMEM((nz, na, rw, wide), BF),
        pltpu.VMEM((2, nz, na, rw, wide), BF),
    ]


def every_pair(pairs, work, between):
    def step(p, carry):
        work(p)
        for at, steps in enumerate(between):

            @pl.when(p == at)
            def _():
                for run in steps:
                    run()

        return carry

    lax.fori_loop(0, pairs, step, 0)


def gelu_parts(u):
    cdf = 0.5 + 0.5 * lax.erf(u * 0.7071067811865476)
    return u * cdf, cdf + u * jnp.exp(-0.5 * u * u) * 0.3989422804014327


def norm_rows(v):
    mean = jnp.mean(v, axis=-1, keepdims=True)
    c = v - mean
    inv = lax.rsqrt(jnp.mean(c * c, axis=-1, keepdims=True) + EPS)
    return c * inv, inv


def norm_back(g, normed, inv, gain):
    gn = g * gain
    return inv * (
        gn
        - jnp.mean(gn, axis=-1, keepdims=True)
        - normed * jnp.mean(gn * normed, axis=-1, keepdims=True)
    )


def partner_at(step):
    return (6 - step) % 4


def middle_kernel(comm, row_steps, *refs):
    drop_ref, att_ref, x_ref, cot_ref, crows_ref, wo_ref, up_ref, dn_ref = refs[:8]
    vecs, bin_ref = refs[8:14], refs[14]
    lo_ref, gatt_ref, ghpre_ref, gup_ref, gdn_ref, gwo_ref, vecg_ref, bing_ref = refs[15:23]
    att_s, act_s, gpre_s, slope_s, ht_s, gb2t_s, gbt_s = refs[23:30]
    step = pl.program_id(0)
    parts, d, fl = up_ref.shape[0], att_ref.shape[1], up_ref.shape[3]
    up = lambda t: up_ref[t].reshape(d, fl)
    dn = lambda t: dn_ref[t].reshape(d, fl)
    vec = lambda r: vecs[r][...][None, :]
    if comm:
        cot_s, c3_s, l_s, lsend, lrecv, csend, crecv = refs[30:]
        here = Here(row_steps)
        z = here.z
        layer = Exchange(here, l_s, lo_ref, lsend, lrecv)
        last_cot = lambda: remote(
            crows_ref.at[flip(z, 3)], c3_s, csend.at[0], crecv.at[0], here.dp, flip(z, 3)
        )

    @pl.when(step == 0)
    def _():
        if comm:
            barrier = pltpu.get_barrier_semaphore()
            for k in range(1, row_steps):
                pl.semaphore_signal(
                    barrier, inc=1, device_id=(here.dp, flip(z, k)), device_id_type=pl.DeviceIdType.MESH
                )
            pl.semaphore_wait(barrier, row_steps - 1)
            last_cot().start()
        vecg_ref[...] = jnp.zeros_like(vecg_ref)
        bing_ref[...] = jnp.zeros_like(bing_ref)

    if comm:

        @pl.when(step < row_steps - 1)
        def _():
            cot_s[...] = cot_ref[...]

        @pl.when(step == row_steps - 1)
        def _():
            landed(c3_s, crecv.at[0])
            cot_s[...] = c3_s[...]

    @pl.when(step < row_steps)
    def _():
        at = pl.ds(pl.multiple_of(step * BLK, BLK), BLK)
        dropped = drop_ref[lax.axis_index("tensor")] == 1
        cot = (cot_s if comm else cot_ref)[...].astype(F32)
        att = att_ref[...]
        att_s[at, :] = att
        x = x_ref[...].astype(F32)
        branch = dot_nt(att, wo_ref[...]) + vec(0)
        n1, inv1 = norm_rows(x + branch)
        hidden = n1 * vec(1) + vec(2)
        low = hidden.astype(BF)
        ht_s[:, at] = jnp.transpose(low)
        ffn = hidden + vec(3)
        for t in range(parts):
            pre = dot_nn(low, up(t)) + bin_ref[t * fl : (t + 1) * fl][None, :]
            act, slope = gelu_parts(pre)
            act = act.astype(BF)
            act_s[t, at, :] = act
            slope_s[t] = slope
            ffn = ffn + dot_nt(act, dn(t))
        n2, inv2 = norm_rows(ffn)
        final = n2 * vec(4) + vec(5)
        layer_rows = jnp.where(dropped, x, final).astype(BF)
        if comm:
            l_s[flip(z, partner_at(step))] = layer_rows
        else:
            lo_ref[...] = layer_rows
        g_final = jnp.where(dropped, 0.0, cot)
        g_fpre = norm_back(g_final, n2, inv2, vec(4))
        gb2 = g_fpre.astype(BF)
        gb2t_s[:, at] = jnp.transpose(gb2)
        g_hidden = g_fpre
        for t in range(parts):
            gpre = (dot_nn(gb2, dn(t)) * slope_s[t]).astype(BF)
            gpre_s[t, at, :] = gpre
            bing_ref[:, t * fl : (t + 1) * fl] += jnp.sum(gpre.astype(F32), axis=0, keepdims=True)
            g_hidden = g_hidden + dot_nt(gpre, up(t))
        g_hpre = norm_back(g_hidden, n1, inv1, vec(1))
        gb = g_hpre.astype(BF)
        gbt_s[:, at] = jnp.transpose(gb)
        gatt_ref[...] = dot_nn(gb, wo_ref[...]).astype(BF)
        ghpre_ref[...] = g_hpre + jnp.where(dropped, cot, 0.0)
        for r, v in enumerate(
            (gb.astype(F32), g_hidden * n1, g_hidden, gb2.astype(F32), g_final * n2, g_final)
        ):
            vecg_ref[r : r + 1, :] += jnp.sum(v, axis=0, keepdims=True)

    if comm:
        for k in range(row_steps):

            @pl.when(step == k)
            def _():
                if partner_at(k) == 0:
                    layer.own().start()
                else:
                    layer.copy(partner_at(k)).start()

    @pl.when((step >= row_steps) & (step < row_steps + parts))
    def _():
        t = step - row_steps
        gup_ref[...] = dot_nn(ht_s[...], gpre_s[t]).astype(BF)
        gdn_ref[...] = dot_nn(gb2t_s[...], act_s[t]).astype(BF)

    @pl.when(step == row_steps + parts)
    def _():
        gwo_ref[...] = dot_nn(gbt_s[...], att_s[...]).astype(BF)
        if comm:
            last_cot().wait_send()
            layer.wait_recv()
            layer.wait_send()


def middle(comm, drop, att, x, cot, cot_rows, wo, w, vecs, bias_in):
    length, d = att.shape
    parts, groups, _, group, fl = w.shape
    nr = length // BLK

    def place_of(i):
        return flip(lax.axis_index("tensor"), partner_at(i)) if comm else i

    rows = pl.BlockSpec((BLK, d), lambda i: (place_of(jnp.minimum(i, nr - 1)), 0))
    cot_spec = pl.BlockSpec((BLK, d), lambda i: (place_of(jnp.minimum(i, nr - 1 - comm)), 0))
    any_ = pl.BlockSpec(memory_space=pl.ANY)
    once = lambda shape: pl.BlockSpec(
        shape, lambda i: (0,) * len(shape), pipeline_mode=pl.Buffered(1)
    )
    weight = lambda a: pl.BlockSpec(
        (parts, groups, None, group, fl), lambda i: (0, 0, a, 0, 0), pipeline_mode=pl.Buffered(1)
    )
    part = pl.BlockSpec((None, d, fl), lambda i: (jnp.clip(i - nr, 0, parts - 1), 0, 0))
    whole = lambda shape: pl.BlockSpec(shape, lambda i: (0,) * len(shape))
    dma = pltpu.SemaphoreType.DMA
    comm_scratch = [
        pltpu.VMEM((BLK, d), BF),
        pltpu.VMEM((BLK, d), BF),
        pltpu.VMEM((nr, BLK, d), BF),
        dma((nr,)),
        dma((nr,)),
        dma((1,)),
        dma((1,)),
    ]
    extra = dict(collective_id=2, has_side_effects=True) if comm else {}
    return pl.pallas_call(
        functools.partial(middle_kernel, comm, nr),
        grid=(nr + parts + 1,),
        out_shape=(
            jax.ShapeDtypeStruct((nr, BLK, d) if comm else (length, d), BF),
            jax.ShapeDtypeStruct((length, d), BF),
            jax.ShapeDtypeStruct((length, d), F32),
            jax.ShapeDtypeStruct((parts, d, fl), BF),
            jax.ShapeDtypeStruct((parts, d, fl), BF),
            jax.ShapeDtypeStruct((d, d), BF),
            jax.ShapeDtypeStruct((8, d), F32),
            jax.ShapeDtypeStruct((1, parts * fl), F32),
        ),
        in_specs=[
            pl.BlockSpec(memory_space=pltpu.SMEM),
            rows,
            rows,
            cot_spec,
            any_,
            once((d, d)),
            weight(0),
            weight(1),
            *[once((d,))] * 6,
            once((parts * fl,)),
        ],
        out_specs=(
            any_ if comm else rows, rows, rows, part, part, whole((d, d)), whole((8, d)), whole((1, parts * fl)),
        ),
        scratch_shapes=[
            pltpu.VMEM((length, d), BF),
            pltpu.VMEM((parts, length, fl), BF),
            pltpu.VMEM((parts, length, fl), BF),
            pltpu.VMEM((parts, BLK, fl), F32),
            pltpu.VMEM((d, length), BF),
            pltpu.VMEM((d, length), BF),
            pltpu.VMEM((d, length), BF),
            *(comm_scratch if comm else []),
        ],
        compiler_params=pltpu.CompilerParams(vmem_limit_bytes=VMEM_LIMIT, **extra),
        name="middle",
    )(drop, att, x, cot, cot_rows, wo, w, w, *vecs, bias_in)


def columns(p, start=0):
    return pl.ds(pl.multiple_of(start + p * LANES, LANES), LANES)


def assemble(mix, nz, wqkv_ref, wo_ref):
    d = wo_ref.shape[0]
    wl = d // nz
    for j in range(4):
        whole = jnp.concatenate([mix(t)[:, j * wl : (j + 1) * wl] for t in range(nz)], axis=1)
        if j < 3:
            wqkv_ref[:, j * d : (j + 1) * d] = whole
        else:
            wo_ref[...] = whole


def first_kernel(
    tok_ref, cot_ref, qkvw_ref, wow_ref, upw_ref, dnw_ref, bias_ref, seg_ref,
    x_out, cot_out, wud_out, qkv_out, wqkv_out, xt_out, wo_ref, att_ref, lse_ref, ext_ref,
    sh_ref, mix_s, x_s, qkv_s, wqkv_s, xt_s, kx_s, qx_s, vt_s,
    out_sem, send, recv, line, local, tsend, trecv, csend, crecv,
):
    nz = mix_s.shape[0]
    length, d = att_ref.shape
    pairs = d // LANES
    blk = length // nz
    here = Here(nz)
    mix = Gather(here, mix_s, sh_ref.at[0:1], 0, send, recv, line, local)
    rest = Gather(here, wud_out, sh_ref.at[1:3], 1, send, recv, line, local)
    tokens = Exchange(here, tok_ref, x_s, tsend, trecv)
    cots = Exchange(here, cot_ref, cot_out, csend, crecv, (1, 2))
    sh_ref[0] = jnp.concatenate(
        (qkvw_ref[0], qkvw_ref[1], qkvw_ref[2], jnp.transpose(wow_ref[...])), axis=1
    )
    out_x = pltpu.make_async_copy(x_s, x_out, out_sem.at[0])
    out_qkv = pltpu.make_async_copy(qkv_s, qkv_out, out_sem.at[1])
    out_w = pltpu.make_async_copy(wqkv_s, wqkv_out, out_sem.at[2])
    out_xt = pltpu.make_async_copy(xt_s, xt_out, out_sem.at[3])
    here.greet()
    mix.stage1(0)
    sh_ref[1] = upw_ref[...]
    sh_ref[2] = dnw_ref[...]
    rest.stage1(0)
    mix.stage1(1)
    mix.stage1(2)
    rest.stage1(1)
    mix.stage1(3)
    tokens.start()
    seg = jnp.transpose(jnp.broadcast_to(seg_ref[pl.ds(here.z, 1), :], (LANES, length)))
    doc_lanes(seg, kx_s, qx_s)
    ext_ref[:, :LANES] = kx_s[:, LANES:]
    ext_ref[:, LANES:] = qx_s[:, LANES:]
    vt_s[:, HD:, :] = jnp.ones((2, vt_s.shape[1] - HD, length), BF)
    mix.stage2(0)
    mix.stage2(1)
    mix.stage3(0)
    mix.stage2(2)
    mix.stage3(1)
    mix.stage2(3)
    mix.stage3(2)
    mix.stage3(3)
    rest.stage2(0)
    rest.stage1(2)
    mix.arrive()
    assemble(lambda t: mix_s[t].reshape(d, -1), nz, wqkv_s, wo_ref)
    out_w.start()
    bias = jnp.concatenate(
        (bias_ref[0:1, :], jnp.zeros((1, d), F32), bias_ref[1:2, :]), axis=1
    )
    tokens.own().wait()

    def project(k, carry):
        @pl.when(k > 0)
        def _():
            tokens.got(k)

        block = flip(here.z, k)
        at = pl.ds(pl.multiple_of(block * blk, blk), blk)
        qkv_s[at, :] = (dot_nn(x_s[block], wqkv_s[...]) + bias).astype(BF)
        xt_s[:, at] = jnp.transpose(x_s[block])

        @pl.when(k == 0)
        def _():
            rest.stage2(1)
            rest.stage3(0)

        @pl.when(k == 2)
        def _():
            rest.stage1(3)

        return carry

    lax.fori_loop(0, nz, project, 0)
    out_x.start()
    out_qkv.start()
    out_xt.start()
    cots.start()
    between = [
        [lambda: rest.stage2(2), lambda: rest.stage3(1)],
        [lambda: rest.stage2(3), lambda: rest.stage3(2)],
        [lambda: rest.stage3(3)],
    ]

    def work(p):
        o, lse = attend_pair(
            qkv_s[:, columns(p)], qkv_s[:, columns(p, d)], qkv_s[:, columns(p, 2 * d)], kx_s, qx_s, vt_s
        )
        att_ref[:, columns(p)] = o
        lse_ref[p] = lse

    every_pair(pairs, work, between)
    rest.arrive()
    rest.sent()
    mix.sent()
    tokens.wait_send()
    cots.wait_recv()
    cots.wait_send()
    for copy in (out_x, out_qkv, out_w, out_xt):
        copy.wait()


def first(tokens, cot, qkv_w, wo_w, up_w, dn_w, qv_b, segment_ids):
    nz, nd = lax.axis_size("tensor"), lax.axis_size("dp")
    na, (rw, wide) = 3, up_w.shape
    _, blk, d = tokens.shape
    length = segment_ids.shape[1]
    pairs = d // LANES
    any_ = pl.BlockSpec(memory_space=pl.ANY)
    vmem = pl.BlockSpec(memory_space=pltpu.VMEM)
    dma = pltpu.SemaphoreType.DMA
    s = jax.ShapeDtypeStruct
    unit = lambda count: (nz, nd // 2, 2, count, rw, wide)
    return pl.pallas_call(
        first_kernel,
        out_shape=(
            s(tokens.shape, BF),
            s(tokens.shape, BF),
            s(unit(na - 1), BF),
            s((length, 3 * d), BF),
            s((d, 3 * d), BF),
            s((d, length), BF),
            s((d, d), BF),
            s((length, d), BF),
            s((pairs, 2, length), F32),
            s((length, 2 * LANES), BF),
        ),
        in_specs=[any_, any_] + [vmem] * 6,
        out_specs=(any_,) * 6 + (vmem,) * 4,
        scratch_shapes=[
            pltpu.VMEM((na, rw, wide), BF),
            pltpu.VMEM(unit(1), BF),
            pltpu.VMEM((nz, blk, d), BF),
            pltpu.VMEM((length, 3 * d), BF),
            pltpu.VMEM((d, 3 * d), BF),
            pltpu.VMEM((d, length), BF),
            pltpu.VMEM((length, 2 * LANES), BF),
            pltpu.VMEM((length, 2 * LANES), BF),
            pltpu.VMEM((2, HD + 16, length), BF),
            dma((4,)),
            dma((2, 8)),
            dma((2, nz, 6)),
            dma((2, nz, 2)),
            dma((2,)),
            dma((nz,)),
            dma((nz,)),
            dma((nz,)),
            dma((nz,)),
        ],
        compiler_params=pltpu.CompilerParams(
            collective_id=0, has_side_effects=True, vmem_limit_bytes=VMEM_LIMIT
        ),
        name="first",
    )(tokens, cot, qkv_w, wo_w, up_w, dn_w, qv_b, segment_ids)


def last_kernel(
    gup_ref, gdn_ref, gwo_ref, ghpre_ref, qkv_ref, att_ref, gatt_ref, wqkv_ref, xt_ref,
    lse_ref, ext_ref, vecg_ref, bing_ref,
    grows_ref, gqkv_ref, gout_ref, gup_out, gdn_out, vsum_ref,
    pair_s, g_s, w_s, xt_s, hpre_s, gwo_s, gx_s, kx_s, qx_s, kt_s, delta_s, dk_s, dv_s, vbuf,
    u0, u1, u2, u3, u4, u5, u6, m0, m1, m2, m3, m4, m5, m6,
    psem, hsem, load, uload, send, recv, xsend, xrecv, vsend, vrecv,
):
    nz = u0.shape[0]
    length, d = g_s.shape[1:]
    pairs = d // LANES
    blk = length // nz
    wl = d // nz
    here = Here(nz)
    z = here.z
    ud = Scatter(here, u0, u1, u2, u3, u4, u5, u6, 1, send, recv)
    mx = Scatter(here, m0, m1, m2, m3, m4, m5, m6, 0, send, recv)
    rows = Exchange(here, gx_s, grows_ref, xsend, xrecv)

    def pair_loads(p, slot):
        srcs = (
            qkv_ref.at[:, columns(p)], qkv_ref.at[:, columns(p, d)], qkv_ref.at[:, columns(p, 2 * d)],
            att_ref.at[:, columns(p)], gatt_ref.at[:, columns(p)],
        )
        return [
            pltpu.make_async_copy(src, pair_s.at[slot, j], psem.at[slot, j])
            for j, src in enumerate(srcs)
        ]

    def ud_loads(k):
        t = ud.order[k]
        return [
            pltpu.make_async_copy(
                g.at[t, :, here.core], u0.at[t, :, here.core, a], uload.at[a, t]
            )
            for a, g in enumerate((gup_ref, gdn_ref))
        ]

    def ud_core(k):
        t = ud.order[k]
        for a, g in enumerate((gup_ref, gdn_ref)):
            remote(
                g.at[t, :, 1 - here.core], u1.at[t, :, a], ud.send(0), ud.recv(t, 0), here.dev_c, z
            ).start()

    later = [
        pltpu.make_async_copy(src, dst, load.at[i])
        for i, (src, dst) in enumerate(((wqkv_ref, w_s), (xt_ref, xt_s), (gwo_ref, gwo_s)))
    ]

    def hpre_load(i, slot):
        return pltpu.make_async_copy(ghpre_ref.at[i], hpre_s.at[slot], hsem.at[slot])

    for copy in pair_loads(0, 0):
        copy.start()
    for k in range(nz):
        for copy in ud_loads(k):
            copy.start()
    here.greet()
    for k in range(nz):
        ud_core(k)
    kx_s[:, LANES:] = ext_ref[:, :LANES]
    qx_s[:, LANES:] = ext_ref[:, LANES:]

    def work(p):
        slot = p % 2

        @pl.when(p + 1 < pairs)
        def _():
            for copy in pair_loads(p + 1, 1 - slot):
                copy.start()

        for copy in pair_loads(p, slot):
            copy.wait()
        q, k, v, att, g = [pair_s.at[slot, j] for j in range(5)]

        def put_q(at, value):
            g_s[0, at, columns(p)] = value

        attend_pair_back(q, k, v, att, g, lse_ref[p], kx_s, qx_s, kt_s, delta_s, dk_s, dv_s, put_q)
        g_s[1, :, columns(p)] = dk_s[...].astype(BF)
        g_s[2, :, columns(p)] = dv_s[...].astype(BF)

    def start_later():
        for copy in later:
            copy.start()

    def run(*names):
        return [lambda name=name, k=k: getattr(ud, name)(k) for name, k in names]

    def halves_here():
        for k in range(nz):
            for copy in ud_loads(k):
                copy.wait()

    between = [
        [halves_here] + run(("stage2", 0), ("stage2", 1)),
        run(("stage2", 2), ("stage3", 0), ("stage2", 3)),
        run(("stage3", 1),) + [start_later],
        run(("stage4", 0), ("stage5", 0), ("stage3", 2)),
        run(("stage3", 3), ("stage4", 1), ("stage5", 1)),
    ]
    every_pair(pairs, work, between)

    place_of = [flip(z, k) for k in (2, 3, 1, 0)]
    hpre_load(place_of[0], 0).start()
    for copy in later:
        copy.wait()
    for i, to in enumerate(place_of):
        if i + 1 < nz:
            hpre_load(place_of[i + 1], (i + 1) % 2).start()
        hpre_load(to, i % 2).wait()
        at = pl.ds(pl.multiple_of(to * blk, blk), blk)
        g_rows = jnp.concatenate([g_s[j, at, :] for j in range(3)], axis=1)
        gx_s[to] = (hpre_s[i % 2] + dot_nt(g_rows, w_s[...])).astype(BF)
        if i + 1 < nz:
            rows.copy((2, 3, 1)[i]).start()
        else:
            rows.own().start()

    ud.stage4(2)
    ud.stage5(2)

    vsum_ref[...] = jnp.zeros_like(vsum_ref)
    vsum_ref[0:8, :] = vecg_ref[...]
    for i in range(bing_ref.shape[1] // d):
        vsum_ref[8 + i : 9 + i, :] = bing_ref[:, i * d : (i + 1) * d]
    xt = xt_s[...]
    for j in range(3):
        grad = dot_nn(xt, g_s[j]).astype(BF)
        for t in range(nz):
            part = grad[:, t * wl : (t + 1) * wl]
            m0[t, :, :, 0, :, j * wl : (j + 1) * wl] = part.reshape(m0.shape[1:3] + (m0.shape[4], wl))
        if j != 1:
            sums = jnp.sum(g_s[j].astype(F32), axis=0, keepdims=True)
            r = vsum_ref.shape[0] - 2 + j // 2
            vsum_ref[r : r + 1, :] = sums
    for t in range(nz):
        part = gwo_s[:, t * wl : (t + 1) * wl]
        m0[t, :, :, 0, :, 3 * wl :] = part.reshape(m0.shape[1:3] + (m0.shape[4], wl))

    partners = [(here.dev_c, z), (here.dev_x, z), (here.dev_y, z)]
    partners += [(here.dp, z + 1 - 2 * (z % 2)), (here.dp, (z + 2) % nz)]

    def vec_copy(k):
        return remote(vbuf.at[0, k], vbuf.at[1, k], vsend.at[k], vrecv.at[k], *partners[k])

    def vec_start(k):
        vbuf[0, k] = vsum_ref[...]
        vec_copy(k).start()

    def vec_finish(k):
        landed(vbuf.at[1, k], vrecv.at[k])
        vsum_ref[...] += vbuf[1, k]

    for k in range(nz):
        mx.stage1(k)
    vec_start(0)
    for k in range(nz + 3):
        if k < nz:
            mx.stage2(k)
        if 1 <= k <= nz:
            mx.stage3(k - 1)
        if k < len(partners):
            vec_finish(k)
            if k + 1 < len(partners):
                vec_start(k + 1)
        if 2 <= k <= nz + 1:
            mx.stage4(k - 2)
        if 3 <= k <= nz + 1:
            mx.stage5(k - 3)
    ud.stage4(3)
    up_sum, dn_sum = ud.total()
    gup_out[...] = up_sum
    gdn_out[...] = dn_sum
    (mix_sum,) = mx.total()
    for j in range(3):
        gqkv_ref[j] = mix_sum[:, j * wl : (j + 1) * wl]
    gout_ref[...] = jnp.transpose(mix_sum[:, 3 * wl :])
    ud.drain()
    mx.drain()
    for k in range(len(partners)):
        vec_copy(k).wait_send()
    rows.wait_recv()
    rows.wait_send()


def last(gup, gdn, gwo, ghpre, qkv, att, gatt, wqkv, xt, lse, ext, vecg, bing):
    nz, nd = lax.axis_size("tensor"), lax.axis_size("dp")
    length, d = att.shape
    rw, wide, wl = d // nd, gup.shape[2], d // nz
    blk = length // nz
    unit = (nz, nd // 2, 2, rw, wide)
    any_ = pl.BlockSpec(memory_space=pl.ANY)
    vmem = pl.BlockSpec(memory_space=pltpu.VMEM)
    dma = pltpu.SemaphoreType.DMA
    s = jax.ShapeDtypeStruct
    steps = 5
    vec_shape = (16, d)
    return pl.pallas_call(
        last_kernel,
        out_shape=(
            s((nz, blk, d), BF),
            s((3, rw, wl), F32),
            s((wl, rw), F32),
            s((rw, wide), F32),
            s((rw, wide), F32),
            s(vec_shape, F32),
        ),
        in_specs=[any_] * 9 + [vmem] * 4,
        out_specs=(any_,) + (vmem,) * 5,
        scratch_shapes=[
            pltpu.VMEM((2, 5, length, LANES), BF),
            pltpu.VMEM((3, length, d), BF),
            pltpu.VMEM((d, 3 * d), BF),
            pltpu.VMEM((d, length), BF),
            pltpu.VMEM((2, blk, d), F32),
            pltpu.VMEM((d, d), BF),
            pltpu.VMEM((nz, blk, d), BF),
            pltpu.VMEM((length, 2 * LANES), BF),
            pltpu.VMEM((length, 2 * LANES), BF),
            pltpu.VMEM((LANES, length), BF),
            pltpu.VMEM((8, length), F32),
            pltpu.VMEM((length, LANES), F32),
            pltpu.VMEM((length, LANES), F32),
            pltpu.VMEM((2, steps) + vec_shape, F32),
        ]
        + scatter_scratch(2, nz, nd, rw, wide)
        + scatter_scratch(1, nz, nd, rw, wide)
        + [
            dma((2, 5)),
            dma((2,)),
            dma((3,)),
            dma((2, nz)),
            dma((2, 6)),
            dma((2, nz, 7)),
            dma((nz,)),
            dma((nz,)),
            dma((steps,)),
            dma((steps,)),
        ],
        compiler_params=pltpu.CompilerParams(
            collective_id=1, has_side_effects=True, vmem_limit_bytes=LAST_LIMIT
        ),
        name="last",
    )(
        gup.reshape(unit), gdn.reshape(unit), gwo, ghpre.reshape(nz, blk, d),
        qkv, att, gatt, wqkv, xt, lse, ext, vecg, bing,
    )


LAST_LIMIT = 61 * 1024 * 1024


def finish_kernel(lrows, grows, gqkv, gout, gup, gdn, sums, *outs):
    (
        layer_out, grad_tokens, o_qkv, o_qvb, o_out, o_outb, o_gain1, o_shift1,
        o_up, o_upb, o_dn, o_dnb, o_gain2, o_shift2,
    ) = outs
    layer_out[...] = lrows[...]
    grad_tokens[...] = grows[...].astype(F32)

    @pl.when(pl.program_id(0) == 0)
    def _():
        d = sums.shape[1]
        for dst, src in ((o_qkv, gqkv), (o_out, gout), (o_up, gup), (o_dn, gdn)):
            dst[...] = src[...]
        for r, dst in enumerate((o_outb, o_gain1, o_shift1, o_dnb, o_gain2, o_shift2)):
            dst[...] = sums[r, :]
        for r in range(o_upb.shape[0] // d):
            o_upb[r * d : (r + 1) * d] = sums[8 + r, :]
        o_qvb[...] = sums[sums.shape[0] - 2 :, :]


def finish(lrows, grows, gqkv, gout, gup, gdn, sums, hidden):
    nz, blk, d = lrows.shape
    rows = pl.BlockSpec((nz // 2, blk, d), lambda i: (i, 0, 0))
    s = jax.ShapeDtypeStruct
    same = lambda a: s(a.shape, a.dtype)
    vector = s((d,), F32)
    outs = (
        same(lrows), s(grows.shape, F32), same(gqkv), s((2, d), F32), same(gout), vector, vector, vector,
        same(gup), s((hidden,), F32), same(gdn), vector, vector, vector,
    )
    whole = lambda a: pl.BlockSpec(a.shape, lambda i: (0,) * len(a.shape))
    return pl.pallas_call(
        finish_kernel,
        grid=(2,),
        out_shape=outs,
        in_specs=[rows, rows] + [whole(a) for a in (gqkv, gout, gup, gdn, sums)],
        out_specs=[rows, rows] + [whole(a) for a in outs[2:]],
        compiler_params=pltpu.CompilerParams(vmem_limit_bytes=VMEM_LIMIT),
        name="finish",
    )(lrows, grows, gqkv, gout, gup, gdn, sums)


def plain_attend_kernel(q_ref, k_ref, v_ref, segc_ref, o_ref, lse_ref, kx_s, qx_s, vt_s):
    doc_lanes(segc_ref[...], kx_s, qx_s)
    vt_s[:, HD:, :] = jnp.ones((2, vt_s.shape[1] - HD, vt_s.shape[2]), BF)
    o_ref[...], lse_ref[...] = attend_pair(q_ref[...], k_ref[...], v_ref[...], kx_s, qx_s, vt_s)


def plain_attend_back_kernel(
    q_ref, k_ref, v_ref, att_ref, g_ref, lse_ref, segc_ref, gq_ref, gk_ref, gv_ref,
    kx_s, qx_s, kt_s, delta_s, dk_s, dv_s,
):
    doc_lanes(segc_ref[...], kx_s, qx_s)

    def put_q(at, value):
        gq_ref[at, :] = value

    attend_pair_back(
        q_ref, k_ref, v_ref, att_ref, g_ref, lse_ref[...], kx_s, qx_s, kt_s, delta_s, dk_s, dv_s, put_q
    )
    gk_ref[...] = dk_s[...].astype(BF)
    gv_ref[...] = dv_s[...].astype(BF)


def plain_specs(length, d):
    col = lambda off: pl.BlockSpec((length, LANES), lambda p: (0, off + p))
    seg = pl.BlockSpec((length, LANES), lambda p: (0, 0))
    lse = pl.BlockSpec((None, 2, length), lambda p: (p, 0, 0))
    wide = pltpu.VMEM((length, 2 * LANES), BF)
    return d // LANES, col, seg, lse, wide


def plain_first(tokens, cot, qkv_w, wo_w, up_w, dn_w, qv_b, segment_ids):
    axes = ("tensor", "dp")
    nz = lax.axis_size("tensor")
    length, d = segment_ids.shape[1], tokens.shape[2]
    pairs, col, seg, lse_spec, wide = plain_specs(length, d)
    mix = jnp.concatenate((qkv_w[0], qkv_w[1], qkv_w[2], wo_w.T), axis=1)
    shards = jnp.stack((mix, up_w, dn_w))
    ids = lax.dynamic_index_in_dim(segment_ids, lax.axis_index("tensor"), 0, keepdims=False)
    segc = jnp.broadcast_to(ids[:, None], (length, LANES))
    bias = jnp.concatenate((qv_b[0], jnp.zeros((d,), F32), qv_b[1]))
    x = lax.all_to_all(tokens, "tensor", 0, 0)
    cot = lax.all_to_all(cot, "tensor", 0, 0)
    w = lax.all_gather(shards, axes, axis=1, tiled=True).reshape(3, nz, d, shards.shape[2])
    parts = w[0].reshape(nz, d, 4, d // nz).transpose(1, 2, 0, 3).reshape(d, 4 * d)
    wqkv, wo = parts[:, : 3 * d], parts[:, 3 * d :]
    rows = x.reshape(length, d)
    qkv = (dot_nn(rows, wqkv) + bias).astype(BF)
    att, lse = pl.pallas_call(
        plain_attend_kernel,
        grid=(pairs,),
        out_shape=(
            jax.ShapeDtypeStruct((length, d), BF),
            jax.ShapeDtypeStruct((pairs, 2, length), F32),
        ),
        in_specs=[col(0), col(pairs), col(2 * pairs), seg],
        out_specs=(col(0), lse_spec),
        scratch_shapes=[wide, wide, pltpu.VMEM((2, HD + 16, length), BF)],
        compiler_params=pltpu.CompilerParams(vmem_limit_bytes=VMEM_LIMIT),
        name="plain_attend",
    )(qkv, qkv, qkv, segc)
    wud = w[1:].reshape(2, nz, 8, d // 8, -1).transpose(1, 2, 0, 3, 4)
    return x, cot, wud, qkv, wqkv, rows.T, wo, att, lse, segc


def plain_last(gup, gdn, gwo, ghpre, qkv, att, gatt, wqkv, xt, lse, segc, vecg, bing):
    axes = ("tensor", "dp")
    nz = lax.axis_size("tensor")
    length, d = att.shape
    pairs, col, seg, lse_spec, wide = plain_specs(length, d)
    f32_wide = pltpu.VMEM((length, LANES), F32)
    grads = pl.pallas_call(
        plain_attend_back_kernel,
        grid=(pairs,),
        out_shape=[jax.ShapeDtypeStruct((length, d), BF)] * 3,
        in_specs=[col(0), col(pairs), col(2 * pairs), col(0), col(0), lse_spec, seg],
        out_specs=[col(0)] * 3,
        scratch_shapes=[
            wide, wide, pltpu.VMEM((LANES, length), BF), pltpu.VMEM((8, length), F32), f32_wide, f32_wide,
        ],
        compiler_params=pltpu.CompilerParams(vmem_limit_bytes=VMEM_LIMIT),
        name="plain_attend_back",
    )(qkv, qkv, qkv, att, gatt, lse, segc)
    g = jnp.concatenate(grads, axis=1)
    gx = (ghpre + dot_nt(g, wqkv)).astype(BF)
    gmix = jnp.concatenate((dot_nn(xt, g).astype(BF), gwo), axis=1)
    gmix = gmix.reshape(d, 4, nz, d // nz).transpose(2, 0, 1, 3).reshape(nz, d, -1)
    split = lambda a: a.reshape(nz, length // nz, d)
    parts = [
        lax.psum_scatter(p.reshape(nz * d, -1), axes, scatter_dimension=0, tiled=True)
        for p in (gmix, gup, gdn)
    ]
    mix_sum, up_sum, dn_sum = [p.astype(F32) for p in parts]
    wl = d // nz
    sums = [jnp.sum(grads[j].astype(F32), axis=0, keepdims=True) for j in (0, 2)]
    bing = bing.reshape(-1, d)
    gap = jnp.zeros((6 - bing.shape[0], d), F32)
    vec = jnp.concatenate((vecg, bing, gap, *sums), axis=0)
    return (
        lax.all_to_all(split(gx), "tensor", 0, 0),
        jnp.stack([mix_sum[:, j * wl : (j + 1) * wl] for j in range(3)]),
        mix_sum[:, 3 * wl :].T,
        up_sum,
        dn_sum,
        lax.psum(vec, axes),
    )


def on_device(
    tokens, segment_ids, drop_flags, qkv_w, qv_b, wo_w, wo_b, gain1, shift1,
    up_w, up_b, dn_w, dn_b, gain2, shift2, cotangent,
):
    nt, nd = lax.axis_size("tensor"), lax.axis_size("dp")
    d = tokens.shape[2]
    length = segment_ids.shape[1]
    wl = qkv_w.shape[2]
    fl = up_w.shape[1]
    comm = (nt, nd) == (4, 8)
    begin, end = (first, last) if comm else (plain_first, plain_last)
    x, cot, wud, qkv, wqkv, xt, wo, att, lse, ext = begin(
        tokens, cotangent, qkv_w, wo_w, up_w, dn_w.T, qv_b, segment_ids
    )
    vecs = (wo_b, gain1, shift1, dn_b, gain2, shift2)
    layer_out, g_att, g_hpre, gup, gdn, gwo, vecg, bing = middle(
        comm, drop_flags, att, x.reshape(length, d), cot.reshape(length, d), cotangent, wo,
        wud.reshape(nt, -1, 2, *wud.shape[-2:]), vecs, up_b,
    )
    if not comm:
        layer_out = lax.all_to_all(layer_out.reshape(nt, length // nt, d), "tensor", 0, 0)
    rows, g_qkv, g_out, g_up, g_dn, total = end(
        gup, gdn, gwo, g_hpre, qkv, att, g_att, wqkv, xt, lse, ext, vecg, bing
    )
    outs = finish(layer_out, rows, g_qkv, g_out, g_up, g_dn, total, nt * fl)
    return (*outs[:10], outs[10].T, *outs[11:])


def solution(mesh):
    rows = P("dp", "tensor", None)
    return jax.shard_map(
        on_device,
        mesh=mesh,
        in_specs=(
            rows, P("dp", None), P("dp"), P(None, "dp", "tensor"), P(), P("tensor", "dp"), P(), P(), P(),
            P("dp", "tensor"), P(), P("tensor", "dp"), P(), P(), P(), rows,
        ),
        out_specs=(
            rows, rows, P(None, "dp", "tensor"), P(), P("tensor", "dp"), P(), P(), P(),
            P("dp", "tensor"), P(), P("tensor", "dp"), P(), P(), P(),
        ),
        check_vma=False,
    )
```
